32 devices in a mesh: rep: 16 (over z, x, core), fsdp: 2 (over y).
Axes of the slice: x: 2, y: 2, z: 4, core: 2. Of those that a mesh axis runs over, the one named last changes fastest.
Arguments:
- hidden_in: bfloat16 [8192, 1024], P(('rep', 'fsdp')), may hold values from -6 to 6
- routes: int32 [8192, 8], P(('rep', 'fsdp')), may hold values from 0 to 15, all different within a row; in each aligned block of 256 rows (0 to 255, 256 to 511, ...) at most 160 rows name the same one
- w_qkv: bfloat16 [1024, 2048], P('fsdp'), may hold values from -0.1875 to 0.1875
- w_out: bfloat16 [1024, 1024], P('fsdp'), may hold values from -2 to 2
- w_router: bfloat16 [1024, 16], P('fsdp'), may hold values from -0.09375 to 0.09375
- attn_gain: bfloat16 [1024], P('fsdp'), may hold values from 0.5 to 1.5
- ffn_gain: bfloat16 [1024], P('fsdp'), may hold values from 0.5 to 1.5
- w_gate_up: bfloat16 [16, 1024, 1024], P('fsdp'), may hold values from -0.1875 to 0.1875
- w_down: bfloat16 [16, 1024, 512], P('fsdp'), may hold values from -2 to 2
- cotangent: bfloat16 [8192, 1024], P(('rep', 'fsdp')), may hold values from -6 to 6
Outputs:
- layer_out: bfloat16 [8192, 1024], P(('rep', 'fsdp'))
- grad_in: float32 [8192, 1024], P(('rep', 'fsdp'))
- grad_w_qkv: float32 [1024, 2048], P('fsdp')
- grad_w_out: float32 [1024, 1024], P('fsdp')
- grad_w_router: float32 [1024, 16], P('fsdp')
- grad_attn_gain: float32 [1024], P('fsdp')
- grad_ffn_gain: float32 [1024], P('fsdp')
- grad_w_gate_up: float32 [16, 1024, 1024], P('fsdp')
- grad_w_down: float32 [16, 1024, 512], P('fsdp')
The draws below stay inside these ranges and needn't reach their ends.
Inputs may be any that keep to these rules, and one draw needn't show every extreme that they name: `routes`: each row names 8 different experts. Within the 256 rows of one device no expert is named by more than 160 rows, and in every draw some expert is named by exactly 160 rows of some device.
All inputs are finite; a program needn't handle non-finite values.
Results may differ from the reference program's by a relative error of at most 0.023.
Values may be sent and summed in bfloat16 or wider, within the bound.
No kernel may reach another device: no remote copies, remote signals or barrier semaphores. Data moves between devices by JAX's collectives and lax.ppermute only.
A program may use at most 448 MiB of HBM per device.

```python
import math
import jax
import jax.numpy as jnp
import numpy as np
from jax import lax

D = 1024
HEADS = 16
KV_HEADS = 8
HEAD_DIM = 64
F = 512
TOP = 8
EXPERTS = 16
BLOCK = 256
SEQ_LEN = 512
TOK_DEV = 256
CAP = 160
QW = 1024
KVW = 512
QKV = 2048
TOKENS = 8192


def levels(key, extent, cuts, least, top_value):
    loudness = 1.0
    for dim, blocks in cuts:
        draws = jax.random.uniform(jax.random.fold_in(jax.random.fold_in(key, 6), dim), (blocks,), jnp.float32, least / len(cuts), top_value / len(cuts))
        loudness = loudness * jnp.repeat(jnp.exp(draws), extent[dim] // blocks).reshape((-1,) + (1,) * (len(extent) - 1 - dim))
    return loudness


def routed_block(stream_key, own, number, rows, number_of, top, reach, slope):
    ranking = jax.random.permutation(stream_key, number_of)
    crowded, usual = portions_of(number_of, rows * top, reach, slope, True), portions_of(number_of, rows * top, reach, slope, False)
    places = jnp.arange(number_of)

    def named(sizes, turn):
        used = int((sizes > 0).sum())
        fixed = max(1, used // 4)
        moved = fixed + (places - fixed + turn * (used - fixed)) % max(1, number_of - fixed)
        return jnp.zeros((number_of,), jnp.int32).at[ranking[jnp.where(places < fixed, places, moved)]].set(jnp.asarray(sizes, jnp.int32))

    sizes = jnp.where(number % 4 == 0, named(crowded, number // 4), named(usual, number - number // 4 - 1))
    mixed = jax.random.permutation(jax.random.fold_in(own, 3), number_of)
    donor, receiver = mixed[0:number_of // 2 * 2:2], mixed[1:number_of // 2 * 2:2]
    margin = jnp.minimum(sizes[donor] - 1, reach - sizes[receiver]) // 2
    margin = jnp.where((donor == ranking[0]) | (receiver == ranking[0]) | (sizes[receiver] == 0), 0, jnp.maximum(margin, 0))
    moved = jax.random.randint(jax.random.fold_in(own, 4), (number_of // 2,), 0, 1 << 20) % (margin + 1)
    sizes = sizes.at[donor].add(-moved).at[receiver].add(moved)
    members = jnp.searchsorted(jnp.cumsum(sizes), jnp.arange(rows * top), side="right").astype(jnp.int32)
    listing = members.reshape(top, rows).T
    listing = listing[jax.random.permutation(jax.random.fold_in(own, 1), rows)]
    turn = jax.random.randint(jax.random.fold_in(own, 2), (rows, 1), 0, top)
    return jnp.take_along_axis(listing, (jnp.arange(top)[None, :] + turn) % top, axis=1)


def portions_of(amount, total, bound, skew, full):
    weights = [(1 << 20) // math.isqrt(rank ** skew) + 1 for rank in range(1, amount + 1)]
    largest = bound if full else min(bound, max(-(-total // amount), total * weights[0] // sum(weights)))
    least = 1 if total - largest >= amount - 1 else 0
    given, spare = [largest] + [least] * (amount - 1), total - largest - least * (amount - 1)
    while spare > 0:
        free = [i for i in range(1, amount) if given[i] < largest] or [i for i in range(1, amount) if given[i] < bound]
        mass, left = sum([weights[i] for i in free]), spare
        for i in free:
            extra = min(bound - given[i], max(1, left * weights[i] // mass), spare)
            given[i] = given[i] + extra
            spare = spare - extra
    return np.array(given)


def noise(stream_key, extent, scale, limit, split=(), held_as=jnp.bfloat16):
    factor_of = levels(stream_key, extent, split, -0.22, 0.18) if split else 1.0
    entries = jax.random.normal(stream_key, extent, jnp.float32) * scale * factor_of
    return jnp.minimum(jnp.maximum(entries, -limit), limit).astype(held_as)


def setup_inputs(seed: int = 0) -> dict:
    seeds = jax.random.split(jax.random.key(seed), 11)
    hidden_in = noise(seeds[0], (TOKENS, D), 1.0, 6.0, ((0, 32),))
    routes_keys = jax.random.split(jax.random.fold_in(seeds[1], 1), TOKENS // TOK_DEV)
    routes_turns = jax.random.permutation(jax.random.fold_in(seeds[1], 3), TOKENS // TOK_DEV)
    routes = jax.vmap(lambda own, number: routed_block(jax.random.fold_in(seeds[1], 2), own, number, TOK_DEV, EXPERTS, TOP, CAP, 1))(routes_keys, routes_turns).reshape((TOKENS, TOP))
    w_qkv = noise(seeds[2], (D, QKV), D ** -0.5, 0.1875, ((0, 2),))
    w_out = noise(seeds[3], (QW, D), (max(D // 128, 1)) ** -0.5, 2.0, ((0, 2),))
    w_router = noise(seeds[4], (D, EXPERTS), (4 * D) ** -0.5, 0.09375, ((0, 2),))
    attn_gain = jnp.clip(1.0 + 0.1 * jax.random.normal(seeds[5], (D,), jnp.float32), 0.5, 1.5).astype(jnp.bfloat16)
    ffn_gain = jnp.clip(1.0 + 0.1 * jax.random.normal(seeds[6], (D,), jnp.float32), 0.5, 1.5).astype(jnp.bfloat16)
    w_gate_up = noise(seeds[7], (EXPERTS, D, 2 * F), D ** -0.5, 0.1875, ((0, 2),))
    w_down = noise(seeds[8], (EXPERTS, D, F), (max(F // 64, 1)) ** -0.5, 2.0, ((0, 2),))
    cotangent = noise(seeds[9], (TOKENS, D), 1.0, 6.0, ((0, 32),))
    return dict(hidden_in=hidden_in, routes=routes, w_qkv=w_qkv, w_out=w_out, w_router=w_router, attn_gain=attn_gain, ffn_gain=ffn_gain, w_gate_up=w_gate_up, w_down=w_down, cotangent=cotangent)


@jax.custom_vjp
def low(v):
    return lax.optimization_barrier(v.astype(jnp.bfloat16)).astype(jnp.float32)

@jax.custom_vjp
def low_back(v):
    return v

def low_keep(v):
    return (low(v), None)

def low_pass(kept, grad):
    return (grad,)

def back_keep(v):
    return (v, None)

def back_low(kept, grad):
    return (low(grad),)
low.defvjp(low_keep, low_pass)
low_back.defvjp(back_keep, back_low)
highest = lax.Precision.HIGHEST
norm_eps = 1e-06
masked_score = -1e+30

def product(left, right):
    return jnp.dot(left, right, precision=highest, preferred_element_type=jnp.float32)

def normalize(input_rows):
    return input_rows * lax.rsqrt(lax.optimization_barrier(jnp.mean(input_rows * input_rows, -1, keepdims=True)) + norm_eps)

def rotate(values):
    middle = values.shape[-1] // 2
    return jnp.concatenate([-values[..., middle:], values[..., :middle]], -1)

def rotary_tables(length, head_width):
    middle = head_width // 2
    places = jnp.arange(length, dtype=jnp.float32)
    frequency = 10000.0 ** (-(2.0 * jnp.arange(middle, dtype=jnp.float32)) / head_width)
    angles = places[:, None] * frequency[None, :]
    cosine_table = jnp.concatenate([jnp.cos(angles), jnp.cos(angles)], -1)
    sine_table = jnp.concatenate([jnp.sin(angles), jnp.sin(angles)], -1)
    return (cosine_table[:, None, :], sine_table[:, None, :])

def slot_tables(route_rows):
    length = route_rows.shape[0]
    assigned = route_rows.reshape(-1).astype(jnp.int32)
    one_hot = (assigned[:, None] == jnp.arange(EXPERTS, dtype=jnp.int32)[None, :]).astype(jnp.int32)
    earlier = (jnp.cumsum(one_hot, 0) - one_hot).astype(jnp.int32)
    position = lax.optimization_barrier(jnp.sum(earlier * one_hot, 1)).astype(jnp.int32)
    target = (assigned * CAP + position).astype(jnp.int32)
    slot_owner = jnp.full((EXPERTS * CAP,), length * TOP, jnp.int32).at[target].set(jnp.arange(length * TOP, dtype=jnp.int32))
    return (target, slot_owner)

def layer(seq_rows, route_rows, params):
    w_qkv, w_out, w_router, attn_gain, ffn_gain, w_gate_up, w_down = params
    length = seq_rows.shape[0]
    groups = HEADS // KV_HEADS
    score_scale = HEAD_DIM ** (-0.5)
    block_of = jnp.arange(length, dtype=jnp.int32) // BLOCK
    allowed = block_of[None, :] <= block_of[:, None]
    cosine_table, sine_table = rotary_tables(length, HEAD_DIM)

    def rotary(values):
        return values * cosine_table + rotate(values) * sine_table

    def group_attention(pieces):
        query_group, key_group, value_group = pieces
        scores = low_back(jnp.einsum('qrd,kd->rqk', query_group, key_group, precision=highest) * score_scale)
        scores = jnp.where(allowed[None], scores, masked_score)
        largest = lax.optimization_barrier(jnp.max(scores, -1, keepdims=True))
        exponent = jnp.exp(scores - largest)
        attn_probs = exponent / lax.optimization_barrier(jnp.sum(exponent, -1, keepdims=True))
        return jnp.einsum('rqk,kd->qrd', low(attn_probs), value_group, precision=highest)
    input_one = low(normalize(seq_rows) * attn_gain)
    qkv_proj = low_back(product(input_one, w_qkv))
    queries = low(rotary(qkv_proj[:, :QW].reshape(length, HEADS, HEAD_DIM)))
    keys = low(rotary(qkv_proj[:, QW:QW + KVW].reshape(length, KV_HEADS, HEAD_DIM)))
    values = low(qkv_proj[:, QW + KVW:].reshape(length, KV_HEADS, HEAD_DIM))
    query_groups = jnp.transpose(queries.reshape(length, KV_HEADS, groups, HEAD_DIM), (1, 0, 2, 3))
    key_groups = jnp.transpose(keys, (1, 0, 2))
    value_groups = jnp.transpose(values, (1, 0, 2))
    attended = lax.map(jax.checkpoint(group_attention), (query_groups, key_groups, value_groups))
    attended = jnp.transpose(attended, (1, 0, 2, 3)).reshape(length, QW)
    attended = low_back(low(attended))
    residual = seq_rows + low_back(product(attended, w_out))
    input_two = low(normalize(residual) * ffn_gain)
    logits = low_back(product(input_two, w_router))
    router = jax.nn.softmax(logits, -1)
    gate_vals = jnp.take_along_axis(router, route_rows, 1)
    halves = length // TOK_DEV

    def mixture(rows_half, routes_half, gates_half):
        target, slot_owner = slot_tables(routes_half)
        padded = jnp.concatenate([rows_half, jnp.zeros((1, D), jnp.float32)], 0)
        slotted = padded[slot_owner // TOP].reshape(EXPERTS, CAP, D)
        gate_up = low_back(jnp.einsum('ecd,edf->ecf', slotted, w_gate_up, precision=highest))
        hidden = low(jax.nn.silu(gate_up[..., :F]) * gate_up[..., F:])
        expert_rows = low_back(low(jnp.einsum('ecf,edf->ecd', hidden, w_down, precision=highest)))
        picked = expert_rows.reshape(EXPERTS * CAP, D)[target].reshape(TOK_DEV, TOP, D)
        return jnp.einsum('tk,tkd->td', gates_half, picked, precision=highest)
    mixed = jax.vmap(mixture)(input_two.reshape(halves, TOK_DEV, D), route_rows.reshape(halves, TOK_DEV, TOP), gate_vals.reshape(halves, TOK_DEV, TOP))
    return residual + mixed.reshape(length, D)

def reference(hidden_in, routes, w_qkv, w_out, w_router, attn_gain, ffn_gain, w_gate_up, w_down, cotangent):
    number = hidden_in.shape[0] // SEQ_LEN
    seq_inputs = hidden_in.astype(jnp.float32).reshape(number, SEQ_LEN, D)
    route_seqs = routes.reshape(number, SEQ_LEN, TOP)
    params = (w_qkv.astype(jnp.float32), w_out.astype(jnp.float32), w_router.astype(jnp.float32), attn_gain.astype(jnp.float32), ffn_gain.astype(jnp.float32), w_gate_up.astype(jnp.float32), w_down.astype(jnp.float32))

    def forward_all(x_all, weights):

        def one_sequence(pieces):
            return layer(pieces[0], pieces[1], weights)
        return lax.map(jax.checkpoint(one_sequence), (x_all, route_seqs))
    outputs, pullback = jax.vjp(forward_all, seq_inputs, params)
    grad_seqs, gradients = pullback(cotangent.astype(jnp.float32).reshape(number, SEQ_LEN, D))
    return (outputs.reshape(-1, D).astype(jnp.bfloat16), grad_seqs.reshape(-1, D), gradients[0], gradients[1], gradients[2], gradients[3], gradients[4], gradients[5], gradients[6])
```

```python
import math
from functools import partial

import jax
import jax.numpy as jnp
from jax import lax
from jax.sharding import Mesh, PartitionSpec as P

D = 1024
HEADS = 16
KV_HEADS = 8
HEAD_DIM = 64
F = 512
TOP = 8
EXPERTS = 16
BLOCK = 256


norm_eps = 1e-06
masked_score = -1e30

def turn(value, axes, steps, sizes):
    count = math.prod(sizes)
    pairs = []
    for source in range(count):
        place, rest = [], source
        for size in reversed(sizes):
            place.append(rest % size)
            rest //= size
        place.reverse()
        target = 0
        for at, size, step in zip(place, sizes, steps):
            target = target * size + (at + step) % size
        pairs.append((source, target))
    return lax.ppermute(value, axes, pairs)


def normalize(input_rows):
    scale_inv = lax.rsqrt(jnp.mean(input_rows * input_rows, -1, keepdims=True) + norm_eps)
    return (input_rows * scale_inv, scale_inv)


def norm_back(normed, scale_inv, grad_normed):
    return scale_inv * (grad_normed - normed * jnp.mean(grad_normed * normed, -1, keepdims=True))


def rotate(values):
    middle = values.shape[-1] // 2
    return jnp.concatenate([-values[..., middle:], values[..., :middle]], -1)


def rotate_back(values):
    middle = values.shape[-1] // 2
    return jnp.concatenate([values[..., middle:], -values[..., :middle]], -1)


def rotary_tables(places, head_width):
    middle = head_width // 2
    place_values = places.astype(jnp.float32)
    frequency = 10000.0 ** (-(2.0 * jnp.arange(middle, dtype=jnp.float32)) / head_width)
    angles = place_values[:, None] * frequency[None, :]
    cosine_table = jnp.concatenate([jnp.cos(angles), jnp.cos(angles)], -1)
    sine_table = jnp.concatenate([jnp.sin(angles), jnp.sin(angles)], -1)
    return (cosine_table[:, None, :], sine_table[:, None, :])


def attend_group(pieces, allowed, score_scale):
    query_group, key_group, value_group = pieces
    scores = (
        jnp.einsum("qrd,kd->rqk", query_group, key_group, preferred_element_type=jnp.float32)
        * score_scale
    )
    scores = jnp.where(allowed[None], scores, masked_score)
    largest = jnp.max(scores, -1, keepdims=True)
    exponent = jnp.exp(scores - largest)
    totals = jnp.sum(exponent, -1, keepdims=True)
    attn_probs = (exponent / totals).astype(jnp.bfloat16)
    output = jnp.einsum("rqk,kd->qrd", attn_probs, value_group, preferred_element_type=jnp.float32)
    return (output, (largest + jnp.log(totals))[..., 0])


def attend_back(pieces, allowed, score_scale):
    query_group, key_group, value_group, grad_group, log_total = pieces
    scores = (
        jnp.einsum("qrd,kd->rqk", query_group, key_group, preferred_element_type=jnp.float32)
        * score_scale
    )
    scores = jnp.where(allowed[None], scores, masked_score)
    attn_probs = jnp.exp(scores - log_total[..., None])
    probs_low = attn_probs.astype(jnp.bfloat16)
    grad_value = jnp.einsum(
        "rqk,qrd->kd", probs_low, grad_group, preferred_element_type=jnp.float32
    )
    grad_probs = jnp.einsum(
        "qrd,kd->rqk", grad_group, value_group, preferred_element_type=jnp.float32
    )
    grad_scores = (
        attn_probs * (grad_probs - jnp.sum(attn_probs * grad_probs, -1, keepdims=True))
    ).astype(jnp.bfloat16)
    grad_query = (
        jnp.einsum("rqk,kd->qrd", grad_scores, key_group, preferred_element_type=jnp.float32)
        * score_scale
    )
    grad_key = (
        jnp.einsum("rqk,qrd->kd", grad_scores, query_group, preferred_element_type=jnp.float32)
        * score_scale
    )
    return (grad_query, grad_key, grad_value)


def line_sum(value, axis):
    count = lax.axis_size(axis)
    if count == 1:
        return value
    if count % 2:
        return lax.psum(value, axis)
    middle = count // 2
    total = value
    for step in range(middle - 1):
        total = total + lax.ppermute(total, axis, [(step, step + 1), (count - 1 - step, count - 2 - step)])
    total = total + lax.ppermute(total, axis, [(middle - 1, middle), (middle, middle - 1)])
    place = lax.axis_index(axis)
    for step in range(middle - 1):
        low = middle - 2 - step
        passed = lax.ppermute(total, axis, [(low + 1, low), (count - 2 - low, count - 1 - low)])
        total = jnp.where((place == low) | (place == count - 1 - low), passed, total)
    return total


def own_part(value, axis, index, parts):
    size = value.shape[axis] // parts
    return lax.dynamic_slice_in_dim(value, index * size, size, axis)


def body(
    hidden_in, routes, w_qkv, w_out, w_router, attn_gain, ffn_gain, w_gate_up, w_down, cotangent
):
    length = hidden_in.shape[0]
    groups = HEADS // KV_HEADS
    query_width = HEADS * HEAD_DIM
    key_width = KV_HEADS * HEAD_DIM
    score_scale = HEAD_DIM ** (-0.5)
    shards, side, cores = lax.axis_size("fsdp"), lax.axis_size("side"), lax.axis_size("core")
    shard, side_at, core_at = lax.axis_index("fsdp"), lax.axis_index("side"), lax.axis_index("core")
    near = [(a, s) for a in range(side) for s in range(shards)]
    bf16, f32 = jnp.bfloat16, jnp.float32

    def dot(left, right, dims=((1,), (0,))):
        return lax.dot_general(left, right, (dims, ((), ())), preferred_element_type=f32)

    def fetch(piece):
        out = [[piece]]
        part = own_part(piece, 0, core_at, cores)
        for step in range(1, shards):
            first = turn(part, "fsdp", (step,), (shards,))
            parts = [first]
            for core in range(1, cores):
                parts.append(turn(first, "core", (core,), (cores,)))
            out.append(parts)
        return out

    def spread(rows):
        first = [rows if (a, s) == (0, 0) else turn(rows, ("side", "fsdp"), (a, s), (side, shards)) for a, s in near]
        first = jnp.stack(first)
        out = [first]
        for core in range(1, cores):
            out.append(turn(first, "core", (core,), (cores,)))
        return jnp.concatenate(out, 0)

    def collect(blocks):
        count = len(near)
        total = blocks[:count]
        for core in range(1, cores):
            total = total.astype(f32) + turn(blocks[core * count : (core + 1) * count], "core", (-core % cores,), (cores,)).astype(f32)
        total = total.astype(blocks.dtype)
        out = total[0].astype(f32)
        for i, (a, s) in enumerate(near):
            if (a, s) != (0, 0):
                out = out + turn(total[i], ("side", "fsdp"), (-a % side, -s % shards), (side, shards)).astype(f32)
        return out

    def row_blocks(values, axis):
        width = values.shape[axis] // shards
        out = [[lax.dynamic_slice_in_dim(values, shard * width, width, axis)]]
        for step in range(1, shards):
            base = (shard - step) % shards * width
            parts = []
            for core in range(cores):
                at = base + (core_at - core) % cores * (width // cores)
                parts.append(lax.dynamic_slice_in_dim(values, at, width // cores, axis))
            out.append(parts)
        return out

    def rows_dot(values, pieces):
        total = None
        for parts, weights in zip(row_blocks(values, 1), pieces):
            for part, weight in zip(parts, weights):
                term = dot(part, weight)
                total = term if total is None else total + term
        return total

    def rows_back(grads, pieces, width):
        full = jnp.zeros((grads.shape[0], width), f32)
        block = width // shards
        for step, weights in enumerate(pieces):
            base = (shard - step) % shards * block
            for core, weight in enumerate(weights):
                at = base + ((core_at - core) % cores * (block // cores) if step else 0)
                full = lax.dynamic_update_slice_in_dim(full, dot(grads, weight, ((1,), (1,))), at, 1)
        return full

    def gathered(piece):
        return lax.all_gather(piece, "fsdp", axis=0, tiled=True)

    def owned_sum(partial_sum):
        value = partial_sum.astype(bf16)
        half = own_part(value, 1, core_at, cores)
        for core in range(1, cores):
            other = own_part(value, 1, (core_at + core) % cores, cores)
            half = half + turn(other, "core", (core,), (cores,))
        total = own_part(half, 0, shard, shards)
        for step in range(1, shards):
            other = own_part(half, 0, (shard + step) % shards, shards)
            total = total + turn(other, "fsdp", (step,), (shards,))
        if side > 1:
            mine = own_part(total, 1, side_at, side)
            for step in range(1, side):
                mine = mine + turn(own_part(total, 1, (side_at + step) % side, side), "side", (step,), (side,))
            mine = line_sum(mine, "line")
            full = jnp.zeros(total.shape, bf16)
            width = mine.shape[1]
            full = lax.dynamic_update_slice_in_dim(full, mine, side_at * width, 1)
            for step in range(1, side):
                full = lax.dynamic_update_slice_in_dim(full, turn(mine, "side", (step,), (side,)), (side_at - step) % side * width, 1)
        else:
            full = line_sum(total, "line")
        width = full.shape[1]
        out = jnp.zeros((full.shape[0], width * cores), f32)
        out = lax.dynamic_update_slice_in_dim(out, full.astype(f32), core_at * width, 1)
        for core in range(1, cores):
            out = lax.dynamic_update_slice_in_dim(out, turn(full, "core", (core,), (cores,)).astype(f32), (core_at - core) % cores * width, 1)
        return out

    parity = shard % 2
    local_rows = jnp.arange(length, dtype=jnp.int32)
    places = parity * length + local_rows
    query_block = places // BLOCK
    earlier_block = jnp.where(parity == 1, local_rows // BLOCK, 4 * length)
    key_block = jnp.concatenate([earlier_block, query_block], 0)
    allowed = key_block[None, :] <= query_block[:, None]
    cosine_table, sine_table = rotary_tables(places, HEAD_DIM)
    small = gathered(jnp.concatenate([w_router, attn_gain[:, None], ffn_gain[:, None]], 1))
    full_router, gain_attn, gain_ffn = small[:, :EXPERTS], small[:, EXPERTS], small[:, EXPERTS + 1]
    qkv_pieces = fetch(w_qkv)
    out_pieces = fetch(w_out)
    grads_near = spread(cotangent).reshape(-1, D)
    routes_near = spread(routes).reshape(-1, TOP)
    later = [(i, i + 1) for i in range(0, shards, 2)]
    before = [(i + 1, i) for i in range(0, shards, 2)]

    input_rows = hidden_in.astype(f32)
    normed_one, inverse_one = normalize(input_rows)
    input_one = (normed_one * gain_attn).astype(bf16)
    qkv_proj = rows_dot(input_one, qkv_pieces)
    query_raw = qkv_proj[:, :query_width].reshape(length, HEADS, HEAD_DIM)
    key_raw = qkv_proj[:, query_width : query_width + key_width].reshape(length, KV_HEADS, HEAD_DIM)
    queries = (query_raw * cosine_table + rotate(query_raw) * sine_table).astype(bf16)
    key_flat = (
        (key_raw * cosine_table + rotate(key_raw) * sine_table).astype(bf16).reshape(length, key_width)
    )
    value_flat = qkv_proj[:, query_width + key_width :].astype(bf16)
    both = jnp.concatenate([key_flat, value_flat], 1)
    both = jnp.concatenate([lax.ppermute(both, "fsdp", later), both], 0)
    all_keys = both[:, :key_width].reshape(2 * length, KV_HEADS, HEAD_DIM)
    all_values = both[:, key_width:].reshape(2 * length, KV_HEADS, HEAD_DIM)
    query_groups = jnp.transpose(queries.reshape(length, KV_HEADS, groups, HEAD_DIM), (1, 0, 2, 3))
    key_groups = jnp.transpose(all_keys, (1, 0, 2))
    value_groups = jnp.transpose(all_values, (1, 0, 2))
    attended, log_totals = lax.map(
        partial(attend_group, allowed=allowed, score_scale=score_scale),
        (query_groups, key_groups, value_groups),
    )
    attended = jnp.transpose(attended, (1, 0, 2, 3)).reshape(length, query_width).astype(bf16)
    residual = input_rows + rows_dot(attended, out_pieces)
    normed_two, inverse_two = normalize(residual)
    input_two = (normed_two * gain_ffn).astype(bf16)

    def gates(rows, named):
        router = jax.nn.softmax(dot(rows, full_router), -1)
        routed = jnp.any(named[:, :, None] == jnp.arange(EXPERTS, dtype=jnp.int32), 1)
        return (router, jnp.where(routed, router, 0.0), routed)

    router, _, routed = gates(input_two, routes)
    rows_near = spread(input_two).reshape(-1, D)
    _, gates_near, _ = gates(rows_near, routes_near)

    local_experts = w_gate_up.shape[0]
    count = local_experts // (side * cores)
    mine_at = (side_at * cores + core_at) * count
    own_gate_up = lax.dynamic_slice_in_dim(w_gate_up, mine_at, count, 0)
    own_down = lax.dynamic_slice_in_dim(w_down, mine_at, count, 0)
    first_expert = shard * local_experts + mine_at
    own_gates = lax.dynamic_slice_in_dim(gates_near, first_expert, count, 1)
    grad_slots = jnp.zeros(rows_near.shape, f32)
    mixed = jnp.zeros(rows_near.shape, f32)
    gate_up_sums, down_sums, gate_grads = [], [], []
    for e in range(count):
        gate_up = dot(rows_near, own_gate_up[e])
        gate_part, up_part = gate_up[:, :F], gate_up[:, F:]
        sigmoid_g = jax.nn.sigmoid(gate_part)
        silu_g = gate_part * sigmoid_g
        hidden = silu_g * up_part
        gate = own_gates[:, e : e + 1]
        hidden_gated = (gate * hidden).astype(bf16)
        raw = dot(grads_near, own_down[e])
        gate_grads.append(jnp.sum(raw * hidden, 1))
        grad_hidden = gate * raw
        grad_gate_up = jnp.concatenate(
            [
                grad_hidden * up_part * sigmoid_g * (1.0 + gate_part * (1.0 - sigmoid_g)),
                grad_hidden * silu_g,
            ],
            -1,
        ).astype(bf16)
        gate_up_sums.append(line_sum(dot(rows_near, grad_gate_up, ((0,), (0,))).astype(bf16), "line"))
        down_sums.append(line_sum(dot(grads_near, hidden_gated, ((0,), (0,))).astype(bf16), "line"))
        mixed = mixed + dot(hidden_gated, own_down[e], ((1,), (1,)))
        grad_slots = grad_slots + dot(grad_gate_up, own_gate_up[e], ((1,), (1,)))
    blocks = len(near) * cores
    gate_grads = jnp.stack(gate_grads).reshape(count, blocks, length)
    gate_wide = jnp.zeros((blocks, EXPERTS, length), f32)
    gate_wide = lax.dynamic_update_slice_in_dim(gate_wide, jnp.transpose(gate_grads, (1, 0, 2)), first_expert, 1)
    grad_router = jnp.where(routed, collect(gate_wide).T, 0.0)
    grad_slot_sum = collect(grad_slots.astype(bf16).reshape(blocks, length, D))
    mixture = collect(mixed.astype(bf16).reshape(blocks, length, D))
    layer_out = (residual + mixture).astype(bf16)

    def assemble(sums):
        width = sums[0].shape[-1]
        own = jnp.stack(sums)
        out = jnp.zeros((local_experts, D, width), f32)
        for a in range(side):
            theirs = own if a == 0 else turn(own, "side", (a,), (side,))
            for core in range(cores):
                block = theirs if core == 0 else turn(theirs, "core", (core,), (cores,))
                at = ((side_at - a) % side * cores + (core_at - core) % cores) * count
                out = lax.dynamic_update_slice_in_dim(out, block.astype(f32), at, 0)
        return out

    grad_w_gate_up = assemble(gate_up_sums)
    grad_w_down = assemble(down_sums)

    grad_out = cotangent.astype(f32)
    grad_logits = (
        router * (grad_router - jnp.sum(router * grad_router, -1, keepdims=True))
    ).astype(bf16)
    grad_input_two = grad_slot_sum + dot(grad_logits, full_router, ((1,), (1,)))
    grad_w_router = dot(input_two, grad_logits, ((0,), (0,)))
    grad_ffn_gain = jnp.sum(grad_input_two * normed_two, 0)
    grad_residual = grad_out + norm_back(normed_two, inverse_two, grad_input_two * gain_ffn)
    grad_attn = grad_residual.astype(bf16)
    grad_w_out = dot(attended, grad_attn, ((0,), (0,)))
    grad_attended = rows_back(grad_attn, out_pieces, query_width).astype(bf16)
    grad_groups = jnp.transpose(
        grad_attended.reshape(length, KV_HEADS, groups, HEAD_DIM), (1, 0, 2, 3)
    )
    grad_query, grad_key, grad_value = lax.map(
        partial(attend_back, allowed=allowed, score_scale=score_scale),
        (query_groups, key_groups, value_groups, grad_groups, log_totals),
    )
    grad_query = jnp.transpose(grad_query, (1, 0, 2, 3)).reshape(length, HEADS, HEAD_DIM)
    grad_key = jnp.transpose(grad_key, (1, 0, 2)).reshape(2 * length, key_width)
    grad_value = jnp.transpose(grad_value, (1, 0, 2)).reshape(2 * length, key_width)
    grad_both = jnp.concatenate([grad_key, grad_value], 1)
    grad_both = grad_both[length:] + lax.ppermute(grad_both[:length].astype(bf16), "fsdp", before).astype(f32)
    grad_key = grad_both[:, :key_width].reshape(length, KV_HEADS, HEAD_DIM)
    grad_value = grad_both[:, key_width:]
    query_back = grad_query * cosine_table + rotate_back(grad_query * sine_table)
    key_back = grad_key * cosine_table + rotate_back(grad_key * sine_table)
    grad_qkv = jnp.concatenate(
        [query_back.reshape(length, query_width), key_back.reshape(length, key_width), grad_value],
        -1,
    ).astype(bf16)
    grad_w_qkv = dot(input_one, grad_qkv, ((0,), (0,)))
    grad_input_one = rows_back(grad_qkv, qkv_pieces, D)
    grad_attn_gain = jnp.sum(grad_input_one * normed_one, 0)
    grad_in = grad_residual + norm_back(normed_one, inverse_one, grad_input_one * gain_attn)
    pad = jnp.zeros((D, 128 - EXPERTS - 2), f32)
    rest = jnp.concatenate([grad_w_router, grad_attn_gain[:, None], grad_ffn_gain[:, None], pad], 1)
    out_sum = owned_sum(grad_w_out)
    qkv_sum = owned_sum(grad_w_qkv)
    rest_sum = owned_sum(rest)
    return (
        layer_out,
        grad_in,
        qkv_sum,
        out_sum,
        rest_sum[:, :EXPERTS],
        rest_sum[:, EXPERTS],
        rest_sum[:, EXPERTS + 1],
        grad_w_gate_up,
        grad_w_down,
    )


def solution(mesh):
    copies, shards = mesh.shape["rep"], mesh.shape["fsdp"]
    local = EXPERTS // shards
    cores = 2 if copies % 2 == 0 and local % 2 == 0 else 1
    side = 2 if cores == 2 and copies % 4 == 0 and local % 4 == 0 else 1
    names = ("line", "side", "core", "fsdp")
    parts = Mesh(mesh.devices.reshape(copies // (side * cores), side, cores, shards), names)
    rows, shard = P(names, None), P("fsdp", None)
    experts = P("fsdp", None, None)
    in_specs = (rows, rows, shard, shard, shard, P("fsdp"), P("fsdp"), experts, experts, rows)
    out_specs = (rows, rows, shard, shard, shard, P("fsdp"), P("fsdp"), experts, experts)
    return jax.shard_map(body, mesh=parts, in_specs=in_specs, out_specs=out_specs, check_vma=False)
```

```python
import math
from functools import partial

import jax
import jax.numpy as jnp
from jax import lax
from jax.experimental import pallas as pl
from jax.experimental.pallas import tpu as pltpu
from jax.sharding import Mesh, PartitionSpec as P

D = 1024
HEADS = 16
KV_HEADS = 8
HEAD_DIM = 64
F = 512
TOP = 8
EXPERTS = 16
BLOCK = 256
QW = HEADS * HEAD_DIM
KVW = KV_HEADS * HEAD_DIM
EXTRA = 16
CHUNKS = 2
PAIR = 2 * HEAD_DIM

norm_eps = 1e-06
masked_score = -1e30
score_scale = HEAD_DIM ** (-0.5)
bf16, f32 = jnp.bfloat16, jnp.float32
VMEM = 56 * 1024 * 1024


def dot(left, right, dims=((1,), (0,))):
    return lax.dot_general(left, right, (dims, ((), ())), preferred_element_type=f32)


def turn(value, axes, steps, sizes):
    pairs = []
    for source in range(math.prod(sizes)):
        place, rest = [], source
        for size in reversed(sizes):
            place.append(rest % size)
            rest //= size
        place.reverse()
        target = 0
        for at, size, step in zip(place, sizes, steps):
            target = target * size + (at + step) % size
        pairs.append((source, target))
    return lax.ppermute(value, axes, pairs)


def own_part(value, axis, index, parts):
    size = value.shape[axis] // parts
    return lax.dynamic_slice_in_dim(value, index * size, size, axis)


def whole(shape):
    return pl.BlockSpec(shape, lambda *_: (0,) * len(shape))


SCALARS = pl.BlockSpec(memory_space=pltpu.SMEM)
STAY = pl.BlockSpec(memory_space=pl.ANY)


def call(kernel, out_shape, in_specs, operands, out_specs=None, scratch=(), grid=None, prefetch=0, aliases=None, flops=0):
    out_specs = [whole(s.shape) for s in out_shape] if out_specs is None else out_specs
    moved = sum(math.prod(s.shape) * s.dtype.itemsize for s in list(operands) + list(out_shape))
    spec = pltpu.PrefetchScalarGridSpec(
        num_scalar_prefetch=prefetch,
        grid=grid or (1,),
        in_specs=in_specs,
        out_specs=out_specs,
        scratch_shapes=list(scratch),
    )
    return pl.pallas_call(
        kernel,
        out_shape=list(out_shape),
        grid_spec=spec,
        input_output_aliases=aliases or {},
        compiler_params=pltpu.CompilerParams(vmem_limit_bytes=VMEM),
        cost_estimate=pl.CostEstimate(flops=flops, transcendentals=0, bytes_accessed=moved),
    )(*operands)


def array(shape, dtype):
    return jax.ShapeDtypeStruct(shape, dtype)


def normalize(rows):
    scale_inv = lax.rsqrt(jnp.mean(rows * rows, -1, keepdims=True) + norm_eps)
    return (rows * scale_inv, scale_inv)


def norm_back(normed, scale_inv, grad_normed):
    return scale_inv * (grad_normed - normed * jnp.mean(grad_normed * normed, -1, keepdims=True))


def lanes(shape):
    return lax.broadcasted_iota(jnp.int32, shape, len(shape) - 1)


def halves(values):
    low = lanes(values.shape) % HEAD_DIM < HEAD_DIM // 2
    half = HEAD_DIM // 2
    return jnp.where(low, pltpu.roll(values, PAIR - half, 1), pltpu.roll(values, half, 1))


def rotary_tables(places):
    at = jnp.arange(PAIR, dtype=jnp.int32) % HEAD_DIM
    middle = HEAD_DIM // 2
    frequency = 10000.0 ** (-(2.0 * (at % middle).astype(f32)) / HEAD_DIM)
    angles = places.astype(f32)[:, None] * frequency[None, :]
    sign = jnp.where(at < middle, -1.0, 1.0)[None, :]
    return (jnp.cos(angles), jnp.sin(angles) * sign)


def load_rows(pieces, offsets, target, sems):
    copies = []
    for i, piece in enumerate(pieces):
        copy = pltpu.make_async_copy(piece, target.at[pl.ds(pl.multiple_of(offsets[i], 16), piece.shape[0]), :], sems.at[i])
        copy.start()
        copies.append(copy)
    return copies


def project(hidden_prev, hidden_own, gain, cosines, sines, pieces, offsets):
    length, count = hidden_own.shape[0], len(pieces)

    def kernel(offsets_ref, prev_ref, own_ref, gain_ref, cos_ref, sin_ref, *rest):
        piece_refs, (q_ref, kv_ref, in_ref, weight, sems) = rest[:count], rest[count:]
        copies = load_rows(piece_refs, offsets_ref, weight, sems)
        for i, ref in enumerate((prev_ref, own_ref)):
            normed, _ = normalize(ref[...].astype(f32))
            in_ref[i * length : (i + 1) * length, :] = (normed * gain_ref[...]).astype(bf16)
        for copy in copies:
            copy.wait()
        values = dot(in_ref[length:, :], weight[:, :QW])
        cos_own, sin_own = cos_ref[length:, :], sin_ref[length:, :]
        for g in range(QW // PAIR):
            u = values[:, g * PAIR : (g + 1) * PAIR]
            q_ref[:, g * PAIR : (g + 1) * PAIR] = (u * cos_own + halves(u) * sin_own).astype(bf16)
        values = dot(in_ref[...], weight[:, QW:])
        for g in range(KVW // PAIR):
            u = values[:, g * PAIR : (g + 1) * PAIR]
            kv_ref[:, g * PAIR : (g + 1) * PAIR] = (u * cos_ref[...] + halves(u) * sin_ref[...]).astype(bf16)
        kv_ref[:, KVW:] = values[:, KVW:].astype(bf16)

    width = QW + 2 * KVW
    return call(
        kernel,
        [array((length, QW), bf16), array((2 * length, 2 * KVW), bf16), array((2 * length, D), bf16)],
        [SCALARS] + [whole(v.shape) for v in (hidden_prev, hidden_own, gain, cosines, sines)] + [STAY] * count,
        (offsets, hidden_prev, hidden_own, gain, cosines, sines, *pieces),
        scratch=[pltpu.VMEM((D, width), bf16), pltpu.SemaphoreType.DMA((count,))],
        flops=6 * length * D * D,
    )


def doubled(values, which):
    low = lanes(values.shape) < HEAD_DIM
    swapped = pltpu.roll(values, HEAD_DIM, 1)
    return jnp.where(low, values, swapped) if which == 0 else jnp.where(low, swapped, values)


def two_rows(pair):
    low = lanes(pair.shape) < HEAD_DIM
    zero = jnp.zeros_like(pair)
    return jnp.concatenate([jnp.where(low, pair, zero), jnp.where(low, zero, pair)], 0)


def named_experts(routes):
    shape = (routes.shape[0], 128)
    named = routes[:, 0:1] == lanes(shape)
    for k in range(1, TOP):
        named = named | (routes[:, k : k + 1] == lanes(shape))
    return named


def attend(query, kv, hidden_own, gain, router_w, routes, pieces, offsets, flag):
    length, count = query.shape[0], len(pieces)

    def kernel(offsets_ref, flag_ref, q_ref, kv_ref, own_ref, gain_ref, router_ref, routes_ref, *rest):
        piece_refs = rest[:count]
        att_ref, lse_ref, res_ref, gate_ref, pay_ref, weight, sems = rest[count:]
        copies = load_rows(piece_refs, offsets_ref, weight, sems)
        wide = (2 * length, 2 * length)
        bias = jnp.where((lanes((1, 2 * length)) >= length) | (flag_ref[0] > 0), 0.0, masked_score)
        lse_ref[...] = jnp.zeros(lse_ref.shape, f32)

        def pair_of_keys(jj, carry):
            at = pl.multiple_of(jj * PAIR, PAIR)
            keys = kv_ref[:, pl.ds(at, PAIR)].astype(f32)
            vals = kv_ref[:, pl.ds(KVW + at, PAIR)].astype(f32)
            for t in range(2):
                place = pl.multiple_of((2 * jj + t) * PAIR, PAIR)
                both = two_rows(q_ref[:, pl.ds(place, PAIR)].astype(f32)).astype(bf16)
                scores = dot(both, doubled(keys, t).astype(bf16), ((1,), (1,))) * score_scale + bias
                largest = jnp.max(scores, -1, keepdims=True)
                exponent = jnp.exp(scores - largest)
                totals = jnp.sum(exponent, -1, keepdims=True)
                probs = (exponent * (1.0 / totals)).astype(bf16)
                lse = largest + jnp.log(totals)
                lse_ref[...] = jnp.where(lanes(lse_ref.shape) == 2 * jj + t, lse, lse_ref[...])
                val = doubled(vals, t)
                low = lanes(val.shape) < HEAD_DIM
                zero = jnp.zeros_like(val)
                out = dot(probs[:length], jnp.where(low, val, zero).astype(bf16))
                out = out + dot(probs[length:], jnp.where(low, zero, val).astype(bf16))
                att_ref[:, pl.ds(place, PAIR)] = out.astype(bf16)
            return carry

        lax.fori_loop(0, KVW // PAIR, pair_of_keys, 0)
        for copy in copies:
            copy.wait()
        residual = own_ref[...].astype(f32) + dot(att_ref[...], weight[...])
        res_ref[...] = residual
        normed, _ = normalize(residual)
        rows = (normed * gain_ref[...]).astype(bf16)
        pay_ref[:length, :] = rows
        logits = dot(rows, router_ref[...], ((1,), (1,)))
        real = lanes(logits.shape) < EXPERTS
        logits = jnp.where(real, logits, masked_score)
        raised = jnp.where(real, jnp.exp(logits - jnp.max(logits, -1, keepdims=True)), 0.0)
        router = raised * (1.0 / jnp.sum(raised, -1, keepdims=True))
        gate_ref[...] = router
        gates = jnp.where(named_experts(routes_ref[...]), router, 0.0).T[:EXTRA]
        high = gates.astype(bf16)
        pay_ref[length:, :length] = high
        pay_ref[length:, length : 2 * length] = (gates - high.astype(f32)).astype(bf16)
        pay_ref[length:, 2 * length :] = jnp.zeros((EXTRA, D - 2 * length), bf16)

    return call(
        kernel,
        [
            array((length, QW), bf16),
            array((2 * length, 128), f32),
            array((length, D), f32),
            array((length, 128), f32),
            array((length + EXTRA, D), bf16),
        ],
        [SCALARS, SCALARS] + [whole(v.shape) for v in (query, kv, hidden_own, gain, router_w, routes)] + [STAY] * count,
        (offsets, flag, query, kv, hidden_own, gain, router_w, routes, *pieces),
        scratch=[pltpu.VMEM((QW, D), bf16), pltpu.SemaphoreType.DMA((count,))],
        flops=8 * length * D * D,
    )


def expert(rows, grads, w_gate_up, w_down, index, chunk, chunks):
    sources, tall = len(rows), rows[0].shape[1]
    blocks = sources * rows[0].shape[0]
    length = tall - EXTRA
    step = 2
    part = F // chunks
    turns = rows[0].shape[0] // step

    def kernel(index_ref, *refs):
        row_refs, grad_refs = refs[:sources], refs[sources : 2 * sources]
        gate_ref, up_ref, down_ref, dgu_ref, hid_ref, sum_ref, out_ref, acc, both_ref, grad_ref, table_ref = refs[2 * sources :]
        i = pl.program_id(0)
        for source, (row_ref, source_ref) in enumerate(zip(row_refs, grad_refs)):

            @pl.when((i >= source * turns) & (i < (source + 1) * turns))
            def _():
                for b in range(step):
                    both_ref[b * length : (b + 1) * length, :] = row_ref[b, :length, :]
                    grad_ref[b * length : (b + 1) * length, :] = source_ref[b]
                    high, low = row_ref[b, length:, :length], row_ref[b, length:, length : 2 * length]
                    table_ref[b] = high.astype(f32) + low.astype(f32)

        both, grad = both_ref[...], grad_ref[...]
        columns = []
        for b in range(step):
            table = table_ref[b]
            mine = lax.broadcasted_iota(jnp.int32, table.shape, 0) == index_ref[1]
            row = jnp.sum(jnp.where(mine, table, 0.0), 0, keepdims=True)
            columns.append(jnp.broadcast_to(row, (128, length)).T[:, :1])
        gate = jnp.concatenate(columns, 0)
        gate_part, up_part = dot(both, gate_ref[0]), dot(both, up_ref[0])
        sigmoid_g = jax.nn.sigmoid(gate_part)
        silu_g = gate_part * sigmoid_g
        hidden = silu_g * up_part
        raw = dot(grad, down_ref[0])
        sums = jnp.sum(raw * hidden, 1, keepdims=True)
        gated = (gate * hidden).astype(bf16)
        grad_hidden = gate * raw
        grad_gate = (grad_hidden * up_part * sigmoid_g * (1.0 + gate_part * (1.0 - sigmoid_g))).astype(bf16)
        grad_up = (grad_hidden * silu_g).astype(bf16)
        for b in range(step):
            at = slice(b * length, (b + 1) * length)
            dgu_ref[b, :, :part] = grad_gate[at]
            dgu_ref[b, :, part:] = grad_up[at]
            hid_ref[b] = gated[at]
            sum_ref[b] = jnp.broadcast_to(sums[at], (length, 128)).T[:8]
        terms = (
            dot(both, grad_gate, ((0,), (0,))),
            dot(both, grad_up, ((0,), (0,))),
            dot(grad, gated, ((0,), (0,))),
        )
        for p, term in enumerate(terms):
            at = slice(p * part, (p + 1) * part)

            @pl.when(i == 0)
            def _():
                acc[:, at] = term

            @pl.when((i > 0) & (i < blocks // step - 1))
            def _():
                acc[:, at] += term

            @pl.when(i == blocks // step - 1)
            def _():
                out_ref[:, at] = (acc[:, at] + term).astype(bf16)

    def block(*shape):
        return pl.BlockSpec((step,) + shape, lambda i, index: (i,) + (0,) * len(shape))

    def source_block(source, *shape):
        def at(i, index):
            return (jnp.clip(i - source * turns, 0, turns - 1),) + (0,) * len(shape)

        return pl.BlockSpec((step,) + shape, at)

    def columns_of(at):
        return pl.BlockSpec((1, D, part), lambda i, index: (index[0], 0, at))

    return call(
        kernel,
        [
            array((blocks, length, 2 * part), bf16),
            array((blocks, length, part), bf16),
            array((blocks, 8, length), f32),
            array((D, 3 * part), bf16),
        ],
        [source_block(s, tall, D) for s in range(sources)]
        + [source_block(s, length, D) for s in range(sources)]
        + [columns_of(chunk), columns_of(chunks + chunk), columns_of(chunk)],
        (index, *rows, *grads, w_gate_up, w_gate_up, w_down),
        out_specs=[
            block(length, 2 * part),
            block(length, part),
            block(8, length),
            pl.BlockSpec((D, 3 * part), lambda i, index: (0, 0)),
        ],
        scratch=[
            pltpu.VMEM((D, 3 * part), f32),
            pltpu.VMEM((step * length, D), bf16),
            pltpu.VMEM((step * length, D), bf16),
            pltpu.VMEM((step, EXTRA, length), f32),
        ],
        grid=(blocks // step,),
        prefetch=1,
        flops=blocks * length * D * part * 12,
    )


def row_grads(parts, sums, weights, indices, chunks):
    blocks, length = parts[0].shape[0], parts[0].shape[1]
    count, experts = len(parts), len(parts) // chunks
    wide = parts[0].shape[2] * chunks // F
    part = F // chunks
    tall = length + (EXTRA if sums else 0)
    step = 2

    def kernel(indices_ref, *refs):
        part_refs, weight_refs = refs[:count], refs[count : count + experts]
        sum_refs, out_ref = refs[count + experts : -1], refs[-1]
        total = None
        for e in range(experts):
            for c in range(chunks):
                ref = part_refs[e * chunks + c]
                both = jnp.concatenate([ref[b] for b in range(step)], 0)
                for w in range(wide):
                    at = w * F + c * part
                    term = dot(both[:, w * part : (w + 1) * part], weight_refs[e][0, :, at : at + part], ((1,), (1,)))
                    total = term if total is None else total + term
        for b in range(step):
            out_ref[b, :length, :] = total[b * length : (b + 1) * length].astype(bf16)
            if sums:
                table = jnp.zeros((EXTRA, length), f32)
                at = lax.broadcasted_iota(jnp.int32, table.shape, 0)
                for e in range(experts):
                    grads = sum_refs[e * chunks][b, :1, :]
                    for c in range(1, chunks):
                        grads = grads + sum_refs[e * chunks + c][b, :1, :]
                    table = jnp.where(at == indices_ref[2 * e + 1], grads, table)
                high = table.astype(bf16)
                out_ref[b, length:, :length] = high
                out_ref[b, length:, length : 2 * length] = (table - high.astype(f32)).astype(bf16)
                out_ref[b, length:, 2 * length :] = jnp.zeros((EXTRA, D - 2 * length), bf16)

    def block(*shape):
        return pl.BlockSpec((step,) + shape, lambda i, index: (i,) + (0,) * len(shape))

    def weight(e):
        return pl.BlockSpec((1,) + weights.shape[1:], lambda i, index: (index[2 * e], 0, 0))

    return call(
        kernel,
        [array((blocks, tall, D), bf16)],
        [block(*v.shape[1:]) for v in parts] + [weight(e) for e in range(experts)] + [block(8, length)] * len(sums),
        (indices, *parts, *[weights] * experts, *sums),
        out_specs=[block(tall, D)],
        grid=(blocks // step,),
        prefetch=1,
        flops=blocks * length * D * part * wide * 2 * count,
    )[0]


def middle_back(returned, residual, router, routes, cotangent, gain, router_w, pieces, offsets):
    length, count, terms = residual.shape[0], len(pieces), len(returned)

    def kernel(offsets_ref, *rest):
        term_refs, rest = rest[:terms], rest[terms:]
        res_ref, gate_ref, routes_ref, cot_ref, gain_ref, router_ref = rest[:6]
        piece_refs = rest[6 : 6 + count]
        gres_ref, gatt_ref, small_ref, weight, sems = rest[6 + count :]
        copies = load_rows(piece_refs, offsets_ref, weight, sems)
        total = term_refs[0][...].astype(f32)
        for ref in term_refs[1:]:
            total = total + ref[...].astype(f32)
        table = total[length:, :length] + total[length:, length : 2 * length]
        gate_grads = jnp.concatenate([table, jnp.zeros((128 - EXTRA, length), f32)], 0).T
        grad_router = jnp.where(named_experts(routes_ref[...]), gate_grads, 0.0)
        router = gate_ref[...]
        grad_logits = (router * (grad_router - jnp.sum(router * grad_router, -1, keepdims=True))).astype(bf16)
        grad_input = total[:length] + dot(grad_logits, router_ref[...])
        normed, inverse = normalize(res_ref[...])
        gain_row = gain_ref[...]
        rows = (normed * gain_row).astype(bf16)
        small_ref[...] = dot(rows, grad_logits, ((0,), (0,)))
        gain_grad = jnp.sum(grad_input * normed, 0, keepdims=True)
        column = jnp.broadcast_to(gain_grad, (128, D)).T
        small_ref[...] = jnp.where(lanes((D, 128)) == EXPERTS, column, small_ref[...])
        grad_residual = cot_ref[...].astype(f32) + norm_back(normed, inverse, grad_input * gain_row)
        gres_ref[...] = grad_residual
        grad_attn = grad_residual.astype(bf16)
        for copy in copies:
            copy.wait()
        gatt_ref[...] = dot(grad_attn, weight[...], ((1,), (1,))).astype(bf16)

    operands = (*returned, residual, router, routes, cotangent, gain, router_w)
    return call(
        kernel,
        [array((length, D), f32), array((length, QW), bf16), array((D, 128), f32)],
        [SCALARS] + [whole(v.shape) for v in operands] + [STAY] * count,
        (offsets, *operands, *pieces),
        scratch=[pltpu.VMEM((QW, D), bf16), pltpu.SemaphoreType.DMA((count,))],
        flops=5 * length * D * D,
    )


def attend_back(query, kv, grad, lse, cosines, sines, flag):
    length = query.shape[0]

    def kernel(flag_ref, q_ref, kv_ref, grad_ref, lse_ref, cos_ref, sin_ref, dq_ref, dkv_ref):
        bias = jnp.where((lanes((1, 2 * length)) >= length) | (flag_ref[0] > 0), 0.0, masked_score)
        cos_own, sin_own = cos_ref[length:, :], sin_ref[length:, :]

        def back(values, cos, sin):
            return (values * cos - halves(values) * sin).astype(bf16)

        def pair_of_keys(jj, carry):
            at = pl.multiple_of(jj * PAIR, PAIR)
            keys = kv_ref[:, pl.ds(at, PAIR)].astype(f32)
            vals = kv_ref[:, pl.ds(KVW + at, PAIR)].astype(f32)
            key_grads, val_grads = [], []
            for t in range(2):
                place = pl.multiple_of((2 * jj + t) * PAIR, PAIR)
                both = two_rows(q_ref[:, pl.ds(place, PAIR)].astype(f32)).astype(bf16)
                outs = two_rows(grad_ref[:, pl.ds(place, PAIR)].astype(f32)).astype(bf16)
                key = doubled(keys, t).astype(bf16)
                val = doubled(vals, t).astype(bf16)
                own = lanes(lse_ref.shape) == 2 * jj + t
                total = jnp.sum(jnp.where(own, lse_ref[...], 0.0), -1, keepdims=True)
                scores = dot(both, key, ((1,), (1,))) * score_scale + bias
                probs = jnp.exp(scores - total)
                grad_probs = dot(outs, val, ((1,), (1,)))
                inner = jnp.sum(probs * grad_probs, -1, keepdims=True)
                grad_scores = (probs * (grad_probs - inner)).astype(bf16)
                grad_query = dot(grad_scores, key) * score_scale
                low = lanes((length, PAIR)) < HEAD_DIM
                grad_query = jnp.where(low, grad_query[:length], grad_query[length:])
                dq_ref[:, pl.ds(place, PAIR)] = back(grad_query, cos_own, sin_own)
                key_grad = dot(grad_scores, both, ((0,), (0,))) * score_scale
                val_grad = dot(probs.astype(bf16), outs, ((0,), (0,)))
                key_grads.append(key_grad + pltpu.roll(key_grad, HEAD_DIM, 1))
                val_grads.append(val_grad + pltpu.roll(val_grad, HEAD_DIM, 1))
            low = lanes((2 * length, PAIR)) < HEAD_DIM
            dkv_ref[:, pl.ds(at, PAIR)] = back(jnp.where(low, *key_grads), cos_ref[...], sin_ref[...])
            dkv_ref[:, pl.ds(KVW + at, PAIR)] = jnp.where(low, *val_grads).astype(bf16)
            return carry

        lax.fori_loop(0, KVW // PAIR, pair_of_keys, 0)

    operands = (query, kv, grad, lse, cosines, sines)
    return call(
        kernel,
        [array((length, QW), bf16), array((2 * length, 2 * KVW), bf16)],
        [SCALARS] + [whole(v.shape) for v in operands],
        (flag, *operands),
        flops=20 * length * D * D,
    )


def project_back(inputs, grad_query, grad_kv, hidden_prev, hidden_own, attended, grad_residual, small, pieces, offsets, parts):
    length, count = grad_query.shape[0], len(pieces)
    width = QW + 2 * KVW

    def kernel(offsets_ref, in_ref, dq_ref, dkv_ref, prev_ref, own_ref, att_ref, res_ref, small_ref, *rest):
        piece_refs, (grad_ref, gown_ref, gprev_ref, weight, sems) = rest[:count], rest[count:]
        copies = load_rows(piece_refs, offsets_ref, weight, sems)
        rows = D // parts

        def write(at, values):
            for p in range(parts):
                grad_ref[p, :, at : at + values.shape[1]] = values[p * rows : (p + 1) * rows].astype(bf16)

        write(0, dot(in_ref[length:, :], dq_ref[...], ((0,), (0,))))
        write(QW, dot(in_ref[...], dkv_ref[...], ((0,), (0,))))
        write(width, dot(att_ref[...], res_ref[...].astype(bf16), ((0,), (0,))))
        for copy in copies:
            copy.wait()
        from_kv = dot(dkv_ref[...], weight[:, QW:], ((1,), (1,)))
        own = from_kv[length:] + dot(dq_ref[...], weight[:, :QW], ((1,), (1,)))
        gown_ref[...] = own
        gprev_ref[...] = from_kv[:length].astype(bf16)
        normed_own, _ = normalize(own_ref[...].astype(f32))
        normed_prev, _ = normalize(prev_ref[...].astype(f32))
        gain_grad = jnp.sum(own * normed_own + from_kv[:length] * normed_prev, 0, keepdims=True)
        column = jnp.broadcast_to(gain_grad, (128, D)).T
        write(width + D, jnp.where(lanes((D, 128)) == EXPERTS + 1, column, small_ref[...]))

    operands = (inputs, grad_query, grad_kv, hidden_prev, hidden_own, attended, grad_residual, small)
    return call(
        kernel,
        [array((parts, D // parts, width + D + 128), bf16), array((length, D), f32), array((length, D), bf16)],
        [SCALARS] + [whole(v.shape) for v in operands] + [STAY] * count,
        (offsets, *operands, *pieces),
        scratch=[pltpu.VMEM((D, width), bf16), pltpu.SemaphoreType.DMA((count,))],
        flops=10 * length * D * D,
    )


def first_back(grad_own, grad_later, grad_residual, hidden_own, gain):
    def kernel(own_ref, later_ref, res_ref, hid_ref, gain_ref, out_ref):
        normed, inverse = normalize(hid_ref[...].astype(f32))
        grad = (own_ref[...] + later_ref[...].astype(f32)) * gain_ref[...]
        out_ref[...] = res_ref[...] + norm_back(normed, inverse, grad)

    operands = (grad_own, grad_later, grad_residual, hidden_own, gain)
    return call(kernel, [array(grad_own.shape, f32)], [whole(v.shape) for v in operands], operands)[0]


def place(sources, experts, outs, shapes, chunk, chunks):
    part = F // chunks
    count = sum(source.shape[0] for source in sources)

    def kernel(experts_ref, *refs):
        source_refs = refs[: len(sources)]
        gate_up_ref, down_ref, wide, sems = refs[len(sources) + len(outs) :]
        copies = []
        values = [ref.at[i] for ref in source_refs for i in range(ref.shape[0])]
        for i, source in enumerate(values):
            wide[i] = source[...].astype(f32)
            for p, target in enumerate(
                (
                    gate_up_ref.at[experts_ref[i], :, chunk * part : (chunk + 1) * part],
                    gate_up_ref.at[experts_ref[i], :, F + chunk * part : F + (chunk + 1) * part],
                    down_ref.at[experts_ref[i], :, chunk * part : (chunk + 1) * part],
                )
            ):
                copy = pltpu.make_async_copy(wide.at[i, :, p * part : (p + 1) * part], target, sems.at[i, p])
                copy.start()
                copies.append(copy)
        for copy in copies:
            copy.wait()

    return call(
        kernel,
        shapes,
        [SCALARS] + [whole(v.shape) for v in sources] + [STAY] * len(outs),
        (experts, *sources, *outs),
        out_specs=[STAY, STAY],
        scratch=[pltpu.VMEM((count, D, 3 * part), f32), pltpu.SemaphoreType.DMA((count, 3))],
        aliases={1 + len(sources) + i: i for i in range(len(outs))},
    )


def unpack(sources, offsets, rows):
    count = sum(source.shape[0] for source in sources)
    deep, wide = sources[0].shape[1:]
    widths = (QW + 2 * KVW, D, wide - QW - 2 * KVW - D)

    def kernel(offsets_ref, *refs):
        source_refs, out_refs, (values_ref, sems) = refs[: len(sources)], refs[len(sources) : -2], refs[-2:]
        copies = []
        for i, source in enumerate([ref.at[i] for ref in source_refs for i in range(ref.shape[0])]):
            values_ref[i] = source[...].astype(f32)
            start = 0
            for p, (out_ref, width) in enumerate(zip(out_refs, widths)):
                target = out_ref.at[pl.ds(pl.multiple_of(offsets_ref[i], 8), deep), :]
                copy = pltpu.make_async_copy(values_ref.at[i, :, start : start + width], target, sems.at[i, p])
                copy.start()
                copies.append(copy)
                start += width
        for copy in copies:
            copy.wait()

    return call(
        kernel,
        [array((rows, width), f32) for width in widths],
        [SCALARS] + [whole(v.shape) for v in sources],
        (offsets, *sources),
        out_specs=[STAY] * 3,
        scratch=[pltpu.VMEM((count, deep, wide), f32), pltpu.SemaphoreType.DMA((count, 3))],
    )


def tie(values, after):
    return lax.optimization_barrier((values, after))[0]


def doubling_sum(value, axis):
    count, step = lax.axis_size(axis), 1
    if count & (count - 1):
        return lax.psum(value, axis)
    while step < count:
        value = value + lax.ppermute(value, axis, [(i, i ^ step) for i in range(count)])
        step *= 2
    return value


def body(
    hidden_in, routes, w_qkv, w_out, w_router, attn_gain, ffn_gain, w_gate_up, w_down, cotangent
):
    length = hidden_in.shape[0]
    line, shards = lax.axis_size("line"), lax.axis_size("fsdp")
    side, cores = lax.axis_size("side"), lax.axis_size("core")
    shard, side_at, core_at = lax.axis_index("fsdp"), lax.axis_index("side"), lax.axis_index("core")
    near = [(a, s) for s in range(shards) for a in range(side)]
    local_experts = w_gate_up.shape[0]
    count = local_experts // (side * cores)
    barrier = lax.optimization_barrier

    def other_core(value, core=1):
        return turn(value, "core", (core,), (cores,))

    def other_side(value, step=1):
        return turn(value, "side", (step,), (side,))

    def fetch(piece, after=()):
        rows = piece.shape[0]
        out, offsets = [piece], [shard * rows]
        part = own_part(piece, 0, core_at * side + side_at, cores * side)
        if after:
            part = tie(part, after)
        small_rows = part.shape[0]
        for step in range(1, shards):
            base = (shard - step) % shards * rows
            first = turn(part, "fsdp", (step,), (shards,))
            for a in range(side):
                theirs = other_side(first, a) if a else first
                for core in range(cores):
                    out.append(other_core(theirs, core) if core else theirs)
                    at = (core_at - core) % cores * side + (side_at - a) % side
                    offsets.append(base + at * small_rows)
        return out, jnp.stack(offsets).astype(jnp.int32)

    def over_cores(first):
        return [other_core(first, core) if core else first for core in range(cores)]

    def core_sums(blocks):
        total = blocks[: len(near)]
        for core in range(1, cores):
            total = total + other_core(blocks[core * len(near) : (core + 1) * len(near)], -core % cores)
        return total

    def shard_sums(total, step_of=None):
        total = total.reshape((shards, side) + total.shape[1:])
        out = total[0].astype(f32)
        for s in range(1, shards):
            out = out + turn(total[s], "fsdp", (-s % shards,), (shards,)).astype(f32)
        return out.astype(bf16)

    def send_back(total):
        out = [total[0]]
        for i, (a, s) in enumerate(near):
            if (a, s) != (0, 0):
                out.append(turn(total[i], ("side", "fsdp"), (-a % side, -s % shards), (side, shards)))
        return out

    parity = shard % 2
    flag = parity.astype(jnp.int32)[None]
    later = [(i, i + 1) for i in range(0, shards, 2)]
    before = [(i + 1, i) for i in range(0, shards, 2)]
    small_rows = w_router.shape[0]
    small = jnp.concatenate([w_router.T, attn_gain[None], ffn_gain[None]], 0)
    qkv_pieces, qkv_offsets = fetch(w_qkv)
    hidden_prev = lax.ppermute(hidden_in, "fsdp", later)
    full_small = jnp.zeros((EXPERTS + 2, D), bf16)
    for step in range(shards):
        theirs = turn(small, "fsdp", (step,), (shards,)) if step else small
        full_small = lax.dynamic_update_slice_in_dim(full_small, theirs, (shard - step) % shards * small_rows, 1)
    gain_attn = full_small[EXPERTS : EXPERTS + 1].astype(f32)
    gain_ffn = full_small[EXPERTS + 1 :].astype(f32)
    router_w = jnp.pad(full_small[:EXPERTS], ((0, 128 - EXPERTS), (0, 0)))
    sideways = jnp.stack([other_side(cotangent, a) if a else cotangent for a in range(side)])
    out_pieces, out_offsets = fetch(w_out, (hidden_prev, qkv_pieces[1:]))
    sideways = tie(sideways, out_pieces[1:2])
    grads_near = [turn(sideways, "fsdp", (s,), (shards,)) if s else sideways for s in range(shards)]
    grads_near = over_cores(jnp.concatenate(grads_near, 0))
    rows_at = jnp.arange(length, dtype=jnp.int32)
    cosines, sines = rotary_tables(jnp.concatenate([rows_at, parity * length + rows_at]))

    queries, kv, inputs = project(hidden_prev, hidden_in, gain_attn, cosines, sines, qkv_pieces, qkv_offsets)
    attended, lse, residual, router, payload = attend(
        queries, kv, hidden_in, gain_ffn, router_w, routes, out_pieces, out_offsets, flag
    )
    rows_near = [turn(payload, ("side", "fsdp"), (a, s), (side, shards)) if (a, s) != (0, 0) else payload for a, s in near]
    rows_near = over_cores(jnp.stack(rows_near))

    mine_at = (side_at * cores + core_at) * count
    indices = [jnp.stack([mine_at + e, shard * local_experts + mine_at + e]).astype(jnp.int32) for e in range(count)]
    minis = [(e, c) for e in range(count) for c in range(CHUNKS)]
    number = len(minis)
    order = jnp.stack([((side_at - a) % side * cores + (core_at - core) % cores) for core in range(cores) for a in range(side)])
    order = order.astype(jnp.int32)
    shapes = [array((local_experts, D, 2 * F), f32), array((local_experts, D, F), f32)]

    now = {"indices": indices, "offsets": (out_offsets, qkv_offsets), "order": order, "chunks": {}, "outs": ()}
    now.update(half={}, total={}, full={}, pair={}, grads_gu=[], hiddens=[], sums=[])
    flying = {}

    def mini():
        i = len(now["sums"])
        e, c = minis[i]
        found = expert(rows_near, grads_near, w_gate_up, w_down, now["indices"][e], c, CHUNKS)
        now["grads_gu"].append(found[0])
        now["hiddens"].append(found[1])
        now["sums"].append(found[2])
        now["chunks"][i] = found[3]

    def returns():
        grads = row_grads(now["grads_gu"], now["sums"], w_gate_up, jnp.concatenate(now["indices"]), CHUNKS)
        flying["returned"] = send_back(core_sums(grads))
        now["indices"] = tie(now["indices"], grads)
        now["mixed"] = row_grads(now["hiddens"], (), w_down, jnp.concatenate(now["indices"]), CHUNKS)
        for name in ("grads_gu", "hiddens", "sums"):
            del now[name]

    def middle():
        now["grad_residual"], grad_attended, now["small"] = middle_back(
            flying.pop("returned"), residual, router, routes, cotangent, gain_ffn, router_w, out_pieces, now["offsets"][0]
        )
        now["grad_query"], now["grad_kv"] = attend_back(queries, kv, grad_attended, lse, cosines, sines, flag)

    def ending():
        weights, now["grad_own"], grad_prev = project_back(
            inputs, now.pop("grad_query"), now.pop("grad_kv"), hidden_prev, hidden_in, attended,
            now["grad_residual"], now.pop("small"), qkv_pieces, now["offsets"][1], shards * cores * side,
        )
        weights = weights.reshape((shards, cores, side) + weights.shape[1:])
        total = own_part(weights, 1, core_at, cores)
        for core in range(1, cores):
            total = total + other_core(own_part(weights, 1, (core_at + core) % cores, cores), core)
        flying["owned"] = own_part(total, 0, shard, shards)
        for step in range(1, shards):
            theirs = turn(own_part(total, 0, (shard + step) % shards, shards), "fsdp", (step,), (shards,))
            flying["owned"] = flying["owned"] + theirs
        flying["grad_later"] = lax.ppermute(tie(grad_prev, total), "fsdp", before)

    def sideways_sum():
        value = flying.pop("owned")
        total = own_part(value, 2, side_at, side)
        for a in range(1, side):
            total = total + other_side(own_part(value, 2, (side_at + a) % side, side), a)
        flying["chunk"] = total[0, 0, 0]

    def first():
        now["grad_in"] = first_back(now["grad_own"], flying.pop("grad_later"), now["grad_residual"], hidden_in, gain_attn)

    def mixture_one():
        flying["mixed"] = shard_sums(core_sums(now.pop("mixed")))

    def mixture_two():
        mixed = flying.pop("mixed")
        total = residual + mixed[0].astype(f32)
        for a in range(1, side):
            total = total + other_side(mixed[a], -a % side).astype(f32)
        now["layer_out"] = total.astype(bf16)

    def last_chunk():
        now["chunks"][number] = flying.pop("chunk")

    def put(i, sources):
        if i < number:
            e, c = minis[i]
            now["outs"] = place(sources, now["order"] * count + e, now["outs"], shapes, c, CHUNKS)
        else:
            rows = sources[0].shape[1]
            at = jnp.stack([(core_at - core) % cores * side + (side_at - a) % side for core in range(cores) for a in range(side)])
            now["owned"] = unpack(sources, at.astype(jnp.int32) * rows, rows * cores * side)

    jobs = {
        0: [mini, mini],
        1: [mini] * (number - 3) + [returns],
        2: [middle],
        3: [ending],
        4: [sideways_sum, mixture_one, last_chunk],
        5: [first, mixture_two],
    }
    if number < 4:
        jobs.update({0: [mini] * (number - 1), 1: [returns]})
    mini()
    place_at = lax.axis_index("line")
    end = (place_at == 0) | (place_at == line - 1)
    entry = {i: i for i in range(number)}
    entry[number] = max(number, 5)
    for r in range(entry[number] + 5):
        got = {}
        enters = [i for i in entry if entry[i] == r]
        at = {s: [i for i in entry if entry[i] + s == r] for s in range(5)}
        if line == 4:
            raw = now["chunks"].get(enters[0]) if enters else None
            leaves = at[2]
            done = now["total"].get(leaves[0]) if leaves else None
            if raw is not None and done is not None and raw.shape == done.shape:
                got["pair"] = lax.ppermute(jnp.where(end, raw, done), "line", [(0, 1), (1, 0), (2, 3), (3, 2)])
            else:
                if raw is not None:
                    got["in"] = lax.ppermute(raw, "line", [(0, 1), (3, 2)])
                if done is not None:
                    got["out"] = lax.ppermute(done, "line", [(1, 0), (2, 3)])
            for i in at[1]:
                got["middle"] = lax.ppermute(now["half"][i], "line", [(1, 2), (2, 1)])
        else:
            for i in at[2]:
                now["full"][i] = doubling_sum(now["chunks"][i], "line")
        for i in at[3]:
            got["side"] = [other_side(now["full"][i], a) for a in range(1, side)]
        for i in at[4]:
            got["core"] = [other_core(now["pair"][i], core) for core in range(1, cores)]
        for job in jobs.get(r, ()):
            job()
        now, got = barrier((now, got))
        for i in at[4]:
            put(i, [now["pair"].pop(i)] + got["core"])
        for i in at[3]:
            now["pair"][i] = jnp.stack([now["full"].pop(i)] + got["side"])
        if line == 4:
            for i in at[2]:
                now["full"][i] = jnp.where(end, got["pair"] if "pair" in got else got["out"], now["total"].pop(i))
            for i in at[1]:
                now["total"][i] = now["half"].pop(i) + got["middle"]
            for i in enters:
                now["half"][i] = now["chunks"].pop(i) + (got["pair"] if "pair" in got else got["in"])

    qkv_sum, out_sum, rest = now["owned"]
    return (
        now["layer_out"],
        now["grad_in"],
        qkv_sum,
        out_sum,
        rest[:, :EXPERTS],
        rest[:, EXPERTS + 1],
        rest[:, EXPERTS],
        now["outs"][0],
        now["outs"][1],
    )


def solution(mesh):
    copies, shards = mesh.shape["rep"], mesh.shape["fsdp"]
    local = EXPERTS // shards
    cores = 2 if copies % 2 == 0 and local % 2 == 0 else 1
    side = 2 if cores == 2 and copies % 4 == 0 and local % 4 == 0 else 1
    names = ("line", "side", "core", "fsdp")
    parts = Mesh(mesh.devices.reshape(copies // (side * cores), side, cores, shards), names)
    rows, shard = P(names, None), P("fsdp", None)
    experts = P("fsdp", None, None)
    in_specs = (rows, rows, shard, shard, shard, P("fsdp"), P("fsdp"), experts, experts, rows)
    out_specs = (rows, rows, shard, shard, shard, P("fsdp"), P("fsdp"), experts, experts)
    return jax.shard_map(body, mesh=parts, in_specs=in_specs, out_specs=out_specs, check_vma=False)
```

```python
import math
from functools import partial

import jax
import jax.numpy as jnp
from jax import lax
from jax.experimental import pallas as pl
from jax.experimental.pallas import tpu as pltpu
from jax.sharding import Mesh, PartitionSpec as P

D = 1024
HEADS = 16
KV_HEADS = 8
HEAD_DIM = 64
F = 512
TOP = 8
EXPERTS = 16
BLOCK = 256
QW = HEADS * HEAD_DIM
KVW = KV_HEADS * HEAD_DIM
EXTRA = 16
CHUNKS = 2
PAIR = 2 * HEAD_DIM

norm_eps = 1e-06
masked_score = -1e30
score_scale = HEAD_DIM ** (-0.5)
bf16, f32 = jnp.bfloat16, jnp.float32
VMEM = 56 * 1024 * 1024


def dot(left, right, dims=((1,), (0,))):
    return lax.dot_general(left, right, (dims, ((), ())), preferred_element_type=f32)


def turn(value, axes, steps, sizes):
    pairs = []
    for source in range(math.prod(sizes)):
        place, rest = [], source
        for size in reversed(sizes):
            place.append(rest % size)
            rest //= size
        place.reverse()
        target = 0
        for at, size, step in zip(place, sizes, steps):
            target = target * size + (at + step) % size
        pairs.append((source, target))
    return lax.ppermute(value, axes, pairs)


def own_part(value, axis, index, parts):
    size = value.shape[axis] // parts
    return lax.dynamic_slice_in_dim(value, index * size, size, axis)


def whole(shape):
    return pl.BlockSpec(shape, lambda *_: (0,) * len(shape))


SCALARS = pl.BlockSpec(memory_space=pltpu.SMEM)
STAY = pl.BlockSpec(memory_space=pl.ANY)


def call(kernel, out_shape, in_specs, operands, out_specs=None, scratch=(), grid=None, prefetch=0, aliases=None):
    out_specs = [whole(s.shape) for s in out_shape] if out_specs is None else out_specs
    spec = pltpu.PrefetchScalarGridSpec(
        num_scalar_prefetch=prefetch,
        grid=grid or (1,),
        in_specs=in_specs,
        out_specs=out_specs,
        scratch_shapes=list(scratch),
    )
    return pl.pallas_call(
        kernel,
        out_shape=list(out_shape),
        grid_spec=spec,
        input_output_aliases=aliases or {},
        compiler_params=pltpu.CompilerParams(vmem_limit_bytes=VMEM),
        cost_estimate=pl.CostEstimate(flops=0, transcendentals=0, bytes_accessed=0),
    )(*operands)


def array(shape, dtype):
    return jax.ShapeDtypeStruct(shape, dtype)


def normalize(rows):
    scale_inv = lax.rsqrt(jnp.mean(rows * rows, -1, keepdims=True) + norm_eps)
    return (rows * scale_inv, scale_inv)


def norm_back(normed, scale_inv, grad_normed):
    return scale_inv * (grad_normed - normed * jnp.mean(grad_normed * normed, -1, keepdims=True))


def lanes(shape):
    return lax.broadcasted_iota(jnp.int32, shape, len(shape) - 1)


def halves(values):
    low = lanes(values.shape) % HEAD_DIM < HEAD_DIM // 2
    half = HEAD_DIM // 2
    return jnp.where(low, pltpu.roll(values, PAIR - half, 1), pltpu.roll(values, half, 1))


def rotary_tables(places):
    at = jnp.arange(PAIR, dtype=jnp.int32) % HEAD_DIM
    middle = HEAD_DIM // 2
    frequency = 10000.0 ** (-(2.0 * (at % middle).astype(f32)) / HEAD_DIM)
    angles = places.astype(f32)[:, None] * frequency[None, :]
    sign = jnp.where(at < middle, -1.0, 1.0)[None, :]
    return (jnp.cos(angles), jnp.sin(angles) * sign)


def load_rows(pieces, offsets, target, sems):
    copies = []
    for i, piece in enumerate(pieces):
        copy = pltpu.make_async_copy(piece, target.at[pl.ds(pl.multiple_of(offsets[i], 16), piece.shape[0]), :], sems.at[i])
        copy.start()
        copies.append(copy)
    return copies


def project(hidden_prev, hidden_own, gain, cosines, sines, pieces, offsets):
    length, count = hidden_own.shape[0], len(pieces)

    def kernel(offsets_ref, prev_ref, own_ref, gain_ref, cos_ref, sin_ref, *rest):
        piece_refs, (q_ref, kv_ref, in_ref, weight, sems) = rest[:count], rest[count:]
        copies = load_rows(piece_refs, offsets_ref, weight, sems)
        for i, ref in enumerate((prev_ref, own_ref)):
            normed, _ = normalize(ref[...].astype(f32))
            in_ref[i * length : (i + 1) * length, :] = (normed * gain_ref[...]).astype(bf16)
        for copy in copies:
            copy.wait()
        values = dot(in_ref[length:, :], weight[:, :QW])
        cos_own, sin_own = cos_ref[length:, :], sin_ref[length:, :]
        for g in range(QW // PAIR):
            u = values[:, g * PAIR : (g + 1) * PAIR]
            q_ref[:, g * PAIR : (g + 1) * PAIR] = (u * cos_own + halves(u) * sin_own).astype(bf16)
        values = dot(in_ref[...], weight[:, QW:])
        for g in range(KVW // PAIR):
            u = values[:, g * PAIR : (g + 1) * PAIR]
            kv_ref[:, g * PAIR : (g + 1) * PAIR] = (u * cos_ref[...] + halves(u) * sin_ref[...]).astype(bf16)
        kv_ref[:, KVW:] = values[:, KVW:].astype(bf16)

    width = QW + 2 * KVW
    return call(
        kernel,
        [array((length, QW), bf16), array((2 * length, 2 * KVW), bf16), array((2 * length, D), bf16)],
        [SCALARS] + [whole(v.shape) for v in (hidden_prev, hidden_own, gain, cosines, sines)] + [STAY] * count,
        (offsets, hidden_prev, hidden_own, gain, cosines, sines, *pieces),
        scratch=[pltpu.VMEM((D, width), bf16), pltpu.SemaphoreType.DMA((count,))],
    )


def doubled(values, which):
    low = lanes(values.shape) < HEAD_DIM
    swapped = pltpu.roll(values, HEAD_DIM, 1)
    return jnp.where(low, values, swapped) if which == 0 else jnp.where(low, swapped, values)


def two_rows(pair):
    low = lanes(pair.shape) < HEAD_DIM
    zero = jnp.zeros_like(pair)
    return jnp.concatenate([jnp.where(low, pair, zero), jnp.where(low, zero, pair)], 0)


def named_experts(routes):
    shape = (routes.shape[0], 128)
    named = routes[:, 0:1] == lanes(shape)
    for k in range(1, TOP):
        named = named | (routes[:, k : k + 1] == lanes(shape))
    return named


def attend(query, kv, flag):
    length = query.shape[0]

    def kernel(flag_ref, q_ref, kv_ref, att_ref, lse_ref):
        bias = jnp.where((lanes((1, 2 * length)) >= length) | (flag_ref[0] > 0), 0.0, masked_score)
        lse_ref[...] = jnp.zeros(lse_ref.shape, f32)

        def pair_of_keys(jj, carry):
            at = pl.multiple_of(jj * PAIR, PAIR)
            keys = kv_ref[:, pl.ds(at, PAIR)].astype(f32)
            vals = kv_ref[:, pl.ds(KVW + at, PAIR)].astype(f32)
            for t in range(2):
                place = pl.multiple_of((2 * jj + t) * PAIR, PAIR)
                both = two_rows(q_ref[:, pl.ds(place, PAIR)].astype(f32)).astype(bf16)
                scores = dot(both, doubled(keys, t).astype(bf16), ((1,), (1,))) * score_scale + bias
                largest = jnp.max(scores, -1, keepdims=True)
                exponent = jnp.exp(scores - largest)
                totals = jnp.sum(exponent, -1, keepdims=True)
                probs = (exponent * (1.0 / totals)).astype(bf16)
                lse = largest + jnp.log(totals)
                lse_ref[...] = jnp.where(lanes(lse_ref.shape) == 2 * jj + t, lse, lse_ref[...])
                val = doubled(vals, t)
                low = lanes(val.shape) < HEAD_DIM
                zero = jnp.zeros_like(val)
                out = dot(probs[:length], jnp.where(low, val, zero).astype(bf16))
                out = out + dot(probs[length:], jnp.where(low, zero, val).astype(bf16))
                att_ref[:, pl.ds(place, PAIR)] = out.astype(bf16)
            return carry

        lax.fori_loop(0, KVW // PAIR, pair_of_keys, 0)

    return call(
        kernel,
        [array((length, QW), bf16), array((2 * length, 128), f32)],
        [SCALARS, whole(query.shape), whole(kv.shape)],
        (flag, query, kv),
    )


def enter_experts(attended, hidden_own, gain, router_w, routes, pieces, offsets):
    length, count = attended.shape[0], len(pieces)

    def kernel(offsets_ref, att_ref, own_ref, gain_ref, router_ref, routes_ref, *rest):
        piece_refs, (res_ref, gate_ref, pay_ref, weight, sems) = rest[:count], rest[count:]
        copies = load_rows(piece_refs, offsets_ref, weight, sems)
        for copy in copies:
            copy.wait()
        residual = own_ref[...].astype(f32) + dot(att_ref[...], weight[...])
        res_ref[...] = residual
        normed, _ = normalize(residual)
        rows = (normed * gain_ref[...]).astype(bf16)
        pay_ref[:length, :] = rows
        logits = dot(rows, router_ref[...], ((1,), (1,)))
        real = lanes(logits.shape) < EXPERTS
        logits = jnp.where(real, logits, masked_score)
        raised = jnp.where(real, jnp.exp(logits - jnp.max(logits, -1, keepdims=True)), 0.0)
        router = raised * (1.0 / jnp.sum(raised, -1, keepdims=True))
        gate_ref[...] = router
        gates = jnp.where(named_experts(routes_ref[...]), router, 0.0).T[:EXTRA]
        high = gates.astype(bf16)
        pay_ref[length:, :length] = high
        pay_ref[length:, length : 2 * length] = (gates - high.astype(f32)).astype(bf16)
        pay_ref[length:, 2 * length :] = jnp.zeros((EXTRA, D - 2 * length), bf16)

    operands = (attended, hidden_own, gain, router_w, routes)
    return call(
        kernel,
        [array((length, D), f32), array((length, 128), f32), array((length + EXTRA, D), bf16)],
        [SCALARS] + [whole(v.shape) for v in operands] + [STAY] * count,
        (offsets, *operands, *pieces),
        scratch=[pltpu.VMEM((QW, D), bf16), pltpu.SemaphoreType.DMA((count,))],
    )


def write_chunks(out_refs, at, values):
    part = F // len(out_refs)
    for c, out_ref in enumerate(out_refs):
        out_ref[:, at * part : (at + 1) * part] = values[:, c * part : (c + 1) * part].astype(bf16)


def expert(rows, grads, w_gate_up, w_down, index, chunks):
    sources, blocks, tall = len(grads), len(rows), rows[0].shape[0]
    length = tall - EXTRA
    step = 2
    turns = grads[0].shape[0] // step
    steps = blocks // step

    def kernel(index_ref, *refs):
        row_refs, grad_refs, refs = refs[:blocks], refs[blocks : blocks + sources], refs[blocks + sources :]
        gate_up_ref, down_ref, dgu_ref, hid_ref, sum_ref = refs[:5]
        out_refs, (both_ref, grad_ref, table_ref, *accs) = refs[5 : 5 + chunks], refs[5 + chunks :]
        i = pl.program_id(0)
        for source, source_ref in enumerate(grad_refs):

            @pl.when((i >= source * turns) & (i < (source + 1) * turns))
            def _():
                for b in range(step):
                    grad_ref[b * length : (b + 1) * length, :] = source_ref[b]

        for j, row_ref in enumerate(row_refs):
            b = j % step

            @pl.when(i == j // step)
            def _():
                both_ref[b * length : (b + 1) * length, :] = row_ref[:length, :]
                high, low = row_ref[length:, :length], row_ref[length:, length : 2 * length]
                table_ref[b] = high.astype(f32) + low.astype(f32)

        both, grad = both_ref[...], grad_ref[...]
        columns = []
        for b in range(step):
            table = table_ref[b]
            mine = lax.broadcasted_iota(jnp.int32, table.shape, 0) == index_ref[1]
            row = jnp.sum(jnp.where(mine, table, 0.0), 0, keepdims=True)
            columns.append(jnp.broadcast_to(row, (128, length)).T[:, :1])
        gate = jnp.concatenate(columns, 0)
        gate_up = dot(both, gate_up_ref[0])
        gate_part, up_part = gate_up[:, :F], gate_up[:, F:]
        sigmoid_g = jax.nn.sigmoid(gate_part)
        silu_g = gate_part * sigmoid_g
        hidden = silu_g * up_part
        raw = dot(grad, down_ref[0])
        sums = jnp.sum(raw * hidden, 1, keepdims=True)
        gated = (gate * hidden).astype(bf16)
        grad_hidden = gate * raw
        grad_gate = (grad_hidden * up_part * sigmoid_g * (1.0 + gate_part * (1.0 - sigmoid_g))).astype(bf16)
        grad_up = (grad_hidden * silu_g).astype(bf16)
        for b in range(step):
            at = slice(b * length, (b + 1) * length)
            dgu_ref[b, :, :F] = grad_gate[at]
            dgu_ref[b, :, F:] = grad_up[at]
            hid_ref[b] = gated[at]
            sum_ref[b] = jnp.broadcast_to(sums[at], (length, 128)).T[:8]
        if not chunks:
            return
        for p, (left, right) in enumerate(((both, grad_gate), (both, grad_up), (grad, gated))):
            term, acc = dot(left, right, ((0,), (0,))), accs[p]

            @pl.when(i == 0)
            def _():
                acc[...] = term

            @pl.when((i > 0) & (i < steps - 1))
            def _():
                acc[...] += term

            @pl.when(i == steps - 1)
            def _():
                write_chunks(out_refs, p, acc[...] + term)

    def block(*shape):
        return pl.BlockSpec((step,) + shape, lambda i, index: (i,) + (0,) * len(shape))

    def source_block(source, *shape):
        def at(i, index):
            return (jnp.clip(i - source * turns, 0, turns - 1),) + (0,) * len(shape)

        return pl.BlockSpec((step,) + shape, at)

    def weight(*shape):
        return pl.BlockSpec((1,) + shape, lambda i, index: (index[0], 0, 0))

    shapes = [array((blocks, length, 2 * F), bf16), array((blocks, length, F), bf16), array((blocks, 8, length), f32)]
    scratch = [
        pltpu.VMEM((step * length, D), bf16),
        pltpu.VMEM((step * length, D), bf16),
        pltpu.VMEM((step, EXTRA, length), f32),
    ]
    return call(
        kernel,
        shapes + [array((D, 3 * F // chunks), bf16)] * chunks if chunks else shapes,
        [whole((tall, D))] * blocks
        + [source_block(s, length, D) for s in range(sources)]
        + [weight(D, 2 * F), weight(D, F)],
        (index, *rows, *grads, w_gate_up, w_down),
        out_specs=[block(length, 2 * F), block(length, F), block(8, length)]
        + [pl.BlockSpec((D, 3 * F // chunks), lambda i, index: (0, 0)) for _ in range(chunks)],
        scratch=scratch + ([pltpu.VMEM((D, F), f32)] * 3 if chunks else []),
        grid=(steps,),
        prefetch=1,
    )


def gate_column(table, expert):
    mine = lax.broadcasted_iota(jnp.int32, table.shape, 0) == expert
    row = jnp.sum(jnp.where(mine, table, 0.0), 0, keepdims=True)
    return jnp.broadcast_to(row, (128, table.shape[1])).T[:, :1]


def last_expert(rows, grads, w_gate_up, w_down, indices, earlier, sums):
    sources, blocks, tall = len(grads), len(rows), rows[0].shape[0]
    length = tall - EXTRA
    step = 2
    turns = grads[0].shape[0] // step
    steps = blocks // step
    others = len(earlier)

    def kernel(indices_ref, *refs):
        row_refs, grad_refs, refs = refs[:blocks], refs[blocks : blocks + sources], refs[blocks + sources :]
        gate_up_ref, down_ref, refs = refs[0], refs[1], refs[2:]
        earlier_refs, weight_refs, sum_refs, refs = refs[:others], refs[others : 2 * others], refs[2 * others : 3 * others], refs[3 * others :]
        dgu_ref, hid_ref, out_refs, (both_ref, grad_ref, table_ref) = refs[0], refs[1], refs[2 : 2 + sources], refs[2 + sources :]
        i = pl.program_id(0)
        for source, source_ref in enumerate(grad_refs):

            @pl.when((i >= source * turns) & (i < (source + 1) * turns))
            def _():
                for b in range(step):
                    grad_ref[b * length : (b + 1) * length, :] = source_ref[b]

        for j, row_ref in enumerate(row_refs):
            b = j % step

            @pl.when(i == j // step)
            def _():
                both_ref[b * length : (b + 1) * length, :] = row_ref[:length, :]
                high, low = row_ref[length:, :length], row_ref[length:, length : 2 * length]
                table_ref[b] = high.astype(f32) + low.astype(f32)

        both, grad = both_ref[...], grad_ref[...]
        gate = jnp.concatenate([gate_column(table_ref[b], indices_ref[2 * others + 1]) for b in range(step)], 0)
        gate_up = dot(both, gate_up_ref[0])
        gate_part, up_part = gate_up[:, :F], gate_up[:, F:]
        sigmoid_g = jax.nn.sigmoid(gate_part)
        silu_g = gate_part * sigmoid_g
        hidden = silu_g * up_part
        raw = dot(grad, down_ref[0])
        own = jnp.sum(raw * hidden, 1, keepdims=True)
        gated = (gate * hidden).astype(bf16)
        grad_hidden = gate * raw
        grad_gate = (grad_hidden * up_part * sigmoid_g * (1.0 + gate_part * (1.0 - sigmoid_g))).astype(bf16)
        grad_up = (grad_hidden * silu_g).astype(bf16)
        total = dot(jnp.concatenate([grad_gate, grad_up], 1), gate_up_ref[0], ((1,), (1,)))
        for part_ref, weight_ref in zip(earlier_refs, weight_refs):
            part = jnp.concatenate([part_ref[b] for b in range(step)], 0)
            total = total + dot(part, weight_ref[0], ((1,), (1,)))
        for b in range(step):
            at = slice(b * length, (b + 1) * length)
            dgu_ref[b, :, :F] = grad_gate[at]
            dgu_ref[b, :, F:] = grad_up[at]
            hid_ref[b] = gated[at]
            table = jnp.zeros((EXTRA, length), f32)
            place = lax.broadcasted_iota(jnp.int32, table.shape, 0)
            for e in range(others):
                table = jnp.where(place == indices_ref[2 * e + 1], sum_refs[e][b, :1, :], table)
            row = jnp.broadcast_to(own[at], (length, 128)).T[:1]
            table = jnp.where(place == indices_ref[2 * others + 1], row, table)
            high = table.astype(bf16)
            for source, out_ref in enumerate(out_refs):

                @pl.when((i >= source * turns) & (i < (source + 1) * turns))
                def _():
                    out_ref[b, :length, :] = total[at].astype(bf16)
                    out_ref[b, length:, :length] = high
                    out_ref[b, length:, length : 2 * length] = (table - high.astype(f32)).astype(bf16)
                    out_ref[b, length:, 2 * length :] = jnp.zeros((EXTRA, D - 2 * length), bf16)

    def block(*shape):
        return pl.BlockSpec((step,) + shape, lambda i, index: (i,) + (0,) * len(shape))

    def source_block(source, *shape):
        def at(i, index):
            return (jnp.clip(i - source * turns, 0, turns - 1),) + (0,) * len(shape)

        return pl.BlockSpec((step,) + shape, at)

    def weight(e, *shape):
        return pl.BlockSpec((1,) + shape, lambda i, index: (index[2 * e], 0, 0))

    return call(
        kernel,
        [array((blocks, length, 2 * F), bf16), array((blocks, length, F), bf16)]
        + [array((blocks // sources, tall, D), bf16)] * sources,
        [whole((tall, D))] * blocks
        + [source_block(s, length, D) for s in range(sources)]
        + [weight(others, D, 2 * F), weight(others, D, F)]
        + [block(length, 2 * F)] * others
        + [weight(e, D, 2 * F) for e in range(others)]
        + [block(8, length)] * others,
        (indices, *rows, *grads, w_gate_up, w_down, *earlier, *[w_gate_up] * others, *sums),
        out_specs=[block(length, 2 * F), block(length, F)] + [source_block(s, tall, D) for s in range(sources)],
        scratch=[
            pltpu.VMEM((step * length, D), bf16),
            pltpu.VMEM((step * length, D), bf16),
            pltpu.VMEM((step, EXTRA, length), f32),
        ],
        grid=(steps,),
        prefetch=1,
    )


def weight_grads(rows, grads, grad_gate_up, hidden, chunks, after):
    sources, blocks, tall = len(grads), len(rows), rows[0].shape[0]
    length = tall - EXTRA
    step = 2
    turns = grads[0].shape[0] // step
    steps = blocks // step

    def kernel(after_ref, *refs):
        row_refs, grad_refs, refs = refs[:blocks], refs[blocks : blocks + sources], refs[blocks + sources :]
        dgu_ref, hid_ref, out_refs = refs[0], refs[1], refs[2 : 2 + chunks]
        both_ref, grad_ref, *accs = refs[2 + chunks :]
        i = pl.program_id(0)
        for source, source_ref in enumerate(grad_refs):

            @pl.when((i >= source * turns) & (i < (source + 1) * turns))
            def _():
                for b in range(step):
                    grad_ref[b * length : (b + 1) * length, :] = source_ref[b]

        for j, row_ref in enumerate(row_refs):
            b = j % step

            @pl.when(i == j // step)
            def _():
                both_ref[b * length : (b + 1) * length, :] = row_ref[:length, :]

        both, grad = both_ref[...], grad_ref[...]
        grad_gate = jnp.concatenate([dgu_ref[b, :, :F] for b in range(step)], 0)
        grad_up = jnp.concatenate([dgu_ref[b, :, F:] for b in range(step)], 0)
        gated = jnp.concatenate([hid_ref[b] for b in range(step)], 0)
        for p, (left, right) in enumerate(((both, grad_gate), (both, grad_up), (grad, gated))):
            term, acc = dot(left, right, ((0,), (0,))), accs[p]

            @pl.when(i == 0)
            def _():
                acc[...] = term

            @pl.when((i > 0) & (i < steps - 1))
            def _():
                acc[...] += term

            @pl.when(i == steps - 1)
            def _():
                write_chunks(out_refs, p, acc[...] + term)

    def block(*shape):
        return pl.BlockSpec((step,) + shape, lambda i, after: (i,) + (0,) * len(shape))

    def source_block(source, *shape):
        def at(i, after):
            return (jnp.clip(i - source * turns, 0, turns - 1),) + (0,) * len(shape)

        return pl.BlockSpec((step,) + shape, at)

    return call(
        kernel,
        [array((D, 3 * F // chunks), bf16)] * chunks,
        [whole((tall, D))] * blocks
        + [source_block(s, length, D) for s in range(sources)]
        + [block(length, 2 * F), block(length, F)],
        (after, *rows, *grads, grad_gate_up, hidden),
        out_specs=[pl.BlockSpec((D, 3 * F // chunks), lambda i, after: (0, 0)) for _ in range(chunks)],
        scratch=[pltpu.VMEM((step * length, D), bf16)] * 2 + [pltpu.VMEM((D, F), f32)] * 3,
        grid=(steps,),
        prefetch=1,
    )


def row_terms(parts, weights, indices, sources):
    blocks, length, width = parts[0].shape
    count = len(parts)
    step = 2
    turns = blocks // step // sources

    def kernel(indices_ref, *refs):
        part_refs, weight_refs, out_refs = refs[:count], refs[count : 2 * count], refs[2 * count :]
        i = pl.program_id(0)
        total = None
        for part_ref, weight_ref in zip(part_refs, weight_refs):
            term = dot(jnp.concatenate([part_ref[b] for b in range(step)], 0), weight_ref[0], ((1,), (1,)))
            total = term if total is None else total + term
        for source, out_ref in enumerate(out_refs):

            @pl.when((i >= source * turns) & (i < (source + 1) * turns))
            def _():
                for b in range(step):
                    out_ref[b] = total[b * length : (b + 1) * length].astype(bf16)

    def weight(e):
        return pl.BlockSpec((1,) + weights.shape[1:], lambda i, index: (index[2 * e], 0, 0))

    def source_block(source):
        return pl.BlockSpec((step, length, D), lambda i, index: (jnp.clip(i - source * turns, 0, turns - 1), 0, 0))

    return call(
        kernel,
        [array((blocks // sources, length, D), bf16)] * sources,
        [pl.BlockSpec((step, length, width), lambda i, index: (i, 0, 0))] * count + [weight(e) for e in range(count)],
        (indices, *parts, *[weights] * count),
        out_specs=[source_block(s) for s in range(sources)],
        grid=(blocks // step,),
        prefetch=1,
    )


def backward(
    returned, residual, router, routes, cotangent, gain, router_w, query, kv, lse, cosines, sines, inputs,
    hidden_prev, hidden_own, attended, out_pieces, out_offsets, qkv_pieces, qkv_offsets, flag, core, shards, cores,
):
    length, terms = residual.shape[0], len(returned)
    width = QW + 2 * KVW
    out_count, qkv_count = len(out_pieces), len(qkv_pieces)

    deep = D // (shards * cores)

    def kernel(out_offsets_ref, qkv_offsets_ref, flag_ref, core_ref, *rest):
        term_refs, rest = rest[:terms], rest[terms:]
        res_ref, gate_ref, routes_ref, cot_ref, gain_ref, router_ref, q_ref, kv_ref, lse_ref, cos_ref, sin_ref = rest[:11]
        in_ref, prev_ref, own_ref, att_ref, rest = *rest[11:15], rest[15:]
        out_refs, qkv_refs, rest = rest[:out_count], rest[out_count : out_count + qkv_count], rest[out_count + qkv_count :]
        gres_ref, gown_ref, gprev_ref, own_grad_ref = rest[:4]
        far_refs, rest = rest[4 : 4 + 3 * (cores - 1)], rest[4 + 3 * (cores - 1) :]
        w_out, w_qkv, gatt_ref, dq_ref, dkv_ref, small_ref, out_sems, qkv_sems = rest
        out_copies = load_rows(out_refs, out_offsets_ref, w_out, out_sems)
        qkv_copies = load_rows(qkv_refs, qkv_offsets_ref, w_qkv, qkv_sems)
        total = term_refs[0][...].astype(f32)
        for ref in term_refs[1:]:
            total = total + ref[...].astype(f32)
        table = total[length:, :length] + total[length:, length : 2 * length]
        gate_grads = jnp.concatenate([table, jnp.zeros((128 - EXTRA, length), f32)], 0).T
        grad_router = jnp.where(named_experts(routes_ref[...]), gate_grads, 0.0)
        router = gate_ref[...]
        grad_logits = (router * (grad_router - jnp.sum(router * grad_router, -1, keepdims=True))).astype(bf16)
        grad_input = total[:length] + dot(grad_logits, router_ref[...])
        normed, inverse = normalize(res_ref[...])
        gain_row = gain_ref[...]
        rows = (normed * gain_row).astype(bf16)
        small = dot(rows, grad_logits, ((0,), (0,)))
        gain_grad = jnp.sum(grad_input * normed, 0, keepdims=True)
        small_ref[...] = jnp.where(lanes((D, 128)) == EXPERTS, jnp.broadcast_to(gain_grad, (128, D)).T, small)
        grad_residual = cot_ref[...].astype(f32) + norm_back(normed, inverse, grad_input * gain_row)
        gres_ref[...] = grad_residual
        grad_attn = grad_residual.astype(bf16)
        for copy in out_copies:
            copy.wait()
        gatt_ref[...] = dot(grad_attn, w_out[...], ((1,), (1,))).astype(bf16)

        def write(at, values):
            group = min(at // D, 2)
            start = at - group * D
            for p in range(shards * cores):
                rows_of = values[p * deep : (p + 1) * deep]
                for j in range(cores):

                    @pl.when((core_ref[0] + j) % cores == p % cores)
                    def _():
                        if j == 0:
                            own_grad_ref[p // cores, :, at : at + values.shape[1]] = rows_of.astype(bf16)
                        else:
                            ref = far_refs[3 * (j - 1) + group]
                            ref[p // cores, :, start : start + values.shape[1]] = rows_of.astype(bf16)

        write(width, dot(att_ref[...], grad_attn, ((0,), (0,))))

        bias = jnp.where((lanes((1, 2 * length)) >= length) | (flag_ref[0] > 0), 0.0, masked_score)
        cos_own, sin_own = cos_ref[length:, :], sin_ref[length:, :]

        def back(values, cos, sin):
            return (values * cos - halves(values) * sin).astype(bf16)

        def pair_of_keys(jj, carry):
            at = pl.multiple_of(jj * PAIR, PAIR)
            keys = kv_ref[:, pl.ds(at, PAIR)].astype(f32)
            vals = kv_ref[:, pl.ds(KVW + at, PAIR)].astype(f32)
            key_grads, val_grads = [], []
            for t in range(2):
                place = pl.multiple_of((2 * jj + t) * PAIR, PAIR)
                both = two_rows(q_ref[:, pl.ds(place, PAIR)].astype(f32)).astype(bf16)
                outs = two_rows(gatt_ref[:, pl.ds(place, PAIR)].astype(f32)).astype(bf16)
                key = doubled(keys, t).astype(bf16)
                val = doubled(vals, t).astype(bf16)
                own = lanes(lse_ref.shape) == 2 * jj + t
                log_total = jnp.sum(jnp.where(own, lse_ref[...], 0.0), -1, keepdims=True)
                scores = dot(both, key, ((1,), (1,))) * score_scale + bias
                probs = jnp.exp(scores - log_total)
                grad_probs = dot(outs, val, ((1,), (1,)))
                inner = jnp.sum(probs * grad_probs, -1, keepdims=True)
                grad_scores = (probs * (grad_probs - inner)).astype(bf16)
                grad_query = dot(grad_scores, key) * score_scale
                low = lanes((length, PAIR)) < HEAD_DIM
                grad_query = jnp.where(low, grad_query[:length], grad_query[length:])
                dq_ref[:, pl.ds(place, PAIR)] = back(grad_query, cos_own, sin_own)
                key_grad = dot(grad_scores, both, ((0,), (0,))) * score_scale
                val_grad = dot(probs.astype(bf16), outs, ((0,), (0,)))
                key_grads.append(key_grad + pltpu.roll(key_grad, HEAD_DIM, 1))
                val_grads.append(val_grad + pltpu.roll(val_grad, HEAD_DIM, 1))
            low = lanes((2 * length, PAIR)) < HEAD_DIM
            dkv_ref[:, pl.ds(at, PAIR)] = back(jnp.where(low, *key_grads), cos_ref[...], sin_ref[...])
            dkv_ref[:, pl.ds(KVW + at, PAIR)] = jnp.where(low, *val_grads).astype(bf16)
            return carry

        lax.fori_loop(0, KVW // PAIR, pair_of_keys, 0)
        write(0, dot(in_ref[length:, :], dq_ref[...], ((0,), (0,))))
        write(QW, dot(in_ref[...], dkv_ref[...], ((0,), (0,))))
        for copy in qkv_copies:
            copy.wait()
        from_kv = dot(dkv_ref[...], w_qkv[:, QW:], ((1,), (1,)))
        own = from_kv[length:] + dot(dq_ref[...], w_qkv[:, :QW], ((1,), (1,)))
        gown_ref[...] = own
        gprev_ref[...] = from_kv[:length].astype(bf16)
        normed_own, _ = normalize(own_ref[...].astype(f32))
        normed_prev, _ = normalize(prev_ref[...].astype(f32))
        gain_grad = jnp.sum(own * normed_own + from_kv[:length] * normed_prev, 0, keepdims=True)
        column = jnp.broadcast_to(gain_grad, (128, D)).T
        write(width + D, jnp.where(lanes((D, 128)) == EXPERTS + 1, column, small_ref[...]))

    operands = (
        *returned, residual, router, routes, cotangent, gain, router_w, query, kv, lse, cosines, sines, inputs,
        hidden_prev, hidden_own, attended,
    )
    return call(
        kernel,
        [
            array((length, D), f32),
            array((length, D), f32),
            array((length, D), bf16),
        ]
        + [array((shards, deep, width + D + 128), bf16)]
        + [array((shards, deep, w), bf16) for w in (D, D, D + 128)] * (cores - 1),
        [SCALARS] * 4 + [whole(v.shape) for v in operands] + [STAY] * (out_count + qkv_count),
        (out_offsets, qkv_offsets, flag, core, *operands, *out_pieces, *qkv_pieces),
        scratch=[
            pltpu.VMEM((QW, D), bf16),
            pltpu.VMEM((D, width), bf16),
            pltpu.VMEM((length, QW), bf16),
            pltpu.VMEM((length, QW), bf16),
            pltpu.VMEM((2 * length, 2 * KVW), bf16),
            pltpu.VMEM((D, 128), f32),
            pltpu.SemaphoreType.DMA((out_count,)),
            pltpu.SemaphoreType.DMA((qkv_count,)),
        ],
    )


def first_back(grad_sum, grad_residual, hidden_own, gain):
    def kernel(sum_ref, res_ref, hid_ref, gain_ref, out_ref):
        normed, inverse = normalize(hid_ref[...].astype(f32))
        grad = sum_ref[...] * gain_ref[...]
        out_ref[...] = res_ref[...] + norm_back(normed, inverse, grad)

    operands = (grad_sum, grad_residual, hidden_own, gain)
    return call(kernel, [array(grad_sum.shape, f32)], [whole(v.shape) for v in operands], operands)[0]


def place(sources, experts, outs, shapes, chunk, chunks):
    part = F // chunks
    count = sum(source.shape[0] for source in sources)

    def kernel(experts_ref, *refs):
        source_refs = refs[: len(sources)]
        gate_up_ref, down_ref, wide, sems = refs[len(sources) + len(outs) :]
        copies = []
        values = [ref.at[i] for ref in source_refs for i in range(ref.shape[0])]
        for i, source in enumerate(values):
            wide[i] = source[...].astype(f32)
            for p, target in enumerate(
                (
                    gate_up_ref.at[experts_ref[i], :, chunk * part : (chunk + 1) * part],
                    gate_up_ref.at[experts_ref[i], :, F + chunk * part : F + (chunk + 1) * part],
                    down_ref.at[experts_ref[i], :, chunk * part : (chunk + 1) * part],
                )
            ):
                copy = pltpu.make_async_copy(wide.at[i, :, p * part : (p + 1) * part], target, sems.at[i, p])
                copy.start()
                copies.append(copy)
        for copy in copies:
            copy.wait()

    return call(
        kernel,
        shapes,
        [SCALARS] + [whole(v.shape) for v in sources] + [STAY] * len(outs),
        (experts, *sources, *outs),
        out_specs=[STAY, STAY],
        scratch=[pltpu.VMEM((count, D, 3 * part), f32), pltpu.SemaphoreType.DMA((count, 3))],
        aliases={1 + len(sources) + i: i for i in range(len(outs))},
    )


def unpack(sources, offsets, rows):
    count = sum(source.shape[0] for source in sources)
    deep, wide = sources[0].shape[1:]
    widths = (QW + 2 * KVW, D)

    def kernel(offsets_ref, *refs):
        source_refs, refs = refs[: len(sources)], refs[len(sources) :]
        out_refs, router_ref, ffn_ref, attn_ref, values_ref, rest_ref, sems = refs[:2], *refs[2:]
        copies = []
        for i, source in enumerate([ref.at[i] for ref in source_refs for i in range(ref.shape[0])]):
            values_ref[i] = source[...].astype(f32)
            at = pl.multiple_of(offsets_ref[i], 8)
            start = 0
            for p, (out_ref, width) in enumerate(zip(out_refs, widths)):
                copy = pltpu.make_async_copy(values_ref.at[i, :, start : start + width], out_ref.at[pl.ds(at, deep), :], sems.at[i, p])
                copy.start()
                copies.append(copy)
                start += width
            rest_ref[pl.ds(at, deep), :] = values_ref[i, :, start:]
        router_ref[...] = rest_ref[:, :EXPERTS]
        turned = rest_ref[...].T
        ffn_ref[...] = turned[EXPERTS : EXPERTS + 1]
        attn_ref[...] = turned[EXPERTS + 1 : EXPERTS + 2]
        for copy in copies:
            copy.wait()

    return call(
        kernel,
        [array((rows, width), f32) for width in widths] + [array((rows, EXPERTS), f32)] + [array((1, rows), f32)] * 2,
        [SCALARS] + [whole(v.shape) for v in sources],
        (offsets, *sources),
        out_specs=[STAY] * 2 + [whole((rows, EXPERTS))] + [whole((1, rows))] * 2,
        scratch=[
            pltpu.VMEM((count, deep, wide), f32),
            pltpu.VMEM((rows, wide - sum(widths)), f32),
            pltpu.SemaphoreType.DMA((count, 2)),
        ],
    )


def post(function, flags, arrays, outs):
    parts = 4

    def cut(shape):
        return shape[:-2] + (shape[-2] // parts, shape[-1])

    def kernel(flags_ref, *refs):
        values = function([flags_ref[i] for i in range(flags.shape[0])], *[ref[...] for ref in refs[: len(arrays)]])
        for ref, value in zip(refs[len(arrays) :], values):
            if isinstance(value, tuple):
                for i, v in enumerate(value):
                    ref[i] = v.astype(ref.dtype)
            else:
                ref[...] = value.astype(ref.dtype)

    def spec(shape):
        return pl.BlockSpec(cut(shape), lambda i: (0,) * (len(shape) - 2) + (i, 0))

    return call(
        kernel,
        outs,
        [SCALARS] + [spec(v.shape) for v in arrays],
        (flags, *arrays),
        out_specs=[spec(v.shape) for v in outs],
        grid=(parts,),
    )


def tie(values, after):
    return lax.optimization_barrier((values, after))[0]


def doubling_sum(value, axis):
    count, step = lax.axis_size(axis), 1
    if count & (count - 1):
        return lax.psum(value, axis)
    while step < count:
        value = value + lax.ppermute(value, axis, [(i, i ^ step) for i in range(count)])
        step *= 2
    return value


def body(
    hidden_in, routes, w_qkv, w_out, w_router, attn_gain, ffn_gain, w_gate_up, w_down, cotangent
):
    line, shards = lax.axis_size("line"), lax.axis_size("fsdp")
    side, cores = lax.axis_size("side"), lax.axis_size("core")
    shard, side_at, core_at = lax.axis_index("fsdp"), lax.axis_index("side"), lax.axis_index("core")
    length = hidden_in.shape[0]
    near = [(a, s) for s in range(shards) for a in range(side)]
    local_experts = w_gate_up.shape[0]
    count = local_experts // (side * cores)
    barrier = lax.optimization_barrier

    def other_core(value, core=1):
        return turn(value, "core", (core,), (cores,))

    def other_side(value, step=1):
        return turn(value, "side", (step,), (side,))

    def from_shard(part, step):
        return turn(part, "fsdp", (step,), (shards,))

    def fetch_start(piece, sides):
        part = own_part(piece, 0, core_at * sides + side_at % sides, cores * sides)
        return [from_shard(part, step) for step in range(1, shards)]

    def fetch_end(piece, first, sides):
        rows = piece.shape[0]
        out, offsets = [piece], [shard * rows]
        for step, part in enumerate(first, 1):
            base = (shard - step) % shards * rows
            for a in range(sides):
                theirs = other_side(part, a) if a else part
                for core in range(cores):
                    out.append(other_core(theirs, core) if core else theirs)
                    at = (core_at - core) % cores * sides + (side_at - a) % sides
                    offsets.append(base + at * part.shape[0])
        return out, jnp.stack(offsets).astype(jnp.int32)

    def over_cores(first):
        return [other_core(first, core) if core else first for core in range(cores)]

    def far_blocks(blocks):
        return [other_core(blocks[core * len(near) : (core + 1) * len(near)], -core % cores) for core in range(1, cores)]

    def add_up(first, others):
        for other in others:
            first = first + other
        return first

    def send_back(total):
        out = [total[0]]
        for i, (a, s) in enumerate(near):
            if (a, s) != (0, 0):
                out.append(turn(total[i], ("side", "fsdp"), (-a % side, -s % shards), (side, shards)))
        return out

    parity = shard % 2
    flag = parity.astype(jnp.int32)[None]
    later = [(i, i + 1) for i in range(0, shards, 2)]
    before = [(i + 1, i) for i in range(0, shards, 2)]

    small_rows = w_router.shape[0]
    small = jnp.concatenate([w_router.T, attn_gain[None], ffn_gain[None]], 0)
    qkv_first = fetch_start(w_qkv, side)
    hidden_prev = lax.ppermute(hidden_in, "fsdp", later)
    full_small = jnp.zeros((EXPERTS + 2, D), bf16)
    for step in range(shards):
        theirs = from_shard(small, step) if step else small
        full_small = lax.dynamic_update_slice_in_dim(full_small, theirs, (shard - step) % shards * small_rows, 1)
    gain_attn = full_small[EXPERTS : EXPERTS + 1].astype(f32)
    gain_ffn = full_small[EXPERTS + 1 :].astype(f32)
    router_w = jnp.pad(full_small[:EXPERTS], ((0, 128 - EXPERTS), (0, 0)))
    sideways = [other_side(cotangent, a) for a in range(1, side)]
    across = [from_shard(cotangent, s) for s in range(1, shards)]
    rows_at = jnp.arange(length, dtype=jnp.int32)
    cosines, sines = rotary_tables(jnp.concatenate([rows_at, parity * length + rows_at]))
    qkv_pieces, qkv_offsets = fetch_end(w_qkv, qkv_first, side)
    out_first = fetch_start(tie(w_out, (hidden_prev, qkv_first)), 1)

    across, hidden_prev = barrier((across, hidden_prev))
    corners = [[other_side(v, a) for a in range(1, side)] for v in across]
    queries, kv, inputs = project(hidden_prev, hidden_in, gain_attn, cosines, sines, qkv_pieces, qkv_offsets)
    out_first, queries, kv = barrier((out_first, queries, kv))
    out_pieces, out_offsets = fetch_end(w_out, out_first, 1)
    attended, lse = attend(queries, kv, flag)
    grads_near = [cotangent] + sideways + [v for first, rest in zip(across, corners) for v in [first] + rest]
    grads_near = jnp.stack(tie(grads_near, attended))
    out_pieces, attended, grads_near = barrier((out_pieces, attended, grads_near))
    grads_near = over_cores(grads_near)
    residual, router, payload = enter_experts(attended, hidden_in, gain_ffn, router_w, routes, out_pieces, out_offsets)
    rows_near = [turn(payload, ("side", "fsdp"), (a, s), (side, shards)) if (a, s) != (0, 0) else payload for a, s in near]
    rows_near = rows_near + [other_core(v, core) for core in range(1, cores) for v in rows_near]

    clock = []

    def run(function, *inputs):
        if clock:
            inputs = barrier((inputs, tuple(clock)))[0]
        out = function(*inputs)
        clock[:] = jax.tree.leaves(out)
        return out

    mine_at = (side_at * cores + core_at) * count
    indices = [jnp.stack([mine_at + e, shard * local_experts + mine_at + e]).astype(jnp.int32) for e in range(count)]
    both = jnp.concatenate(indices)
    order = jnp.stack([((side_at - a) % side * cores + (core_at - core) % cores) for core in range(cores) for a in range(side)])
    order = order.astype(jnp.int32) * count
    shapes = [array((local_experts, D, 2 * F), f32), array((local_experts, D, F), f32)]
    place_at = lax.axis_index("line")
    end = (place_at == 0) | (place_at == line - 1)

    def go_in(raw):
        return lax.ppermute(raw, "line", [(0, 1), (3, 2)])

    def cross(half):
        return lax.ppermute(half, "line", [(1, 2), (2, 1)])

    def in_and_out(sent):
        return lax.ppermute(sent, "line", [(0, 1), (1, 0), (2, 3), (3, 2)])

    def go_out(total):
        return lax.ppermute(total, "line", [(1, 0), (2, 3)])

    def chosen(got, kept):
        return jnp.where(end, got, kept)

    def sides(full):
        return [other_side(full, a) for a in range(1, side)]

    def core_swaps(pair):
        return [other_core(pair, core) for core in range(1, cores)]

    def stacked(full, others):
        return jnp.stack([full] + others)

    def plus(first, second):
        return first + second

    def split(blocks):
        return [blocks[core * len(near) : (core + 1) * len(near)] for core in range(cores)]

    def near_sums(first, others):
        total = add_up(first, others)
        return [total[i] for i in range(len(near))]

    def placed(pair, swaps, outs, e, c):
        return place([pair] + swaps, order + e, outs, shapes, c, CHUNKS)

    def back(terms):
        return backward(
            terms, residual, router, routes, cotangent, gain_ffn, router_w, queries, kv, lse, cosines, sines, inputs, hidden_prev,
            hidden_in, attended, out_pieces, out_offsets, qkv_pieces, qkv_offsets, flag, core_at.astype(jnp.int32)[None], shards, cores,
        )

    def by_shard(total):
        return total[0] if shards == 1 else own_part(total, 0, shard, shards)[0], [
            own_part(total, 0, (shard + step) % shards, shards)[0] for step in range(1, shards)
        ]

    def by_side(total):
        return own_part(total, 0, side_at, side), [own_part(total, 0, (side_at + a) % side, side) for a in range(1, side)]

    def by_step(total):
        return [total[s * side : (s + 1) * side] for s in range(shards)]

    def by_near(total):
        return total[0], [total[a] for a in range(1, side)]

    def swap_lines(value, step):
        return lax.ppermute(value, "line", [(i, i ^ step) for i in range(line)])

    flags = jnp.stack([end, shard > 0, side_at > 0]).astype(jnp.int32)

    def f(value):
        return value.astype(f32)

    def pick(flag, got, kept):
        return jnp.where(flag > 0, f(got), f(kept))

    def steps(function, outs, *arrays):
        outs = [v if isinstance(v, jax.ShapeDtypeStruct) else array(v, bf16) for v in outs]
        return run(lambda *v: tuple(post(function, flags, v, outs)), *arrays)

    if (line, side, cores, shards, count) != (4, 2, 2, 2, 2):
        grads_gu, hiddens, sums, chunks = [], [], [], []
        for e in range(count - 1):
            grad_gu, hidden, total, *parts = expert(rows_near, grads_near, w_gate_up, w_down, indices[e], CHUNKS)
            grads_gu.append(grad_gu)
            hiddens.append(hidden)
            sums.append(total)
            chunks.append(parts)
        grad_gu, hidden, *blocks = last_expert(rows_near, grads_near, w_gate_up, w_down, both, grads_gu, sums)
        hiddens.append(hidden)
        chunks.append(weight_grads(rows_near, grads_near, grad_gu, hidden, CHUNKS, both))
        terms = row_terms(hiddens, w_down, both, cores)
        returned = send_back([v for v in add_up(blocks[0], [other_core(g, -c % cores) for c, g in enumerate(blocks[1:], 1)])])
        mixed = send_back([v for v in add_up(terms[0], [other_core(g, -c % cores) for c, g in enumerate(terms[1:], 1)])])
        grad_residual, grad_own, grad_prev, own_w, *other_w = back(returned)
        joined = [jnp.concatenate(other_w[i : i + 3], -1) for i in range(0, len(other_w), 3)]
        own_w = add_up(own_w, [other_core(w, core) for core, w in enumerate(joined, 1)])
        own_w, other_w = by_shard(own_w)
        own_w = add_up(own_w, [from_shard(w, step) for step, w in enumerate(other_w, 1)])
        own_w = add_up(own_w, [other_side(own_w, a) for a in range(1, side)])

        def line_sum(value):
            if line & (line - 1):
                return lax.psum(value, "line")
            for bit in range(line.bit_length() - 1):
                value = value + swap_lines(value, 1 << bit)
            return value

        sum_w, outs = line_sum(own_w), ()
        for e, parts in enumerate(chunks):
            for c, part in enumerate(parts):
                full = line_sum(part)
                pair = jnp.stack([full] + sides(full))
                outs = placed(pair, core_swaps(pair), outs, e, c)
        at_w = jnp.stack([(core_at - core) % cores for core in range(cores)]).astype(jnp.int32) * sum_w.shape[0]
        qkv_sum, out_sum, router_sum, ffn_sum, attn_sum = unpack(
            [w[None] for w in [sum_w] + core_swaps(sum_w)], at_w, sum_w.shape[0] * cores
        )
        grad_sum = grad_own + lax.ppermute(grad_prev, "fsdp", before).astype(f32)
        grad_in = first_back(grad_sum, grad_residual, hidden_in, gain_attn)
        layer_out = add_up(residual, [m.astype(f32) for m in mixed]).astype(bf16)
        return (
            layer_out, grad_in, qkv_sum, out_sum, router_sum, attn_sum[0], ffn_sum[0], outs[0], outs[1],
        )

    gu_0, hid_0, sum_0, *parts_0 = run(lambda i: expert(rows_near, grads_near, w_gate_up, w_down, i, CHUNKS), indices[0])
    chunk = parts_0[0].shape
    two = (2,) + chunk
    in_0 = go_in(parts_0[0])
    gu_1, hid_1, first_half, other_half = run(
        lambda i: last_expert(rows_near, grads_near, w_gate_up, w_down, i, [gu_0], [sum_0]), both
    )
    far = [other_core(other_half)]
    (half_0,) = steps(lambda flag, raw, got: (f(raw) + f(got),), [chunk], parts_0[0], in_0)
    middle_0, in_1 = cross(half_0), go_in(parts_0[1])
    mixed, mixed_other = run(lambda i: row_terms([hid_0, hid_1], w_down, i, cores), both)
    blocks = run(near_sums, first_half, far)
    returned = send_back(blocks)
    parts_1 = run(lambda i: weight_grads(rows_near, grads_near, gu_1, hid_1, CHUNKS, i), both)

    def step_1(flag, half, middle, own, got, raw):
        total = f(half) + f(middle)
        return total, f(own) + f(got), pick(flag[0], raw, total)

    total_0, half_1, sent_2 = steps(step_1, [chunk] * 3, half_0, middle_0, parts_0[1], in_1, parts_1[0])
    both_2, middle_1 = in_and_out(sent_2), cross(half_1)
    grad_residual, grad_own, grad_prev, own_w, *other_w = run(back, returned)
    far_w = [other_core(w) for w in other_w]
    deep, wide = own_w.shape[1:]

    def step_2(flag, own, got, total, half, middle, raw, w, *far):
        summed = f(half) + f(middle)
        joined = f(w) + jnp.concatenate([f(v) for v in far], -1)
        mine, theirs = pick(flag[1], joined[1], joined[0]), pick(flag[1], joined[0], joined[1])
        return f(own) + f(got), pick(flag[0], got, total), summed, pick(flag[0], raw, summed), mine, theirs

    half_2, full_0, total_1, sent_3, own_w, other_w = steps(
        step_2, [chunk] * 4 + [(deep, wide)] * 2,
        parts_1[0], both_2, total_0, half_1, middle_1, parts_1[1], own_w, *far_w,
    )
    side_0, middle_2, both_3 = other_side(full_0), cross(half_2), in_and_out(sent_3)
    far_w, far_m = from_shard(other_w, 1), other_core(mixed_other)

    def step_3(flag, own, got, total, half, middle, first, other, w, far, m, m_far):
        terms = f(m) + f(m_far)
        return (
            f(own) + f(got), pick(flag[0], got, total), f(half) + f(middle), (first, other), f(w) + f(far), terms[:2], terms[2:],
        )

    rows_of = mixed.shape[1]
    half_3, full_1, total_2, pair_0, own_w, own_m, other_m = steps(
        step_3, [chunk] * 3 + [two, (deep, wide)] + [(2, rows_of, D)] * 2,
        parts_1[1], both_3, total_1, half_2, middle_2, full_0, side_0, own_w, far_w, mixed, far_m,
    )
    side_1, middle_3, out_2, core_0 = other_side(full_1), cross(half_3), go_out(total_2), other_core(pair_0)
    in_w = go_in(own_w)

    def step_4(flag, got, total, half, middle, first, other, w, far):
        return pick(flag[0], got, total), f(half) + f(middle), (first, other), f(w) + f(far)

    full_2, total_3, pair_1, half_w = steps(
        step_4, [chunk] * 2 + [two, (deep, wide)], out_2, total_2, half_3, middle_3, full_1, side_1, own_w, in_w
    )
    side_2, out_3, middle_w, core_1 = other_side(full_2), go_out(total_3), cross(half_w), other_core(pair_1)
    far_m = from_shard(other_m, 1)
    outs = run(lambda pair, swap: placed(pair, [swap], (), 0, 0), pair_0, core_0)

    def step_5(flag, got, total, first, other, w, far, m, m_far):
        terms = f(m) + f(m_far)
        return pick(flag[0], got, total), (first, other), f(w) + f(far), terms[0], terms[1]

    full_3, pair_2, total_w, own_m, other_m = steps(
        step_5, [chunk, two, (deep, wide)] + [(rows_of, D)] * 2, out_3, total_3, full_2, side_2, half_w, middle_w, own_m, far_m
    )
    side_3, out_w, core_2 = other_side(full_3), go_out(total_w), other_core(pair_2)
    far_m = other_side(other_m)
    grad_later = lax.ppermute(grad_prev, "fsdp", before)
    outs = run(lambda pair, swap, outs: placed(pair, [swap], outs, 0, 1), pair_1, core_1, outs)

    def step_6(flag, first, other, got, w, rest, m, m_far, own, back):
        return (first, other), pick(flag[0], got, w), rest + f(m) + f(m_far), own + f(back)

    pair_3, full_w, layer_out, grad_sum = steps(
        step_6, [two, (deep, wide), (rows_of, D), array((rows_of, D), f32)],
        full_3, side_3, out_w, total_w, residual, own_m, far_m, grad_own, grad_later,
    )
    core_3, side_w = other_core(pair_3), other_side(full_w)
    grad_in = run(lambda grad: first_back(grad, grad_residual, hidden_in, gain_attn), grad_sum)
    outs = run(lambda pair, swap, outs: placed(pair, [swap], outs, 1, 0), pair_2, core_2, outs)
    outs = run(lambda pair, swap, outs: placed(pair, [swap], outs, 1, 1), pair_3, core_3, outs)
    (sum_w,) = steps(lambda flag, w, far: (f(w) + f(far),), [(deep, wide)], full_w, side_w)
    core_w = other_core(sum_w)
    at_w = jnp.stack([(core_at - core) % cores for core in range(cores)]).astype(jnp.int32) * deep
    qkv_sum, out_sum, router_sum, ffn_sum, attn_sum = run(lambda *v: unpack([w[None] for w in v], at_w, deep * cores), sum_w, core_w)
    return (
        layer_out,
        grad_in,
        qkv_sum,
        out_sum,
        router_sum,
        attn_sum[0],
        ffn_sum[0],
        outs[0],
        outs[1],
    )


def solution(mesh):
    copies, shards = mesh.shape["rep"], mesh.shape["fsdp"]
    local = EXPERTS // shards
    cores = 2 if copies % 2 == 0 and local % 2 == 0 else 1
    side = 2 if cores == 2 and copies % 4 == 0 and local % 4 == 0 else 1
    names = ("line", "side", "core", "fsdp")
    parts = Mesh(mesh.devices.reshape(copies // (side * cores), side, cores, shards), names)
    rows, shard = P(names, None), P("fsdp", None)
    experts = P("fsdp", None, None)
    in_specs = (rows, rows, shard, shard, shard, P("fsdp"), P("fsdp"), experts, experts, rows)
    out_specs = (rows, rows, shard, shard, shard, P("fsdp"), P("fsdp"), experts, experts)
    return jax.shard_map(body, mesh=parts, in_specs=in_specs, out_specs=out_specs, check_vma=False)
```

```python
import math
from functools import partial

import jax
import jax.numpy as jnp
from jax import lax
from jax.experimental import pallas as pl
from jax.experimental.pallas import tpu as pltpu
from jax.sharding import Mesh, PartitionSpec as P

D = 1024
HEADS = 16
KV_HEADS = 8
HEAD_DIM = 64
F = 512
TOP = 8
EXPERTS = 16
BLOCK = 256
QW = HEADS * HEAD_DIM
KVW = KV_HEADS * HEAD_DIM
EXTRA = 16
CHUNKS = 2
PAIR = 2 * HEAD_DIM

norm_eps = 1e-06
masked_score = -1e30
score_scale = HEAD_DIM ** (-0.5)
bf16, f32 = jnp.bfloat16, jnp.float32
VMEM = 56 * 1024 * 1024
POST_VMEM = 18 * 1024 * 1024


def dot(left, right, dims=((1,), (0,))):
    return lax.dot_general(left, right, (dims, ((), ())), preferred_element_type=f32)


def turn(value, axes, steps, sizes):
    pairs = []
    for source in range(math.prod(sizes)):
        place, rest = [], source
        for size in reversed(sizes):
            place.append(rest % size)
            rest //= size
        place.reverse()
        target = 0
        for at, size, step in zip(place, sizes, steps):
            target = target * size + (at + step) % size
        pairs.append((source, target))
    return lax.ppermute(value, axes, pairs)


def own_part(value, axis, index, parts):
    size = value.shape[axis] // parts
    return lax.dynamic_slice_in_dim(value, index * size, size, axis)


def whole(shape):
    return pl.BlockSpec(shape, lambda *_: (0,) * len(shape))


SCALARS = pl.BlockSpec(memory_space=pltpu.SMEM)
STAY = pl.BlockSpec(memory_space=pl.ANY)


def call(kernel, out_shape, in_specs, operands, out_specs=None, scratch=(), grid=None, prefetch=0, aliases=None, vmem=VMEM):
    out_specs = [whole(s.shape) for s in out_shape] if out_specs is None else out_specs
    spec = pltpu.PrefetchScalarGridSpec(
        num_scalar_prefetch=prefetch,
        grid=grid or (1,),
        in_specs=in_specs,
        out_specs=out_specs,
        scratch_shapes=list(scratch),
    )
    return pl.pallas_call(
        kernel,
        out_shape=list(out_shape),
        grid_spec=spec,
        input_output_aliases=aliases or {},
        compiler_params=pltpu.CompilerParams(vmem_limit_bytes=vmem),
        cost_estimate=pl.CostEstimate(flops=0, transcendentals=0, bytes_accessed=0),
    )(*operands)


def array(shape, dtype):
    return jax.ShapeDtypeStruct(shape, dtype)


def normalize(rows):
    scale_inv = lax.rsqrt(jnp.mean(rows * rows, -1, keepdims=True) + norm_eps)
    return (rows * scale_inv, scale_inv)


def norm_back(normed, scale_inv, grad_normed):
    return scale_inv * (grad_normed - normed * jnp.mean(grad_normed * normed, -1, keepdims=True))


def lanes(shape):
    return lax.broadcasted_iota(jnp.int32, shape, len(shape) - 1)


def halves(values):
    low = lanes(values.shape) % HEAD_DIM < HEAD_DIM // 2
    half = HEAD_DIM // 2
    return jnp.where(low, pltpu.roll(values, PAIR - half, 1), pltpu.roll(values, half, 1))


def rotary_tables(places):
    at = jnp.arange(PAIR, dtype=jnp.int32) % HEAD_DIM
    middle = HEAD_DIM // 2
    frequency = 10000.0 ** (-(2.0 * (at % middle).astype(f32)) / HEAD_DIM)
    angles = places.astype(f32)[:, None] * frequency[None, :]
    sign = jnp.where(at < middle, -1.0, 1.0)[None, :]
    return (jnp.cos(angles), jnp.sin(angles) * sign)


def load_rows(pieces, offsets, target, sems):
    copies = []
    for i, piece in enumerate(pieces):
        copy = pltpu.make_async_copy(piece, target.at[pl.ds(pl.multiple_of(offsets[i], 16), piece.shape[0]), :], sems.at[i])
        copy.start()
        copies.append(copy)
    return copies


def project(hidden_prev, hidden_own, gain, cosines, sines, pieces, offsets):
    length, count = hidden_own.shape[0], len(pieces)

    def kernel(offsets_ref, prev_ref, own_ref, gain_ref, cos_ref, sin_ref, *rest):
        piece_refs, (q_ref, kv_ref, in_ref, weight, sems) = rest[:count], rest[count:]
        copies = load_rows(piece_refs, offsets_ref, weight, sems)
        for i, ref in enumerate((prev_ref, own_ref)):
            normed, _ = normalize(ref[...].astype(f32))
            in_ref[i * length : (i + 1) * length, :] = (normed * gain_ref[...]).astype(bf16)
        for copy in copies:
            copy.wait()
        values = dot(in_ref[length:, :], weight[:, :QW])
        cos_own, sin_own = cos_ref[length:, :], sin_ref[length:, :]
        for g in range(QW // PAIR):
            u = values[:, g * PAIR : (g + 1) * PAIR]
            q_ref[:, g * PAIR : (g + 1) * PAIR] = (u * cos_own + halves(u) * sin_own).astype(bf16)
        values = dot(in_ref[...], weight[:, QW:])
        for g in range(KVW // PAIR):
            u = values[:, g * PAIR : (g + 1) * PAIR]
            kv_ref[:, g * PAIR : (g + 1) * PAIR] = (u * cos_ref[...] + halves(u) * sin_ref[...]).astype(bf16)
        kv_ref[:, KVW:] = values[:, KVW:].astype(bf16)

    width = QW + 2 * KVW
    return call(
        kernel,
        [array((length, QW), bf16), array((2 * length, 2 * KVW), bf16), array((2 * length, D), bf16)],
        [SCALARS] + [whole(v.shape) for v in (hidden_prev, hidden_own, gain, cosines, sines)] + [STAY] * count,
        (offsets, hidden_prev, hidden_own, gain, cosines, sines, *pieces),
        scratch=[pltpu.VMEM((D, width), bf16), pltpu.SemaphoreType.DMA((count,))],
    )


def doubled(values, which):
    low = lanes(values.shape) < HEAD_DIM
    swapped = pltpu.roll(values, HEAD_DIM, 1)
    return jnp.where(low, values, swapped) if which == 0 else jnp.where(low, swapped, values)


def two_rows(pair):
    low = lanes(pair.shape) < HEAD_DIM
    zero = jnp.zeros_like(pair)
    return jnp.concatenate([jnp.where(low, pair, zero), jnp.where(low, zero, pair)], 0)


def named_experts(routes):
    shape = (routes.shape[0], 128)
    named = routes[:, 0:1] == lanes(shape)
    for k in range(1, TOP):
        named = named | (routes[:, k : k + 1] == lanes(shape))
    return named


def attend(query, kv, flag):
    length = query.shape[0]

    def kernel(flag_ref, q_ref, kv_ref, att_ref, lse_ref):
        bias = jnp.where((lanes((1, 2 * length)) >= length) | (flag_ref[0] > 0), 0.0, masked_score)
        lse_ref[...] = jnp.zeros(lse_ref.shape, f32)

        def pair_of_keys(jj, carry):
            at = pl.multiple_of(jj * PAIR, PAIR)
            keys = kv_ref[:, pl.ds(at, PAIR)].astype(f32)
            vals = kv_ref[:, pl.ds(KVW + at, PAIR)].astype(f32)
            for t in range(2):
                place = pl.multiple_of((2 * jj + t) * PAIR, PAIR)
                both = two_rows(q_ref[:, pl.ds(place, PAIR)].astype(f32)).astype(bf16)
                scores = dot(both, doubled(keys, t).astype(bf16), ((1,), (1,))) * score_scale + bias
                largest = jnp.max(scores, -1, keepdims=True)
                exponent = jnp.exp(scores - largest)
                totals = jnp.sum(exponent, -1, keepdims=True)
                probs = (exponent * (1.0 / totals)).astype(bf16)
                lse = largest + jnp.log(totals)
                lse_ref[...] = jnp.where(lanes(lse_ref.shape) == 2 * jj + t, lse, lse_ref[...])
                val = doubled(vals, t)
                low = lanes(val.shape) < HEAD_DIM
                zero = jnp.zeros_like(val)
                out = dot(probs[:length], jnp.where(low, val, zero).astype(bf16))
                out = out + dot(probs[length:], jnp.where(low, zero, val).astype(bf16))
                att_ref[:, pl.ds(place, PAIR)] = out.astype(bf16)
            return carry

        lax.fori_loop(0, KVW // PAIR, pair_of_keys, 0)

    return call(
        kernel,
        [array((length, QW), bf16), array((2 * length, 128), f32)],
        [SCALARS, whole(query.shape), whole(kv.shape)],
        (flag, query, kv),
    )


def enter_experts(attended, hidden_own, gain, router_w, routes, pieces, offsets):
    length, count = attended.shape[0], len(pieces)

    def kernel(offsets_ref, att_ref, own_ref, gain_ref, router_ref, routes_ref, *rest):
        piece_refs, (res_ref, gate_ref, pay_ref, weight, sems) = rest[:count], rest[count:]
        copies = load_rows(piece_refs, offsets_ref, weight, sems)
        for copy in copies:
            copy.wait()
        residual = own_ref[...].astype(f32) + dot(att_ref[...], weight[...])
        res_ref[...] = residual
        normed, _ = normalize(residual)
        rows = (normed * gain_ref[...]).astype(bf16)
        pay_ref[:length, :] = rows
        logits = dot(rows, router_ref[...], ((1,), (1,)))
        real = lanes(logits.shape) < EXPERTS
        logits = jnp.where(real, logits, masked_score)
        raised = jnp.where(real, jnp.exp(logits - jnp.max(logits, -1, keepdims=True)), 0.0)
        router = raised * (1.0 / jnp.sum(raised, -1, keepdims=True))
        gate_ref[...] = router
        gates = jnp.where(named_experts(routes_ref[...]), router, 0.0).T[:EXTRA]
        high = gates.astype(bf16)
        pay_ref[length:, :length] = high
        pay_ref[length:, length : 2 * length] = (gates - high.astype(f32)).astype(bf16)
        pay_ref[length:, 2 * length :] = jnp.zeros((EXTRA, D - 2 * length), bf16)

    operands = (attended, hidden_own, gain, router_w, routes)
    return call(
        kernel,
        [array((length, D), f32), array((length, 128), f32), array((length + EXTRA, D), bf16)],
        [SCALARS] + [whole(v.shape) for v in operands] + [STAY] * count,
        (offsets, *operands, *pieces),
        scratch=[pltpu.VMEM((QW, D), bf16), pltpu.SemaphoreType.DMA((count,))],
    )


def write_chunks(out_refs, at, values):
    part = F // len(out_refs)
    deep = 128

    def rows(r, carry):
        for c, out_ref in enumerate(out_refs):
            piece = values[pl.ds(pl.multiple_of(r * deep, deep), deep), c * part : (c + 1) * part]
            out_ref[pl.ds(pl.multiple_of(r * deep, deep), deep), at * part : (at + 1) * part] = piece.astype(bf16)
        return carry

    lax.fori_loop(0, D // deep, rows, 0)


def clear(i, accs):
    deep = 128

    @pl.when(i == 0)
    def _():
        def rows(r, carry):
            for acc in accs:
                acc[pl.ds(pl.multiple_of(r * deep, deep), deep), :] = jnp.zeros((deep, acc.shape[1]), f32)
            return carry

        lax.fori_loop(0, D // deep, rows, 0)


def expert(rows, grads, w_gate_up, w_down, index, chunks):
    sources, blocks, tall = len(grads), len(rows), rows[0].shape[0]
    length = tall - EXTRA
    step = 2
    turns = grads[0].shape[0] // step
    steps = blocks // step

    def kernel(index_ref, *refs):
        row_refs, grad_refs, refs = refs[:blocks], refs[blocks : blocks + sources], refs[blocks + sources :]
        gate_up_ref, down_ref, dgu_ref, hid_ref, sum_ref = refs[:5]
        out_refs, (both_ref, grad_ref, table_ref, *accs) = refs[5 : 5 + chunks], refs[5 + chunks :]
        i = pl.program_id(0)
        for source, source_ref in enumerate(grad_refs):

            @pl.when((i >= source * turns) & (i < (source + 1) * turns))
            def _():
                for b in range(step):
                    grad_ref[b * length : (b + 1) * length, :] = source_ref[b]

        for j, row_ref in enumerate(row_refs):
            b = j % step

            @pl.when(i == j // step)
            def _():
                both_ref[b * length : (b + 1) * length, :] = row_ref[:length, :]
                high, low = row_ref[length:, :length], row_ref[length:, length : 2 * length]
                table_ref[b] = high.astype(f32) + low.astype(f32)

        both, grad = both_ref[...], grad_ref[...]
        columns = []
        for b in range(step):
            table = table_ref[b]
            mine = lax.broadcasted_iota(jnp.int32, table.shape, 0) == index_ref[1]
            row = jnp.sum(jnp.where(mine, table, 0.0), 0, keepdims=True)
            columns.append(jnp.broadcast_to(row, (128, length)).T[:, :1])
        gate = jnp.concatenate(columns, 0)
        gate_up = dot(both, gate_up_ref[0])
        gate_part, up_part = gate_up[:, :F], gate_up[:, F:]
        sigmoid_g = jax.nn.sigmoid(gate_part)
        silu_g = gate_part * sigmoid_g
        hidden = silu_g * up_part
        raw = dot(grad, down_ref[0])
        sums = jnp.sum(raw * hidden, 1, keepdims=True)
        gated = (gate * hidden).astype(bf16)
        grad_hidden = gate * raw
        grad_gate = (grad_hidden * up_part * sigmoid_g * (1.0 + gate_part * (1.0 - sigmoid_g))).astype(bf16)
        grad_up = (grad_hidden * silu_g).astype(bf16)
        for b in range(step):
            at = slice(b * length, (b + 1) * length)
            dgu_ref[b, :, :F] = grad_gate[at]
            dgu_ref[b, :, F:] = grad_up[at]
            hid_ref[b] = gated[at]
            sum_ref[b] = jnp.broadcast_to(sums[at], (length, 128)).T[:8]
        if not chunks:
            return
        clear(i, accs)
        for p, (left, right) in enumerate(((both, grad_gate), (both, grad_up), (grad, gated))):
            accs[p][...] += dot(left, right, ((0,), (0,)))

            @pl.when(i == steps - 1)
            def _():
                write_chunks(out_refs, p, accs[p])

    def block(*shape):
        return pl.BlockSpec((step,) + shape, lambda i, index: (i,) + (0,) * len(shape))

    def source_block(source, *shape):
        def at(i, index):
            return (jnp.clip(i - source * turns, 0, turns - 1),) + (0,) * len(shape)

        return pl.BlockSpec((step,) + shape, at)

    def weight(*shape):
        return pl.BlockSpec((1,) + shape, lambda i, index: (index[0], 0, 0))

    shapes = [array((blocks, length, 2 * F), bf16), array((blocks, length, F), bf16), array((blocks, 8, length), f32)]
    scratch = [
        pltpu.VMEM((step * length, D), bf16),
        pltpu.VMEM((step * length, D), bf16),
        pltpu.VMEM((step, EXTRA, length), f32),
    ]
    return call(
        kernel,
        shapes + [array((D, 3 * F // chunks), bf16)] * chunks if chunks else shapes,
        [whole((tall, D))] * blocks
        + [source_block(s, length, D) for s in range(sources)]
        + [weight(D, 2 * F), weight(D, F)],
        (index, *rows, *grads, w_gate_up, w_down),
        out_specs=[block(length, 2 * F), block(length, F), block(8, length)]
        + [pl.BlockSpec((D, 3 * F // chunks), lambda i, index: (0, 0)) for _ in range(chunks)],
        scratch=scratch + ([pltpu.VMEM((D, F), f32)] * 3 if chunks else []),
        grid=(steps,),
        prefetch=1,
    )


def gate_column(table, expert):
    mine = lax.broadcasted_iota(jnp.int32, table.shape, 0) == expert
    row = jnp.sum(jnp.where(mine, table, 0.0), 0, keepdims=True)
    return jnp.broadcast_to(row, (128, table.shape[1])).T[:, :1]


def last_expert(rows, grads, w_gate_up, w_down, indices, earlier, sums):
    sources, blocks, tall = len(grads), len(rows), rows[0].shape[0]
    length = tall - EXTRA
    step = 2
    turns = grads[0].shape[0] // step
    steps = blocks // step
    others = len(earlier)

    def kernel(indices_ref, *refs):
        row_refs, grad_refs, refs = refs[:blocks], refs[blocks : blocks + sources], refs[blocks + sources :]
        gate_up_ref, down_ref, refs = refs[0], refs[1], refs[2:]
        earlier_refs, weight_refs, sum_refs, refs = refs[:others], refs[others : 2 * others], refs[2 * others : 3 * others], refs[3 * others :]
        dgu_ref, hid_ref, out_refs, (both_ref, grad_ref, table_ref) = refs[0], refs[1], refs[2 : 2 + sources], refs[2 + sources :]
        i = pl.program_id(0)
        for source, source_ref in enumerate(grad_refs):

            @pl.when((i >= source * turns) & (i < (source + 1) * turns))
            def _():
                for b in range(step):
                    grad_ref[b * length : (b + 1) * length, :] = source_ref[b]

        for j, row_ref in enumerate(row_refs):
            b = j % step

            @pl.when(i == j // step)
            def _():
                both_ref[b * length : (b + 1) * length, :] = row_ref[:length, :]
                high, low = row_ref[length:, :length], row_ref[length:, length : 2 * length]
                table_ref[b] = high.astype(f32) + low.astype(f32)

        both, grad = both_ref[...], grad_ref[...]
        gate = jnp.concatenate([gate_column(table_ref[b], indices_ref[2 * others + 1]) for b in range(step)], 0)
        gate_up = dot(both, gate_up_ref[0])
        gate_part, up_part = gate_up[:, :F], gate_up[:, F:]
        sigmoid_g = jax.nn.sigmoid(gate_part)
        silu_g = gate_part * sigmoid_g
        hidden = silu_g * up_part
        raw = dot(grad, down_ref[0])
        own = jnp.sum(raw * hidden, 1, keepdims=True)
        gated = (gate * hidden).astype(bf16)
        grad_hidden = gate * raw
        grad_gate = (grad_hidden * up_part * sigmoid_g * (1.0 + gate_part * (1.0 - sigmoid_g))).astype(bf16)
        grad_up = (grad_hidden * silu_g).astype(bf16)
        total = dot(jnp.concatenate([grad_gate, grad_up], 1), gate_up_ref[0], ((1,), (1,)))
        for part_ref, weight_ref in zip(earlier_refs, weight_refs):
            part = jnp.concatenate([part_ref[b] for b in range(step)], 0)
            total = total + dot(part, weight_ref[0], ((1,), (1,)))
        for b in range(step):
            at = slice(b * length, (b + 1) * length)
            dgu_ref[b, :, :F] = grad_gate[at]
            dgu_ref[b, :, F:] = grad_up[at]
            hid_ref[b] = gated[at]
            table = jnp.zeros((EXTRA, length), f32)
            place = lax.broadcasted_iota(jnp.int32, table.shape, 0)
            for e in range(others):
                table = jnp.where(place == indices_ref[2 * e + 1], sum_refs[e][b, :1, :], table)
            row = jnp.broadcast_to(own[at], (length, 128)).T[:1]
            table = jnp.where(place == indices_ref[2 * others + 1], row, table)
            high = table.astype(bf16)
            for source, out_ref in enumerate(out_refs):

                @pl.when((i >= source * turns) & (i < (source + 1) * turns))
                def _():
                    out_ref[b, :length, :] = total[at].astype(bf16)
                    out_ref[b, length:, :length] = high
                    out_ref[b, length:, length : 2 * length] = (table - high.astype(f32)).astype(bf16)
                    out_ref[b, length:, 2 * length :] = jnp.zeros((EXTRA, D - 2 * length), bf16)

    def block(*shape):
        return pl.BlockSpec((step,) + shape, lambda i, index: (i,) + (0,) * len(shape))

    def source_block(source, *shape):
        def at(i, index):
            return (jnp.clip(i - source * turns, 0, turns - 1),) + (0,) * len(shape)

        return pl.BlockSpec((step,) + shape, at)

    def weight(e, *shape):
        return pl.BlockSpec((1,) + shape, lambda i, index: (index[2 * e], 0, 0))

    return call(
        kernel,
        [array((blocks, length, 2 * F), bf16), array((blocks, length, F), bf16)]
        + [array((blocks // sources, tall, D), bf16)] * sources,
        [whole((tall, D))] * blocks
        + [source_block(s, length, D) for s in range(sources)]
        + [weight(others, D, 2 * F), weight(others, D, F)]
        + [block(length, 2 * F)] * others
        + [weight(e, D, 2 * F) for e in range(others)]
        + [block(8, length)] * others,
        (indices, *rows, *grads, w_gate_up, w_down, *earlier, *[w_gate_up] * others, *sums),
        out_specs=[block(length, 2 * F), block(length, F)] + [source_block(s, tall, D) for s in range(sources)],
        scratch=[
            pltpu.VMEM((step * length, D), bf16),
            pltpu.VMEM((step * length, D), bf16),
            pltpu.VMEM((step, EXTRA, length), f32),
        ],
        grid=(steps,),
        prefetch=1,
    )


def weight_grads(rows, grads, grad_gate_up, hidden, chunks, after):
    sources, blocks, tall = len(grads), len(rows), rows[0].shape[0]
    length = tall - EXTRA
    step = 2
    turns = grads[0].shape[0] // step
    steps = blocks // step

    def kernel(after_ref, *refs):
        row_refs, grad_refs, refs = refs[:blocks], refs[blocks : blocks + sources], refs[blocks + sources :]
        dgu_ref, hid_ref, out_refs = refs[0], refs[1], refs[2 : 2 + chunks]
        both_ref, grad_ref, *accs = refs[2 + chunks :]
        i = pl.program_id(0)
        for source, source_ref in enumerate(grad_refs):

            @pl.when((i >= source * turns) & (i < (source + 1) * turns))
            def _():
                for b in range(step):
                    grad_ref[b * length : (b + 1) * length, :] = source_ref[b]

        for j, row_ref in enumerate(row_refs):
            b = j % step

            @pl.when(i == j // step)
            def _():
                both_ref[b * length : (b + 1) * length, :] = row_ref[:length, :]

        both, grad = both_ref[...], grad_ref[...]
        grad_gate = jnp.concatenate([dgu_ref[b, :, :F] for b in range(step)], 0)
        grad_up = jnp.concatenate([dgu_ref[b, :, F:] for b in range(step)], 0)
        gated = jnp.concatenate([hid_ref[b] for b in range(step)], 0)
        clear(i, accs)
        for p, (left, right) in enumerate(((both, grad_gate), (both, grad_up), (grad, gated))):
            accs[p][...] += dot(left, right, ((0,), (0,)))

            @pl.when(i == steps - 1)
            def _():
                write_chunks(out_refs, p, accs[p])

    def block(*shape):
        return pl.BlockSpec((step,) + shape, lambda i, after: (i,) + (0,) * len(shape))

    def source_block(source, *shape):
        def at(i, after):
            return (jnp.clip(i - source * turns, 0, turns - 1),) + (0,) * len(shape)

        return pl.BlockSpec((step,) + shape, at)

    return call(
        kernel,
        [array((D, 3 * F // chunks), bf16)] * chunks,
        [whole((tall, D))] * blocks
        + [source_block(s, length, D) for s in range(sources)]
        + [block(length, 2 * F), block(length, F)],
        (after, *rows, *grads, grad_gate_up, hidden),
        out_specs=[pl.BlockSpec((D, 3 * F // chunks), lambda i, after: (0, 0)) for _ in range(chunks)],
        scratch=[pltpu.VMEM((step * length, D), bf16)] * 2 + [pltpu.VMEM((D, F), f32)] * 3,
        grid=(steps,),
        prefetch=1,
    )


def row_terms(parts, weights, indices, sources):
    blocks, length, width = parts[0].shape
    count = len(parts)
    step = 2
    turns = blocks // step // sources

    def kernel(indices_ref, *refs):
        part_refs, weight_refs, out_refs = refs[:count], refs[count : 2 * count], refs[2 * count :]
        i = pl.program_id(0)
        total = None
        for part_ref, weight_ref in zip(part_refs, weight_refs):
            term = dot(jnp.concatenate([part_ref[b] for b in range(step)], 0), weight_ref[0], ((1,), (1,)))
            total = term if total is None else total + term
        for source, out_ref in enumerate(out_refs):

            @pl.when((i >= source * turns) & (i < (source + 1) * turns))
            def _():
                for b in range(step):
                    out_ref[b] = total[b * length : (b + 1) * length].astype(bf16)

    def weight(e):
        return pl.BlockSpec((1,) + weights.shape[1:], lambda i, index: (index[2 * e], 0, 0))

    def source_block(source):
        return pl.BlockSpec((step, length, D), lambda i, index: (jnp.clip(i - source * turns, 0, turns - 1), 0, 0))

    return call(
        kernel,
        [array((blocks // sources, length, D), bf16)] * sources,
        [pl.BlockSpec((step, length, width), lambda i, index: (i, 0, 0))] * count + [weight(e) for e in range(count)],
        (indices, *parts, *[weights] * count),
        out_specs=[source_block(s) for s in range(sources)],
        grid=(blocks // step,),
        prefetch=1,
    )


def backward(
    returned, residual, router, routes, cotangent, gain, router_w, query, kv, lse, cosines, sines, inputs,
    hidden_prev, hidden_own, attended, out_pieces, out_offsets, qkv_pieces, qkv_offsets, flag, core, shards, cores,
):
    length, terms = residual.shape[0], len(returned)
    width = QW + 2 * KVW
    out_count, qkv_count = len(out_pieces), len(qkv_pieces)

    deep = D // (shards * cores)

    def kernel(out_offsets_ref, qkv_offsets_ref, flag_ref, core_ref, *rest):
        term_refs, rest = rest[:terms], rest[terms:]
        res_ref, gate_ref, routes_ref, cot_ref, gain_ref, router_ref, q_ref, kv_ref, lse_ref, cos_ref, sin_ref = rest[:11]
        in_ref, prev_ref, own_ref, att_ref, rest = *rest[11:15], rest[15:]
        out_refs, qkv_refs, rest = rest[:out_count], rest[out_count : out_count + qkv_count], rest[out_count + qkv_count :]
        gres_ref, gown_ref, gprev_ref, own_grad_ref = rest[:4]
        far_refs, rest = rest[4 : 4 + 3 * (cores - 1)], rest[4 + 3 * (cores - 1) :]
        w_out, w_qkv, gatt_ref, dq_ref, dkv_ref, small_ref, sum_ref, out_sems, qkv_sems, end_sems = rest
        out_copies = load_rows(out_refs, out_offsets_ref, w_out, out_sems)
        qkv_copies = load_rows(qkv_refs, qkv_offsets_ref, w_qkv, qkv_sems)
        total = term_refs[0][...].astype(f32)
        for ref in term_refs[1:]:
            total = total + ref[...].astype(f32)
        table = total[length:, :length] + total[length:, length : 2 * length]
        gate_grads = jnp.concatenate([table, jnp.zeros((128 - EXTRA, length), f32)], 0).T
        grad_router = jnp.where(named_experts(routes_ref[...]), gate_grads, 0.0)
        router = gate_ref[...]
        grad_logits = (router * (grad_router - jnp.sum(router * grad_router, -1, keepdims=True))).astype(bf16)
        grad_input = total[:length] + dot(grad_logits, router_ref[...])
        normed, inverse = normalize(res_ref[...])
        gain_row = gain_ref[...]
        rows = (normed * gain_row).astype(bf16)
        small = dot(rows, grad_logits, ((0,), (0,)))
        gain_grad = jnp.sum(grad_input * normed, 0, keepdims=True)
        small_ref[...] = jnp.where(lanes((D, 128)) == EXPERTS, jnp.broadcast_to(gain_grad, (128, D)).T, small)
        grad_residual = cot_ref[...].astype(f32) + norm_back(normed, inverse, grad_input * gain_row)
        gres_ref[...] = grad_residual
        grad_attn = grad_residual.astype(bf16)
        for copy in out_copies:
            copy.wait()
        gatt_ref[...] = dot(grad_attn, w_out[...], ((1,), (1,))).astype(bf16)

        def write(at, values):
            sum_ref[:, at : at + values.shape[1]] = values.astype(bf16)

        write(width, dot(att_ref[...], grad_attn, ((0,), (0,))))

        bias = jnp.where((lanes((1, 2 * length)) >= length) | (flag_ref[0] > 0), 0.0, masked_score)
        cos_own, sin_own = cos_ref[length:, :], sin_ref[length:, :]

        def back(values, cos, sin):
            return (values * cos - halves(values) * sin).astype(bf16)

        def pair_of_keys(jj, carry):
            at = pl.multiple_of(jj * PAIR, PAIR)
            keys = kv_ref[:, pl.ds(at, PAIR)].astype(f32)
            vals = kv_ref[:, pl.ds(KVW + at, PAIR)].astype(f32)
            key_grads, val_grads = [], []
            for t in range(2):
                place = pl.multiple_of((2 * jj + t) * PAIR, PAIR)
                both = two_rows(q_ref[:, pl.ds(place, PAIR)].astype(f32)).astype(bf16)
                outs = two_rows(gatt_ref[:, pl.ds(place, PAIR)].astype(f32)).astype(bf16)
                key = doubled(keys, t).astype(bf16)
                val = doubled(vals, t).astype(bf16)
                own = lanes(lse_ref.shape) == 2 * jj + t
                log_total = jnp.sum(jnp.where(own, lse_ref[...], 0.0), -1, keepdims=True)
                scores = dot(both, key, ((1,), (1,))) * score_scale + bias
                probs = jnp.exp(scores - log_total)
                grad_probs = dot(outs, val, ((1,), (1,)))
                inner = jnp.sum(probs * grad_probs, -1, keepdims=True)
                grad_scores = (probs * (grad_probs - inner)).astype(bf16)
                grad_query = dot(grad_scores, key) * score_scale
                low = lanes((length, PAIR)) < HEAD_DIM
                grad_query = jnp.where(low, grad_query[:length], grad_query[length:])
                dq_ref[:, pl.ds(place, PAIR)] = back(grad_query, cos_own, sin_own)
                key_grad = dot(grad_scores, both, ((0,), (0,))) * score_scale
                val_grad = dot(probs.astype(bf16), outs, ((0,), (0,)))
                key_grads.append(key_grad + pltpu.roll(key_grad, HEAD_DIM, 1))
                val_grads.append(val_grad + pltpu.roll(val_grad, HEAD_DIM, 1))
            low = lanes((2 * length, PAIR)) < HEAD_DIM
            dkv_ref[:, pl.ds(at, PAIR)] = back(jnp.where(low, *key_grads), cos_ref[...], sin_ref[...])
            dkv_ref[:, pl.ds(KVW + at, PAIR)] = jnp.where(low, *val_grads).astype(bf16)
            return carry

        lax.fori_loop(0, KVW // PAIR, pair_of_keys, 0)
        write(0, dot(in_ref[length:, :], dq_ref[...], ((0,), (0,))))
        write(QW, dot(in_ref[...], dkv_ref[...], ((0,), (0,))))
        for copy in qkv_copies:
            copy.wait()
        from_kv = dot(dkv_ref[...], w_qkv[:, QW:], ((1,), (1,)))
        own = from_kv[length:] + dot(dq_ref[...], w_qkv[:, :QW], ((1,), (1,)))
        gown_ref[...] = own
        gprev_ref[...] = from_kv[:length].astype(bf16)
        normed_own, _ = normalize(own_ref[...].astype(f32))
        normed_prev, _ = normalize(prev_ref[...].astype(f32))
        gain_grad = jnp.sum(own * normed_own + from_kv[:length] * normed_prev, 0, keepdims=True)
        column = jnp.broadcast_to(gain_grad, (128, D)).T
        write(width + D, jnp.where(lanes((D, 128)) == EXPERTS + 1, column, small_ref[...]))
        copies = []
        for s in range(shards):
            for j in range(cores):
                at = pl.multiple_of((s * cores + (core_ref[0] + j) % cores) * deep, 16)
                targets = [(own_grad_ref, 0)] if j == 0 else [(far_refs[3 * (j - 1) + g], g * D) for g in range(3)]
                for g, (target, start) in enumerate(targets):
                    source = sum_ref.at[pl.ds(at, deep), start : start + target.shape[2]]
                    copy = pltpu.make_async_copy(source, target.at[s], end_sems.at[s, j, g])
                    copy.start()
                    copies.append(copy)
        for copy in copies:
            copy.wait()

    operands = (
        *returned, residual, router, routes, cotangent, gain, router_w, query, kv, lse, cosines, sines, inputs,
        hidden_prev, hidden_own, attended,
    )
    return call(
        kernel,
        [
            array((length, D), f32),
            array((length, D), f32),
            array((length, D), bf16),
        ]
        + [array((shards, deep, width + D + 128), bf16)]
        + [array((shards, deep, w), bf16) for w in (D, D, D + 128)] * (cores - 1),
        [SCALARS] * 4 + [whole(v.shape) for v in operands] + [STAY] * (out_count + qkv_count),
        (out_offsets, qkv_offsets, flag, core, *operands, *out_pieces, *qkv_pieces),
        out_specs=[whole((length, D)), whole((length, D)), whole((length, D))] + [STAY] * (1 + 3 * (cores - 1)),
        scratch=[
            pltpu.VMEM((QW, D), bf16),
            pltpu.VMEM((D, width), bf16),
            pltpu.VMEM((length, QW), bf16),
            pltpu.VMEM((length, QW), bf16),
            pltpu.VMEM((2 * length, 2 * KVW), bf16),
            pltpu.VMEM((D, 128), f32),
            pltpu.VMEM((D, width + D + 128), bf16),
            pltpu.SemaphoreType.DMA((out_count,)),
            pltpu.SemaphoreType.DMA((qkv_count,)),
            pltpu.SemaphoreType.DMA((shards, cores, 3)),
        ],
    )


def first_back(grad_sum, grad_residual, hidden_own, gain):
    def kernel(sum_ref, res_ref, hid_ref, gain_ref, out_ref):
        normed, inverse = normalize(hid_ref[...].astype(f32))
        grad = sum_ref[...] * gain_ref[...]
        out_ref[...] = res_ref[...] + norm_back(normed, inverse, grad)

    operands = (grad_sum, grad_residual, hidden_own, gain)
    return call(kernel, [array(grad_sum.shape, f32)], [whole(v.shape) for v in operands], operands, vmem=16 * 1024 * 1024)[0]


def place(sources, experts, outs, shapes, chunk, chunks):
    part = F // chunks
    count = sum(source.shape[0] for source in sources)

    def kernel(experts_ref, *refs):
        source_refs = refs[: len(sources)]
        gate_up_ref, down_ref, wide, sems = refs[len(sources) + len(outs) :]
        copies = []
        deep = 128
        values = [ref.at[i] for ref in source_refs for i in range(ref.shape[0])]
        for i, source in enumerate(values):

            def rows(r, carry):
                at = pl.ds(pl.multiple_of(r * deep, deep), deep)
                wide[i, at, :] = source[at, :].astype(f32)
                return carry

            lax.fori_loop(0, D // deep, rows, 0)
            for p, target in enumerate(
                (
                    gate_up_ref.at[experts_ref[i], :, chunk * part : (chunk + 1) * part],
                    gate_up_ref.at[experts_ref[i], :, F + chunk * part : F + (chunk + 1) * part],
                    down_ref.at[experts_ref[i], :, chunk * part : (chunk + 1) * part],
                )
            ):
                copy = pltpu.make_async_copy(wide.at[i, :, p * part : (p + 1) * part], target, sems.at[i, p])
                copy.start()
                copies.append(copy)
        for copy in copies:
            copy.wait()

    return call(
        kernel,
        shapes,
        [SCALARS] + [whole(v.shape) for v in sources] + [STAY] * len(outs),
        (experts, *sources, *outs),
        out_specs=[STAY, STAY],
        scratch=[pltpu.VMEM((count, D, 3 * part), f32), pltpu.SemaphoreType.DMA((count, 3))],
        aliases={1 + len(sources) + i: i for i in range(len(outs))},
        vmem=28 * 1024 * 1024,
    )


def unpack(sources, offsets, rows):
    count = sum(source.shape[0] for source in sources)
    deep, wide = sources[0].shape[1:]
    widths = (QW + 2 * KVW, D)

    def kernel(offsets_ref, *refs):
        source_refs, refs = refs[: len(sources)], refs[len(sources) :]
        out_refs, router_ref, ffn_ref, attn_ref, values_ref, rest_ref, sems = refs[:2], *refs[2:]
        copies = []
        for i, source in enumerate([ref.at[i] for ref in source_refs for i in range(ref.shape[0])]):
            values_ref[i] = source[...].astype(f32)
            at = pl.multiple_of(offsets_ref[i], 8)
            start = 0
            for p, (out_ref, width) in enumerate(zip(out_refs, widths)):
                copy = pltpu.make_async_copy(values_ref.at[i, :, start : start + width], out_ref.at[pl.ds(at, deep), :], sems.at[i, p])
                copy.start()
                copies.append(copy)
                start += width
            rest_ref[pl.ds(at, deep), :] = values_ref[i, :, start:]
        router_ref[...] = rest_ref[:, :EXPERTS]
        turned = rest_ref[...].T
        ffn_ref[...] = turned[EXPERTS : EXPERTS + 1]
        attn_ref[...] = turned[EXPERTS + 1 : EXPERTS + 2]
        for copy in copies:
            copy.wait()

    return call(
        kernel,
        [array((rows, width), f32) for width in widths] + [array((rows, EXPERTS), f32)] + [array((1, rows), f32)] * 2,
        [SCALARS] + [whole(v.shape) for v in sources],
        (offsets, *sources),
        out_specs=[STAY] * 2 + [whole((rows, EXPERTS))] + [whole((1, rows))] * 2,
        scratch=[
            pltpu.VMEM((count, deep, wide), f32),
            pltpu.VMEM((rows, wide - sum(widths)), f32),
            pltpu.SemaphoreType.DMA((count, 2)),
        ],
    )


def post(function, flags, arrays, outs):
    parts = 8

    def kernel(flags_ref, *refs):
        ins, results = refs[: len(arrays)], refs[len(arrays) :]
        scalars = [flags_ref[i] for i in range(flags.shape[0])]

        def part_of(ref, r):
            deep = ref.shape[-2] // parts
            return (slice(None),) * (len(ref.shape) - 2) + (pl.ds(pl.multiple_of(r * deep, deep), deep), slice(None))

        def rows(r, carry):
            values = function(scalars, *[ref[part_of(ref, r)] for ref in ins])
            for ref, value in zip(results, values):
                if isinstance(value, tuple):
                    value = jnp.stack(value)
                ref[part_of(ref, r)] = value.astype(ref.dtype)
            return carry

        lax.fori_loop(0, parts, rows, 0)

    near = pl.BlockSpec(memory_space=pltpu.VMEM)
    return pl.pallas_call(
        kernel,
        out_shape=list(outs),
        in_specs=[SCALARS] + [near] * len(arrays),
        out_specs=[near] * len(outs),
        compiler_params=pltpu.CompilerParams(vmem_limit_bytes=POST_VMEM),
        cost_estimate=pl.CostEstimate(flops=0, transcendentals=0, bytes_accessed=0),
    )(flags, *arrays)


def tie(values, after):
    return lax.optimization_barrier((values, after))[0]


def doubling_sum(value, axis):
    count, step = lax.axis_size(axis), 1
    if count & (count - 1):
        return lax.psum(value, axis)
    while step < count:
        value = value + lax.ppermute(value, axis, [(i, i ^ step) for i in range(count)])
        step *= 2
    return value


def body(
    hidden_in, routes, w_qkv, w_out, w_router, attn_gain, ffn_gain, w_gate_up, w_down, cotangent
):
    line, shards = lax.axis_size("line"), lax.axis_size("fsdp")
    side, cores = lax.axis_size("side"), lax.axis_size("core")
    shard, side_at, core_at = lax.axis_index("fsdp"), lax.axis_index("side"), lax.axis_index("core")
    length = hidden_in.shape[0]
    near = [(a, s) for s in range(shards) for a in range(side)]
    local_experts = w_gate_up.shape[0]
    count = local_experts // (side * cores)
    barrier = lax.optimization_barrier

    def other_core(value, core=1):
        return turn(value, "core", (core,), (cores,))

    def other_side(value, step=1):
        return turn(value, "side", (step,), (side,))

    def from_shard(part, step):
        return turn(part, "fsdp", (step,), (shards,))

    def fetch_start(piece, sides):
        part = own_part(piece, 0, core_at * sides + side_at % sides, cores * sides)
        return [from_shard(part, step) for step in range(1, shards)]

    def fetch_end(piece, first, sides):
        rows = piece.shape[0]
        out, offsets = [piece], [shard * rows]
        for step, part in enumerate(first, 1):
            base = (shard - step) % shards * rows
            for a in range(sides):
                theirs = other_side(part, a) if a else part
                for core in range(cores):
                    out.append(other_core(theirs, core) if core else theirs)
                    at = (core_at - core) % cores * sides + (side_at - a) % sides
                    offsets.append(base + at * part.shape[0])
        return out, jnp.stack(offsets).astype(jnp.int32)

    def over_cores(first):
        return [other_core(first, core) if core else first for core in range(cores)]

    def far_blocks(blocks):
        return [other_core(blocks[core * len(near) : (core + 1) * len(near)], -core % cores) for core in range(1, cores)]

    def add_up(first, others):
        for other in others:
            first = first + other
        return first

    def send_back(total):
        out = [total[0]]
        for i, (a, s) in enumerate(near):
            if (a, s) != (0, 0):
                out.append(turn(total[i], ("side", "fsdp"), (-a % side, -s % shards), (side, shards)))
        return out

    parity = shard % 2
    flag = parity.astype(jnp.int32)[None]
    later = [(i, i + 1) for i in range(0, shards, 2)]
    before = [(i + 1, i) for i in range(0, shards, 2)]

    small_rows = w_router.shape[0]
    small = jnp.concatenate([w_router.T, attn_gain[None], ffn_gain[None]], 0)
    qkv_first = fetch_start(w_qkv, side)
    hidden_prev = lax.ppermute(hidden_in, "fsdp", later)
    full_small = jnp.zeros((EXPERTS + 2, D), bf16)
    for step in range(shards):
        theirs = from_shard(small, step) if step else small
        full_small = lax.dynamic_update_slice_in_dim(full_small, theirs, (shard - step) % shards * small_rows, 1)
    gain_attn = full_small[EXPERTS : EXPERTS + 1].astype(f32)
    gain_ffn = full_small[EXPERTS + 1 :].astype(f32)
    router_w = jnp.pad(full_small[:EXPERTS], ((0, 128 - EXPERTS), (0, 0)))
    sideways = [other_side(cotangent, a) for a in range(1, side)]
    across = [from_shard(cotangent, s) for s in range(1, shards)]
    rows_at = jnp.arange(length, dtype=jnp.int32)
    cosines, sines = rotary_tables(jnp.concatenate([rows_at, parity * length + rows_at]))
    qkv_pieces, qkv_offsets = fetch_end(w_qkv, qkv_first, side)
    out_first = fetch_start(tie(w_out, (hidden_prev, qkv_first)), 1)

    across, hidden_prev = barrier((across, hidden_prev))
    corners = [[other_side(v, a) for a in range(1, side)] for v in across]
    queries, kv, inputs = project(hidden_prev, hidden_in, gain_attn, cosines, sines, qkv_pieces, qkv_offsets)
    out_first, queries, kv = barrier((out_first, queries, kv))
    out_pieces, out_offsets = fetch_end(w_out, out_first, 1)
    attended, lse = attend(queries, kv, flag)
    grads_near = [cotangent] + sideways + [v for first, rest in zip(across, corners) for v in [first] + rest]
    grads_near = jnp.stack(tie(grads_near, attended))
    out_pieces, attended, grads_near = barrier((out_pieces, attended, grads_near))
    grads_near = over_cores(grads_near)
    residual, router, payload = enter_experts(attended, hidden_in, gain_ffn, router_w, routes, out_pieces, out_offsets)
    rows_near = [turn(payload, ("side", "fsdp"), (a, s), (side, shards)) if (a, s) != (0, 0) else payload for a, s in near]
    rows_near = rows_near + [other_core(v, core) for core in range(1, cores) for v in rows_near]

    clock = []

    def run(function, *inputs):
        if clock:
            inputs = barrier((inputs, tuple(clock)))[0]
        out = function(*inputs)
        clock[:] = jax.tree.leaves(out)
        return out

    mine_at = (side_at * cores + core_at) * count
    indices = [jnp.stack([mine_at + e, shard * local_experts + mine_at + e]).astype(jnp.int32) for e in range(count)]
    both = jnp.concatenate(indices)
    order = jnp.stack([((side_at - a) % side * cores + (core_at - core) % cores) for core in range(cores) for a in range(side)])
    order = order.astype(jnp.int32) * count
    shapes = [array((local_experts, D, 2 * F), f32), array((local_experts, D, F), f32)]
    place_at = lax.axis_index("line")
    end = (place_at == 0) | (place_at == line - 1)

    def go_in(raw):
        return lax.ppermute(raw, "line", [(0, 1), (3, 2)])

    def cross(half):
        return lax.ppermute(half, "line", [(1, 2), (2, 1)])

    def in_and_out(sent):
        return lax.ppermute(sent, "line", [(0, 1), (1, 0), (2, 3), (3, 2)])

    def go_out(total):
        return lax.ppermute(total, "line", [(1, 0), (2, 3)])

    def chosen(got, kept):
        return jnp.where(end, got, kept)

    def sides(full):
        return [other_side(full, a) for a in range(1, side)]

    def core_swaps(pair):
        return [other_core(pair, core) for core in range(1, cores)]

    def stacked(full, others):
        return jnp.stack([full] + others)

    def plus(first, second):
        return first + second

    def split(blocks):
        return [blocks[core * len(near) : (core + 1) * len(near)] for core in range(cores)]

    def near_sums(first, others):
        total = add_up(first, others)
        return [total[i] for i in range(len(near))]

    def placed(pair, swaps, outs, e, c):
        return place([pair] + swaps, order + e, outs, shapes, c, CHUNKS)

    def back(terms):
        return backward(
            terms, residual, router, routes, cotangent, gain_ffn, router_w, queries, kv, lse, cosines, sines, inputs, hidden_prev,
            hidden_in, attended, out_pieces, out_offsets, qkv_pieces, qkv_offsets, flag, core_at.astype(jnp.int32)[None], shards, cores,
        )

    def by_shard(total):
        return total[0] if shards == 1 else own_part(total, 0, shard, shards)[0], [
            own_part(total, 0, (shard + step) % shards, shards)[0] for step in range(1, shards)
        ]

    def by_side(total):
        return own_part(total, 0, side_at, side), [own_part(total, 0, (side_at + a) % side, side) for a in range(1, side)]

    def by_step(total):
        return [total[s * side : (s + 1) * side] for s in range(shards)]

    def by_near(total):
        return total[0], [total[a] for a in range(1, side)]

    def swap_lines(value, step):
        return lax.ppermute(value, "line", [(i, i ^ step) for i in range(line)])

    flags = jnp.stack([end, shard > 0, side_at > 0]).astype(jnp.int32)

    def f(value):
        return value.astype(f32)

    def pick(flag, got, kept):
        return jnp.where(flag > 0, f(got), f(kept))

    def steps(function, outs, *arrays):
        outs = [v if isinstance(v, jax.ShapeDtypeStruct) else array(v, bf16) for v in outs]
        return run(lambda *v: tuple(post(function, flags, v, outs)), *arrays)

    if (line, side, cores, shards, count) != (4, 2, 2, 2, 2):
        grads_gu, hiddens, sums, chunks = [], [], [], []
        for e in range(count - 1):
            grad_gu, hidden, total, *parts = expert(rows_near, grads_near, w_gate_up, w_down, indices[e], CHUNKS)
            grads_gu.append(grad_gu)
            hiddens.append(hidden)
            sums.append(total)
            chunks.append(parts)
        grad_gu, hidden, *blocks = last_expert(rows_near, grads_near, w_gate_up, w_down, both, grads_gu, sums)
        hiddens.append(hidden)
        chunks.append(weight_grads(rows_near, grads_near, grad_gu, hidden, CHUNKS, both))
        terms = row_terms(hiddens, w_down, both, cores)
        returned = send_back([v for v in add_up(blocks[0], [other_core(g, -c % cores) for c, g in enumerate(blocks[1:], 1)])])
        mixed = send_back([v for v in add_up(terms[0], [other_core(g, -c % cores) for c, g in enumerate(terms[1:], 1)])])
        grad_residual, grad_own, grad_prev, own_w, *other_w = back(returned)
        joined = [jnp.concatenate(other_w[i : i + 3], -1) for i in range(0, len(other_w), 3)]
        own_w = add_up(own_w, [other_core(w, core) for core, w in enumerate(joined, 1)])
        own_w, other_w = by_shard(own_w)
        own_w = add_up(own_w, [from_shard(w, step) for step, w in enumerate(other_w, 1)])
        own_w = add_up(own_w, [other_side(own_w, a) for a in range(1, side)])

        def line_sum(value):
            if line & (line - 1):
                return lax.psum(value, "line")
            for bit in range(line.bit_length() - 1):
                value = value + swap_lines(value, 1 << bit)
            return value

        sum_w, outs = line_sum(own_w), ()
        for e, parts in enumerate(chunks):
            for c, part in enumerate(parts):
                full = line_sum(part)
                pair = jnp.stack([full] + sides(full))
                outs = placed(pair, core_swaps(pair), outs, e, c)
        at_w = jnp.stack([(core_at - core) % cores for core in range(cores)]).astype(jnp.int32) * sum_w.shape[0]
        qkv_sum, out_sum, router_sum, ffn_sum, attn_sum = unpack(
            [w[None] for w in [sum_w] + core_swaps(sum_w)], at_w, sum_w.shape[0] * cores
        )
        grad_sum = grad_own + lax.ppermute(grad_prev, "fsdp", before).astype(f32)
        grad_in = first_back(grad_sum, grad_residual, hidden_in, gain_attn)
        layer_out = add_up(residual, [m.astype(f32) for m in mixed]).astype(bf16)
        return (
            layer_out, grad_in, qkv_sum, out_sum, router_sum, attn_sum[0], ffn_sum[0], outs[0], outs[1],
        )

    gu_0, hid_0, sum_0, *parts_0 = run(lambda i: expert(rows_near, grads_near, w_gate_up, w_down, i, CHUNKS), indices[0])
    chunk = parts_0[0].shape
    two = (2,) + chunk
    in_0 = go_in(parts_0[0])
    gu_1, hid_1, first_half, other_half = run(
        lambda i: last_expert(rows_near, grads_near, w_gate_up, w_down, i, [gu_0], [sum_0]), both
    )
    far = [other_core(other_half)]
    (half_0,) = steps(lambda flag, raw, got: (f(raw) + f(got),), [chunk], parts_0[0], in_0)
    middle_0, in_1 = cross(half_0), go_in(parts_0[1])
    mixed, mixed_other = run(lambda i: row_terms([hid_0, hid_1], w_down, i, cores), both)
    blocks = run(near_sums, first_half, far)
    returned = send_back(blocks)
    parts_1 = run(lambda i: weight_grads(rows_near, grads_near, gu_1, hid_1, CHUNKS, i), both)

    def step_1(flag, half, middle, own, got, raw):
        total = f(half) + f(middle)
        return total, f(own) + f(got), pick(flag[0], raw, total)

    total_0, half_1, sent_2 = steps(step_1, [chunk] * 3, half_0, middle_0, parts_0[1], in_1, parts_1[0])
    both_2, middle_1 = in_and_out(sent_2), cross(half_1)
    grad_residual, grad_own, grad_prev, own_w, *other_w = run(back, returned)
    far_w = [other_core(w) for w in other_w]
    deep, wide = own_w.shape[1:]

    def step_2(flag, own, got, total, half, middle, raw, w, *far):
        summed = f(half) + f(middle)
        joined = f(w) + jnp.concatenate([f(v) for v in far], -1)
        mine, theirs = pick(flag[1], joined[1], joined[0]), pick(flag[1], joined[0], joined[1])
        return f(own) + f(got), pick(flag[0], got, total), summed, pick(flag[0], raw, summed), mine, theirs

    half_2, full_0, total_1, sent_3, own_w, other_w = steps(
        step_2, [chunk] * 4 + [(deep, wide)] * 2,
        parts_1[0], both_2, total_0, half_1, middle_1, parts_1[1], own_w, *far_w,
    )
    side_0, middle_2, both_3 = other_side(full_0), cross(half_2), in_and_out(sent_3)
    far_w, far_m = from_shard(other_w, 1), other_core(mixed_other)

    def step_3(flag, own, got, total, half, middle, first, other, w, far, m, m_far):
        terms = f(m) + f(m_far)
        return (
            f(own) + f(got), pick(flag[0], got, total), f(half) + f(middle), (first, other), f(w) + f(far), terms[:2], terms[2:],
        )

    rows_of = mixed.shape[1]
    half_3, full_1, total_2, pair_0, own_w, own_m, other_m = steps(
        step_3, [chunk] * 3 + [two, (deep, wide)] + [(2, rows_of, D)] * 2,
        parts_1[1], both_3, total_1, half_2, middle_2, full_0, side_0, own_w, far_w, mixed, far_m,
    )
    side_1, middle_3, out_2, core_0 = other_side(full_1), cross(half_3), go_out(total_2), other_core(pair_0)
    in_w = go_in(own_w)

    def step_4(flag, got, total, half, middle, first, other, w, far):
        return pick(flag[0], got, total), f(half) + f(middle), (first, other), f(w) + f(far)

    full_2, total_3, pair_1, half_w = steps(
        step_4, [chunk] * 2 + [two, (deep, wide)], out_2, total_2, half_3, middle_3, full_1, side_1, own_w, in_w
    )
    side_2, out_3, middle_w, core_1 = other_side(full_2), go_out(total_3), cross(half_w), other_core(pair_1)
    far_m = from_shard(other_m, 1)
    outs = run(lambda pair, swap: placed(pair, [swap], (), 0, 0), pair_0, core_0)

    def step_5(flag, got, total, first, other, w, far, m, m_far):
        terms = f(m) + f(m_far)
        return pick(flag[0], got, total), (first, other), f(w) + f(far), terms[0], terms[1]

    full_3, pair_2, total_w, own_m, other_m = steps(
        step_5, [chunk, two, (deep, wide)] + [(rows_of, D)] * 2, out_3, total_3, full_2, side_2, half_w, middle_w, own_m, far_m
    )
    side_3, out_w, core_2 = other_side(full_3), go_out(total_w), other_core(pair_2)
    far_m = other_side(other_m)
    grad_later = lax.ppermute(grad_prev, "fsdp", before)
    outs = run(lambda pair, swap, outs: placed(pair, [swap], outs, 0, 1), pair_1, core_1, outs)

    def step_6(flag, first, other, got, w, rest, m, m_far, own, back):
        return (first, other), pick(flag[0], got, w), rest + f(m) + f(m_far), own + f(back)

    pair_3, full_w, layer_out, grad_sum = steps(
        step_6, [two, (deep, wide), (rows_of, D), array((rows_of, D), f32)],
        full_3, side_3, out_w, total_w, residual, own_m, far_m, grad_own, grad_later,
    )
    core_3, side_w = other_core(pair_3), other_side(full_w)
    grad_in = run(lambda grad: first_back(grad, grad_residual, hidden_in, gain_attn), grad_sum)
    outs = run(lambda pair, swap, outs: placed(pair, [swap], outs, 1, 0), pair_2, core_2, outs)
    outs = run(lambda pair, swap, outs: placed(pair, [swap], outs, 1, 1), pair_3, core_3, outs)
    (sum_w,) = steps(lambda flag, w, far: (f(w) + f(far),), [(deep, wide)], full_w, side_w)
    core_w = other_core(sum_w)
    at_w = jnp.stack([(core_at - core) % cores for core in range(cores)]).astype(jnp.int32) * deep
    qkv_sum, out_sum, router_sum, ffn_sum, attn_sum = run(lambda *v: unpack([w[None] for w in v], at_w, deep * cores), sum_w, core_w)
    return (
        layer_out,
        grad_in,
        qkv_sum,
        out_sum,
        router_sum,
        attn_sum[0],
        ffn_sum[0],
        outs[0],
        outs[1],
    )


def solution(mesh):
    copies, shards = mesh.shape["rep"], mesh.shape["fsdp"]
    local = EXPERTS // shards
    cores = 2 if copies % 2 == 0 and local % 2 == 0 else 1
    side = 2 if cores == 2 and copies % 4 == 0 and local % 4 == 0 else 1
    names = ("line", "side", "core", "fsdp")
    parts = Mesh(mesh.devices.reshape(copies // (side * cores), side, cores, shards), names)
    rows, shard = P(names, None), P("fsdp", None)
    experts = P("fsdp", None, None)
    in_specs = (rows, rows, shard, shard, shard, P("fsdp"), P("fsdp"), experts, experts, rows)
    out_specs = (rows, rows, shard, shard, shard, P("fsdp"), P("fsdp"), experts, experts)
    return jax.shard_map(body, mesh=parts, in_specs=in_specs, out_specs=out_specs, check_vma=False)
```

```python
import math
from functools import partial

import jax
import jax.numpy as jnp
from jax import lax
from jax.experimental import pallas as pl
from jax.experimental.pallas import tpu as pltpu
from jax.sharding import Mesh, PartitionSpec as P

D = 1024
HEADS = 16
KV_HEADS = 8
HEAD_DIM = 64
F = 512
TOP = 8
EXPERTS = 16
BLOCK = 256
QW = HEADS * HEAD_DIM
KVW = KV_HEADS * HEAD_DIM
EXTRA = 16
CHUNKS = 2
PAIR = 2 * HEAD_DIM

norm_eps = 1e-06
masked_score = -1e30
score_scale = HEAD_DIM ** (-0.5)
bf16, f32 = jnp.bfloat16, jnp.float32
VMEM = 56 * 1024 * 1024
POST_VMEM = 18 * 1024 * 1024


def dot(left, right, dims=((1,), (0,))):
    return lax.dot_general(left, right, (dims, ((), ())), preferred_element_type=f32)


def turn(value, axes, steps, sizes):
    pairs = []
    for source in range(math.prod(sizes)):
        place, rest = [], source
        for size in reversed(sizes):
            place.append(rest % size)
            rest //= size
        place.reverse()
        target = 0
        for at, size, step in zip(place, sizes, steps):
            target = target * size + (at + step) % size
        pairs.append((source, target))
    return lax.ppermute(value, axes, pairs)


def own_part(value, axis, index, parts):
    size = value.shape[axis] // parts
    return lax.dynamic_slice_in_dim(value, index * size, size, axis)


def whole(shape):
    return pl.BlockSpec(shape, lambda *_: (0,) * len(shape))


SCALARS = pl.BlockSpec(memory_space=pltpu.SMEM)
STAY = pl.BlockSpec(memory_space=pl.ANY)


def call(kernel, out_shape, in_specs, operands, out_specs=None, scratch=(), grid=None, prefetch=0, aliases=None, vmem=VMEM):
    out_specs = [whole(s.shape) for s in out_shape] if out_specs is None else out_specs
    spec = pltpu.PrefetchScalarGridSpec(
        num_scalar_prefetch=prefetch,
        grid=grid or (1,),
        in_specs=in_specs,
        out_specs=out_specs,
        scratch_shapes=list(scratch),
    )
    return pl.pallas_call(
        kernel,
        out_shape=list(out_shape),
        grid_spec=spec,
        input_output_aliases=aliases or {},
        compiler_params=pltpu.CompilerParams(vmem_limit_bytes=vmem),
        cost_estimate=pl.CostEstimate(flops=0, transcendentals=0, bytes_accessed=0),
    )(*operands)


def array(shape, dtype):
    return jax.ShapeDtypeStruct(shape, dtype)


def normalize(rows):
    scale_inv = lax.rsqrt(jnp.mean(rows * rows, -1, keepdims=True) + norm_eps)
    return (rows * scale_inv, scale_inv)


def norm_back(normed, scale_inv, grad_normed):
    return scale_inv * (grad_normed - normed * jnp.mean(grad_normed * normed, -1, keepdims=True))


def lanes(shape):
    return lax.broadcasted_iota(jnp.int32, shape, len(shape) - 1)


def halves(values):
    low = lanes(values.shape) % HEAD_DIM < HEAD_DIM // 2
    half = HEAD_DIM // 2
    return jnp.where(low, pltpu.roll(values, PAIR - half, 1), pltpu.roll(values, half, 1))


def rotary_tables(places):
    at = jnp.arange(PAIR, dtype=jnp.int32) % HEAD_DIM
    middle = HEAD_DIM // 2
    frequency = 10000.0 ** (-(2.0 * (at % middle).astype(f32)) / HEAD_DIM)
    angles = places.astype(f32)[:, None] * frequency[None, :]
    sign = jnp.where(at < middle, -1.0, 1.0)[None, :]
    return (jnp.cos(angles), jnp.sin(angles) * sign)


def load_rows(pieces, offsets, target, sems):
    copies = []
    for i, piece in enumerate(pieces):
        copy = pltpu.make_async_copy(piece, target.at[pl.ds(pl.multiple_of(offsets[i], 16), piece.shape[0]), :], sems.at[i])
        copy.start()
        copies.append(copy)
    return copies


def project(hidden_prev, hidden_own, gain, cosines, sines, pieces, offsets):
    length, count = hidden_own.shape[0], len(pieces)

    def kernel(offsets_ref, prev_ref, own_ref, gain_ref, cos_ref, sin_ref, *rest):
        piece_refs, (q_ref, kv_ref, in_ref, weight, sems) = rest[:count], rest[count:]
        copies = load_rows(piece_refs, offsets_ref, weight, sems)
        deep = 64
        for i, ref in enumerate((prev_ref, own_ref)):

            def rows(r, carry):
                normed, _ = normalize(ref[pl.ds(pl.multiple_of(r * deep, deep), deep), :].astype(f32))
                at = pl.ds(pl.multiple_of(i * length + r * deep, deep), deep)
                in_ref[at, :] = (normed * gain_ref[...]).astype(bf16)
                return carry

            lax.fori_loop(0, length // deep, rows, 0)
        for copy in copies:
            copy.wait()
        values = dot(in_ref[length:, :], weight[:, :QW])
        cos_own, sin_own = cos_ref[length:, :], sin_ref[length:, :]
        for g in range(QW // PAIR):
            u = values[:, g * PAIR : (g + 1) * PAIR]
            q_ref[:, g * PAIR : (g + 1) * PAIR] = (u * cos_own + halves(u) * sin_own).astype(bf16)
        values = dot(in_ref[...], weight[:, QW:])
        for g in range(KVW // PAIR):
            u = values[:, g * PAIR : (g + 1) * PAIR]
            kv_ref[:, g * PAIR : (g + 1) * PAIR] = (u * cos_ref[...] + halves(u) * sin_ref[...]).astype(bf16)
        kv_ref[:, KVW:] = values[:, KVW:].astype(bf16)

    width = QW + 2 * KVW
    return call(
        kernel,
        [array((length, QW), bf16), array((2 * length, 2 * KVW), bf16), array((2 * length, D), bf16)],
        [SCALARS] + [whole(v.shape) for v in (hidden_prev, hidden_own, gain, cosines, sines)] + [STAY] * count,
        (offsets, hidden_prev, hidden_own, gain, cosines, sines, *pieces),
        scratch=[pltpu.VMEM((D, width), bf16), pltpu.SemaphoreType.DMA((count,))],
    )


def doubled(values, which):
    low = lanes(values.shape) < HEAD_DIM
    swapped = pltpu.roll(values, HEAD_DIM, 1)
    return jnp.where(low, values, swapped) if which == 0 else jnp.where(low, swapped, values)


def two_rows(pair):
    low = lanes(pair.shape) < HEAD_DIM
    zero = jnp.zeros_like(pair)
    return jnp.concatenate([jnp.where(low, pair, zero), jnp.where(low, zero, pair)], 0)


def named_experts(routes):
    shape = (routes.shape[0], 128)
    named = routes[:, 0:1] == lanes(shape)
    for k in range(1, TOP):
        named = named | (routes[:, k : k + 1] == lanes(shape))
    return named


def attend(query, kv, flag):
    length = query.shape[0]

    def kernel(flag_ref, q_ref, kv_ref, att_ref, lse_ref):
        bias = jnp.where((lanes((1, 2 * length)) >= length) | (flag_ref[0] > 0), 0.0, masked_score)
        lse_ref[...] = jnp.zeros(lse_ref.shape, f32)

        def pair_of_keys(jj, carry):
            at = pl.multiple_of(jj * PAIR, PAIR)
            keys = kv_ref[:, pl.ds(at, PAIR)].astype(f32)
            vals = kv_ref[:, pl.ds(KVW + at, PAIR)].astype(f32)
            for t in range(2):
                place = pl.multiple_of((2 * jj + t) * PAIR, PAIR)
                both = (two_rows(q_ref[:, pl.ds(place, PAIR)].astype(f32)) * score_scale).astype(bf16)
                scores = dot(both, doubled(keys, t).astype(bf16), ((1,), (1,))) + bias
                largest = jnp.max(scores, -1, keepdims=True)
                exponent = jnp.exp(scores - largest)
                totals = jnp.sum(exponent, -1, keepdims=True)
                probs = (exponent * (1.0 / totals)).astype(bf16)
                lse = largest + jnp.log(totals)
                lse_ref[...] = jnp.where(lanes(lse_ref.shape) == 2 * jj + t, lse, lse_ref[...])
                val = doubled(vals, t)
                low = lanes(val.shape) < HEAD_DIM
                zero = jnp.zeros_like(val)
                out = dot(probs[:length], jnp.where(low, val, zero).astype(bf16))
                out = out + dot(probs[length:], jnp.where(low, zero, val).astype(bf16))
                att_ref[:, pl.ds(place, PAIR)] = out.astype(bf16)
            return carry

        lax.fori_loop(0, KVW // PAIR, pair_of_keys, 0)

    return call(
        kernel,
        [array((length, QW), bf16), array((2 * length, 128), f32)],
        [SCALARS, whole(query.shape), whole(kv.shape)],
        (flag, query, kv),
    )


def enter_experts(attended, hidden_own, gain, router_w, routes, pieces, offsets):
    length, count = attended.shape[0], len(pieces)

    def kernel(offsets_ref, att_ref, own_ref, gain_ref, router_ref, routes_ref, *rest):
        piece_refs, (res_ref, gate_ref, pay_ref, weight, sems) = rest[:count], rest[count:]
        copies = load_rows(piece_refs, offsets_ref, weight, sems)
        for copy in copies:
            copy.wait()
        residual = own_ref[...].astype(f32) + dot(att_ref[...], weight[...])
        res_ref[...] = residual
        normed, _ = normalize(residual)
        rows = (normed * gain_ref[...]).astype(bf16)
        pay_ref[:length, :] = rows
        logits = dot(rows, router_ref[...], ((1,), (1,)))
        real = lanes(logits.shape) < EXPERTS
        logits = jnp.where(real, logits, masked_score)
        raised = jnp.where(real, jnp.exp(logits - jnp.max(logits, -1, keepdims=True)), 0.0)
        router = raised * (1.0 / jnp.sum(raised, -1, keepdims=True))
        gate_ref[...] = router
        gates = jnp.where(named_experts(routes_ref[...]), router, 0.0).T[:EXTRA]
        high = gates.astype(bf16)
        pay_ref[length:, :length] = high
        pay_ref[length:, length : 2 * length] = (gates - high.astype(f32)).astype(bf16)
        pay_ref[length:, 2 * length :] = jnp.zeros((EXTRA, D - 2 * length), bf16)

    operands = (attended, hidden_own, gain, router_w, routes)
    return call(
        kernel,
        [array((length, D), f32), array((length, 128), f32), array((length + EXTRA, D), bf16)],
        [SCALARS] + [whole(v.shape) for v in operands] + [STAY] * count,
        (offsets, *operands, *pieces),
        scratch=[pltpu.VMEM((QW, D), bf16), pltpu.SemaphoreType.DMA((count,))],
    )


def add_weights(i, steps, lefts, rights, which, chunks, accs, out_refs):
    part = F // chunks
    clear(i, accs)
    for c, acc, out_ref in zip(which, accs, out_refs):
        for p, (left, right) in enumerate(zip(lefts, rights)):
            at = slice(p * part, (p + 1) * part)
            acc[:, at] += dot(left, right[:, c * part : (c + 1) * part], ((0,), (0,)))

        @pl.when(i == steps - 1)
        def _():
            deep = 128

            def rows(r, carry):
                at = pl.ds(pl.multiple_of(r * deep, deep), deep)
                out_ref[at, :] = acc[at, :].astype(bf16)
                return carry

            lax.fori_loop(0, D // deep, rows, 0)


def load_blocks(i, step, row_refs, grad_refs, both_ref, grad_ref, table_ref, sems):
    length, each = row_refs[0].shape[0] - EXTRA, grad_refs[0].shape[0]

    def copies(j, row_ref, block_ref):
        at = pl.ds(pl.multiple_of(j * length, length), length)
        out = [
            pltpu.make_async_copy(row_ref.at[:length, :], both_ref.at[at, :], sems.at[j, 0]),
            pltpu.make_async_copy(block_ref, grad_ref.at[at, :], sems.at[j, 1]),
        ]
        if table_ref is not None:
            out.append(pltpu.make_async_copy(row_ref.at[length:, : 2 * length], table_ref.at[j], sems.at[j, 2]))
        return out

    @pl.when(i == 0)
    def _():
        for j, row_ref in enumerate(row_refs):
            for copy in copies(j, row_ref, grad_refs[j // each].at[j % each]):
                copy.start()

    for b in range(step):
        for copy in copies(i * step + b, row_refs[0], grad_refs[0].at[0]):
            copy.wait()
    at = pl.ds(pl.multiple_of(i * step * length, step * length), step * length)
    return both_ref[at, :], grad_ref[at, :]


def gate_table(pair):
    length = pair.shape[1] // 2
    return pair[:, :length].astype(f32) + pair[:, length:].astype(f32)


def clear(i, accs):
    deep = 128

    @pl.when(i == 0)
    def _():
        def rows(r, carry):
            for acc in accs:
                acc[pl.ds(pl.multiple_of(r * deep, deep), deep), :] = jnp.zeros((deep, acc.shape[1]), f32)
            return carry

        lax.fori_loop(0, D // deep, rows, 0)


def expert(rows, grads, w_gate_up, w_down, index, chunks, which):
    sources, blocks, tall = len(grads), len(rows), rows[0].shape[0]
    length = tall - EXTRA
    step = 2
    turns = grads[0].shape[0] // step
    steps = blocks // step

    def kernel(index_ref, *refs):
        row_refs, grad_refs, refs = refs[:blocks], refs[blocks : blocks + sources], refs[blocks + sources :]
        gate_up_ref, down_ref, dgu_ref, hid_ref, sum_ref = refs[:5]
        out_refs, (both_ref, grad_ref, table_ref, sems, *accs) = refs[5 : 5 + len(which)], refs[5 + len(which) :]
        i = pl.program_id(0)
        both, grad = load_blocks(i, step, row_refs, grad_refs, both_ref, grad_ref, table_ref, sems)
        columns = []
        for b in range(step):
            table = gate_table(table_ref[i * step + b])
            mine = lax.broadcasted_iota(jnp.int32, table.shape, 0) == index_ref[1]
            row = jnp.sum(jnp.where(mine, table, 0.0), 0, keepdims=True)
            columns.append(jnp.broadcast_to(row, (128, length)).T[:, :1])
        gate = jnp.concatenate(columns, 0)
        gate_up = dot(both, gate_up_ref[0])
        gate_part, up_part = gate_up[:, :F], gate_up[:, F:]
        sigmoid_g = jax.nn.sigmoid(gate_part)
        silu_g = gate_part * sigmoid_g
        hidden = silu_g * up_part
        raw = dot(grad, down_ref[0])
        sums = jnp.sum(raw * hidden, 1, keepdims=True)
        gated = (gate * hidden).astype(bf16)
        grad_hidden = gate * raw
        grad_gate = (grad_hidden * up_part * sigmoid_g * (1.0 + gate_part * (1.0 - sigmoid_g))).astype(bf16)
        grad_up = (grad_hidden * silu_g).astype(bf16)
        for b in range(step):
            at = slice(b * length, (b + 1) * length)
            dgu_ref[b, :, :F] = grad_gate[at]
            dgu_ref[b, :, F:] = grad_up[at]
            hid_ref[b] = gated[at]
            sum_ref[b] = jnp.broadcast_to(sums[at], (length, 128)).T[:8]
        add_weights(i, steps, (both, both, grad), (grad_gate, grad_up, gated), which, chunks, accs, out_refs)

    def block(*shape):
        return pl.BlockSpec((step,) + shape, lambda i, index: (i,) + (0,) * len(shape))

    def source_block(source, *shape):
        def at(i, index):
            return (jnp.clip(i - source * turns, 0, turns - 1),) + (0,) * len(shape)

        return pl.BlockSpec((step,) + shape, at)

    def weight(*shape):
        return pl.BlockSpec((1,) + shape, lambda i, index: (index[0], 0, 0))

    shapes = [array((blocks, length, 2 * F), bf16), array((blocks, length, F), bf16), array((blocks, 8, length), f32)]
    scratch = [
        pltpu.VMEM((blocks * length, D), bf16),
        pltpu.VMEM((blocks * length, D), bf16),
        pltpu.VMEM((blocks, EXTRA, 2 * length), bf16),
        pltpu.SemaphoreType.DMA((blocks, 3)),
    ]
    return call(
        kernel,
        shapes + [array((D, 3 * F // chunks), bf16)] * len(which),
        [STAY] * (blocks + sources)
        + [weight(D, 2 * F), weight(D, F)],
        (index, *rows, *grads, w_gate_up, w_down),
        out_specs=[block(length, 2 * F), block(length, F), block(8, length)]
        + [pl.BlockSpec((D, 3 * F // chunks), lambda i, index: (0, 0)) for _ in which],
        scratch=scratch + [pltpu.VMEM((D, 3 * F // chunks), f32)] * len(which),
        grid=(steps,),
        prefetch=1,
    )


def gate_column(table, expert):
    mine = lax.broadcasted_iota(jnp.int32, table.shape, 0) == expert
    row = jnp.sum(jnp.where(mine, table, 0.0), 0, keepdims=True)
    return jnp.broadcast_to(row, (128, table.shape[1])).T[:, :1]


def last_expert(rows, grads, w_gate_up, w_down, indices, earlier, sums):
    sources, blocks, tall = len(grads), len(rows), rows[0].shape[0]
    length = tall - EXTRA
    step = 2
    turns = grads[0].shape[0] // step
    steps = blocks // step
    others = len(earlier)

    def kernel(indices_ref, *refs):
        row_refs, grad_refs, refs = refs[:blocks], refs[blocks : blocks + sources], refs[blocks + sources :]
        gate_up_ref, down_ref, refs = refs[0], refs[1], refs[2:]
        earlier_refs, weight_refs, sum_refs, refs = refs[:others], refs[others : 2 * others], refs[2 * others : 3 * others], refs[3 * others :]
        dgu_ref, hid_ref, out_refs, (both_ref, grad_ref, table_ref, sems) = refs[0], refs[1], refs[2 : 2 + sources], refs[2 + sources :]
        i = pl.program_id(0)
        both, grad = load_blocks(i, step, row_refs, grad_refs, both_ref, grad_ref, table_ref, sems)
        gate = jnp.concatenate([gate_column(gate_table(table_ref[i * step + b]), indices_ref[2 * others + 1]) for b in range(step)], 0)
        gate_up = dot(both, gate_up_ref[0])
        gate_part, up_part = gate_up[:, :F], gate_up[:, F:]
        sigmoid_g = jax.nn.sigmoid(gate_part)
        silu_g = gate_part * sigmoid_g
        hidden = silu_g * up_part
        raw = dot(grad, down_ref[0])
        own = jnp.sum(raw * hidden, 1, keepdims=True)
        gated = (gate * hidden).astype(bf16)
        grad_hidden = gate * raw
        grad_gate = (grad_hidden * up_part * sigmoid_g * (1.0 + gate_part * (1.0 - sigmoid_g))).astype(bf16)
        grad_up = (grad_hidden * silu_g).astype(bf16)
        total = dot(jnp.concatenate([grad_gate, grad_up], 1), gate_up_ref[0], ((1,), (1,)))
        for part_ref, weight_ref in zip(earlier_refs, weight_refs):
            part = jnp.concatenate([part_ref[b] for b in range(step)], 0)
            total = total + dot(part, weight_ref[0], ((1,), (1,)))
        for b in range(step):
            at = slice(b * length, (b + 1) * length)
            dgu_ref[b, :, :F] = grad_gate[at]
            dgu_ref[b, :, F:] = grad_up[at]
            hid_ref[b] = gated[at]
            table = jnp.zeros((EXTRA, length), f32)
            place = lax.broadcasted_iota(jnp.int32, table.shape, 0)
            for e in range(others):
                table = jnp.where(place == indices_ref[2 * e + 1], sum_refs[e][b, :1, :], table)
            row = jnp.broadcast_to(own[at], (length, 128)).T[:1]
            table = jnp.where(place == indices_ref[2 * others + 1], row, table)
            high = table.astype(bf16)
            for source, out_ref in enumerate(out_refs):

                @pl.when((i >= source * turns) & (i < (source + 1) * turns))
                def _():
                    out_ref[b, :length, :] = total[at].astype(bf16)
                    out_ref[b, length:, :length] = high
                    out_ref[b, length:, length : 2 * length] = (table - high.astype(f32)).astype(bf16)
                    out_ref[b, length:, 2 * length :] = jnp.zeros((EXTRA, D - 2 * length), bf16)

    def block(*shape):
        return pl.BlockSpec((step,) + shape, lambda i, index: (i,) + (0,) * len(shape))

    def source_block(source, *shape):
        def at(i, index):
            return (jnp.clip(i - source * turns, 0, turns - 1),) + (0,) * len(shape)

        return pl.BlockSpec((step,) + shape, at)

    def weight(e, *shape):
        return pl.BlockSpec((1,) + shape, lambda i, index: (index[2 * e], 0, 0))

    return call(
        kernel,
        [array((blocks, length, 2 * F), bf16), array((blocks, length, F), bf16)]
        + [array((blocks // sources, tall, D), bf16)] * sources,
        [STAY] * (blocks + sources)
        + [weight(others, D, 2 * F), weight(others, D, F)]
        + [block(length, 2 * F)] * others
        + [weight(e, D, 2 * F) for e in range(others)]
        + [block(8, length)] * others,
        (indices, *rows, *grads, w_gate_up, w_down, *earlier, *[w_gate_up] * others, *sums),
        out_specs=[block(length, 2 * F), block(length, F)] + [source_block(s, tall, D) for s in range(sources)],
        scratch=[
            pltpu.VMEM((blocks * length, D), bf16),
            pltpu.VMEM((blocks * length, D), bf16),
            pltpu.VMEM((blocks, EXTRA, 2 * length), bf16),
            pltpu.SemaphoreType.DMA((blocks, 3)),
        ],
        grid=(steps,),
        prefetch=1,
    )


def weight_grads(rows, grads, grad_gate_up, hidden, chunks, which, after):
    sources, blocks, tall = len(grads), len(rows), rows[0].shape[0]
    length = tall - EXTRA
    step = 2
    turns = grads[0].shape[0] // step
    steps = blocks // step

    def kernel(after_ref, *refs):
        row_refs, grad_refs, refs = refs[:blocks], refs[blocks : blocks + sources], refs[blocks + sources :]
        dgu_ref, hid_ref, out_refs = refs[0], refs[1], refs[2 : 2 + len(which)]
        both_ref, grad_ref, sems, *accs = refs[2 + len(which) :]
        i = pl.program_id(0)
        both, grad = load_blocks(i, step, row_refs, grad_refs, both_ref, grad_ref, None, sems)
        grad_gate = jnp.concatenate([dgu_ref[b, :, :F] for b in range(step)], 0)
        grad_up = jnp.concatenate([dgu_ref[b, :, F:] for b in range(step)], 0)
        gated = jnp.concatenate([hid_ref[b] for b in range(step)], 0)
        add_weights(i, steps, (both, both, grad), (grad_gate, grad_up, gated), which, chunks, accs, out_refs)

    def block(*shape):
        return pl.BlockSpec((step,) + shape, lambda i, after: (i,) + (0,) * len(shape))

    def source_block(source, *shape):
        def at(i, after):
            return (jnp.clip(i - source * turns, 0, turns - 1),) + (0,) * len(shape)

        return pl.BlockSpec((step,) + shape, at)

    return call(
        kernel,
        [array((D, 3 * F // chunks), bf16)] * len(which),
        [STAY] * (blocks + sources)
        + [block(length, 2 * F), block(length, F)],
        (after, *rows, *grads, grad_gate_up, hidden),
        out_specs=[pl.BlockSpec((D, 3 * F // chunks), lambda i, after: (0, 0)) for _ in which],
        scratch=[pltpu.VMEM((blocks * length, D), bf16)] * 2
        + [pltpu.SemaphoreType.DMA((blocks, 3))]
        + [pltpu.VMEM((D, 3 * F // chunks), f32)] * len(which),
        grid=(steps,),
        prefetch=1,
    )


def row_terms(parts, weights, indices, sources):
    blocks, length, width = parts[0].shape
    count = len(parts)
    step = 2
    turns = blocks // step // sources

    def kernel(indices_ref, *refs):
        part_refs, weight_refs, out_refs = refs[:count], refs[count : 2 * count], refs[2 * count :]
        i = pl.program_id(0)
        total = None
        for part_ref, weight_ref in zip(part_refs, weight_refs):
            term = dot(jnp.concatenate([part_ref[b] for b in range(step)], 0), weight_ref[0], ((1,), (1,)))
            total = term if total is None else total + term
        for source, out_ref in enumerate(out_refs):

            @pl.when((i >= source * turns) & (i < (source + 1) * turns))
            def _():
                for b in range(step):
                    out_ref[b] = total[b * length : (b + 1) * length].astype(bf16)

    def weight(e):
        return pl.BlockSpec((1,) + weights.shape[1:], lambda i, index: (index[2 * e], 0, 0))

    def source_block(source):
        return pl.BlockSpec((step, length, D), lambda i, index: (jnp.clip(i - source * turns, 0, turns - 1), 0, 0))

    return call(
        kernel,
        [array((blocks // sources, length, D), bf16)] * sources,
        [pl.BlockSpec((step, length, width), lambda i, index: (i, 0, 0))] * count + [weight(e) for e in range(count)],
        (indices, *parts, *[weights] * count),
        out_specs=[source_block(s) for s in range(sources)],
        grid=(blocks // step,),
        prefetch=1,
    )


def backward(
    returned, residual, router, routes, cotangent, gain, router_w, query, kv, lse, cosines, sines, inputs,
    hidden_prev, hidden_own, attended, out_pieces, out_offsets, qkv_pieces, qkv_offsets, flag, core, shards, cores,
):
    length, terms = residual.shape[0], len(returned)
    width = QW + 2 * KVW
    out_count, qkv_count = len(out_pieces), len(qkv_pieces)

    deep = D // (shards * cores)

    def kernel(out_offsets_ref, qkv_offsets_ref, flag_ref, core_ref, *rest):
        term_refs, rest = rest[:terms], rest[terms:]
        res_ref, gate_ref, routes_ref, cot_ref, gain_ref, router_ref, q_ref, kv_ref, lse_ref, cos_ref, sin_ref = rest[:11]
        in_ref, prev_ref, own_ref, att_ref, rest = *rest[11:15], rest[15:]
        out_refs, qkv_refs, rest = rest[:out_count], rest[out_count : out_count + qkv_count], rest[out_count + qkv_count :]
        gres_ref, gown_ref, gprev_ref, own_grad_ref = rest[:4]
        far_refs, rest = rest[4 : 4 + 3 * (cores - 1)], rest[4 + 3 * (cores - 1) :]
        w_out, w_qkv, gatt_ref, dq_ref, dkv_ref, small_ref, sum_ref, out_sems, qkv_sems, end_sems = rest
        out_copies = load_rows(out_refs, out_offsets_ref, w_out, out_sems)
        qkv_copies = load_rows(qkv_refs, qkv_offsets_ref, w_qkv, qkv_sems)
        total = term_refs[0][...].astype(f32)
        for ref in term_refs[1:]:
            total = total + ref[...].astype(f32)
        table = total[length:, :length] + total[length:, length : 2 * length]
        gate_grads = jnp.concatenate([table, jnp.zeros((128 - EXTRA, length), f32)], 0).T
        grad_router = jnp.where(named_experts(routes_ref[...]), gate_grads, 0.0)
        router = gate_ref[...]
        grad_logits = (router * (grad_router - jnp.sum(router * grad_router, -1, keepdims=True))).astype(bf16)
        grad_input = total[:length] + dot(grad_logits, router_ref[...])
        normed, inverse = normalize(res_ref[...])
        gain_row = gain_ref[...]
        rows = (normed * gain_row).astype(bf16)
        small = dot(rows, grad_logits, ((0,), (0,)))
        gain_grad = jnp.sum(grad_input * normed, 0, keepdims=True)
        small_ref[...] = jnp.where(lanes((D, 128)) == EXPERTS, jnp.broadcast_to(gain_grad, (128, D)).T, small)
        grad_residual = cot_ref[...].astype(f32) + norm_back(normed, inverse, grad_input * gain_row)
        gres_ref[...] = grad_residual
        grad_attn = grad_residual.astype(bf16)
        for copy in out_copies:
            copy.wait()
        gatt_ref[...] = dot(grad_attn, w_out[...], ((1,), (1,))).astype(bf16)

        def write(at, values):
            sum_ref[:, at : at + values.shape[1]] = values.astype(bf16)

        write(width, dot(att_ref[...], grad_attn, ((0,), (0,))))

        bias = jnp.where((lanes((1, 2 * length)) >= length) | (flag_ref[0] > 0), 0.0, masked_score)
        cos_own, sin_own = cos_ref[length:, :], sin_ref[length:, :]

        def back(values, cos, sin):
            return (values * cos - halves(values) * sin).astype(bf16)

        def pair_of_keys(jj, carry):
            at = pl.multiple_of(jj * PAIR, PAIR)
            keys = kv_ref[:, pl.ds(at, PAIR)].astype(f32)
            vals = kv_ref[:, pl.ds(KVW + at, PAIR)].astype(f32)
            key_grads, val_grads = [], []
            for t in range(2):
                place = pl.multiple_of((2 * jj + t) * PAIR, PAIR)
                both = (two_rows(q_ref[:, pl.ds(place, PAIR)].astype(f32)) * score_scale).astype(bf16)
                outs = two_rows(gatt_ref[:, pl.ds(place, PAIR)].astype(f32)).astype(bf16)
                key = doubled(keys, t).astype(bf16)
                val = doubled(vals, t).astype(bf16)
                own = lanes(lse_ref.shape) == 2 * jj + t
                log_total = jnp.sum(jnp.where(own, lse_ref[...], 0.0), -1, keepdims=True)
                scores = dot(both, key, ((1,), (1,))) + bias
                probs = jnp.exp(scores - log_total)
                grad_probs = dot(outs, val, ((1,), (1,)))
                inner = jnp.sum(probs * grad_probs, -1, keepdims=True)
                grad_scores = (probs * (grad_probs - inner)).astype(bf16)
                grad_query = dot(grad_scores, key) * score_scale
                low = lanes((length, PAIR)) < HEAD_DIM
                grad_query = jnp.where(low, grad_query[:length], grad_query[length:])
                dq_ref[:, pl.ds(place, PAIR)] = back(grad_query, cos_own, sin_own)
                key_grad = dot(grad_scores, both, ((0,), (0,)))
                val_grad = dot(probs.astype(bf16), outs, ((0,), (0,)))
                key_grads.append(key_grad + pltpu.roll(key_grad, HEAD_DIM, 1))
                val_grads.append(val_grad + pltpu.roll(val_grad, HEAD_DIM, 1))
            low = lanes((2 * length, PAIR)) < HEAD_DIM
            dkv_ref[:, pl.ds(at, PAIR)] = back(jnp.where(low, *key_grads), cos_ref[...], sin_ref[...])
            dkv_ref[:, pl.ds(KVW + at, PAIR)] = jnp.where(low, *val_grads).astype(bf16)
            return carry

        lax.fori_loop(0, KVW // PAIR, pair_of_keys, 0)
        write(0, dot(in_ref[length:, :], dq_ref[...], ((0,), (0,))))
        write(QW, dot(in_ref[...], dkv_ref[...], ((0,), (0,))))
        for copy in qkv_copies:
            copy.wait()
        from_kv = dot(dkv_ref[...], w_qkv[:, QW:], ((1,), (1,)))
        own = from_kv[length:] + dot(dq_ref[...], w_qkv[:, :QW], ((1,), (1,)))
        gown_ref[...] = own
        gprev_ref[...] = from_kv[:length].astype(bf16)
        normed_own, _ = normalize(own_ref[...].astype(f32))
        normed_prev, _ = normalize(prev_ref[...].astype(f32))
        gain_grad = jnp.sum(own * normed_own + from_kv[:length] * normed_prev, 0, keepdims=True)
        column = jnp.broadcast_to(gain_grad, (128, D)).T
        write(width + D, jnp.where(lanes((D, 128)) == EXPERTS + 1, column, small_ref[...]))
        copies = []
        for s in range(shards):
            for j in range(cores):
                at = pl.multiple_of((s * cores + (core_ref[0] + j) % cores) * deep, 16)
                targets = [(own_grad_ref, 0)] if j == 0 else [(far_refs[3 * (j - 1) + g], g * D) for g in range(3)]
                for g, (target, start) in enumerate(targets):
                    source = sum_ref.at[pl.ds(at, deep), start : start + target.shape[2]]
                    copy = pltpu.make_async_copy(source, target.at[s], end_sems.at[s, j, g])
                    copy.start()
                    copies.append(copy)
        for copy in copies:
            copy.wait()

    operands = (
        *returned, residual, router, routes, cotangent, gain, router_w, query, kv, lse, cosines, sines, inputs,
        hidden_prev, hidden_own, attended,
    )
    return call(
        kernel,
        [
            array((length, D), f32),
            array((length, D), f32),
            array((length, D), bf16),
        ]
        + [array((shards, deep, width + D + 128), bf16)]
        + [array((shards, deep, w), bf16) for w in (D, D, D + 128)] * (cores - 1),
        [SCALARS] * 4 + [whole(v.shape) for v in operands] + [STAY] * (out_count + qkv_count),
        (out_offsets, qkv_offsets, flag, core, *operands, *out_pieces, *qkv_pieces),
        out_specs=[whole((length, D)), whole((length, D)), whole((length, D))] + [STAY] * (1 + 3 * (cores - 1)),
        scratch=[
            pltpu.VMEM((QW, D), bf16),
            pltpu.VMEM((D, width), bf16),
            pltpu.VMEM((length, QW), bf16),
            pltpu.VMEM((length, QW), bf16),
            pltpu.VMEM((2 * length, 2 * KVW), bf16),
            pltpu.VMEM((D, 128), f32),
            pltpu.VMEM((D, width + D + 128), bf16),
            pltpu.SemaphoreType.DMA((out_count,)),
            pltpu.SemaphoreType.DMA((qkv_count,)),
            pltpu.SemaphoreType.DMA((shards, cores, 3)),
        ],
    )


def first_back(grad_sum, grad_residual, hidden_own, gain):
    def kernel(sum_ref, res_ref, hid_ref, gain_ref, out_ref):
        deep = 32

        def rows(r, carry):
            at = pl.ds(pl.multiple_of(r * deep, deep), deep)
            normed, inverse = normalize(hid_ref[at, :].astype(f32))
            out_ref[at, :] = res_ref[at, :] + norm_back(normed, inverse, sum_ref[at, :] * gain_ref[...])
            return carry

        lax.fori_loop(0, out_ref.shape[0] // deep, rows, 0)

    operands = (grad_sum, grad_residual, hidden_own, gain)
    return call(kernel, [array(grad_sum.shape, f32)], [whole(v.shape) for v in operands], operands, vmem=16 * 1024 * 1024)[0]


def place(sources, experts, outs, shapes, chunk, chunks):
    part = F // chunks
    count = sum(source.shape[0] for source in sources)

    def kernel(experts_ref, *refs):
        source_refs = refs[: len(sources)]
        gate_up_ref, down_ref, wide, sems = refs[len(sources) + len(outs) :]
        copies = []
        deep = 128
        values = [ref.at[i] for ref in source_refs for i in range(ref.shape[0])]
        for i, source in enumerate(values):

            def rows(r, carry):
                at = pl.ds(pl.multiple_of(r * deep, deep), deep)
                wide[i, at, :] = source[at, :].astype(f32)
                return carry

            lax.fori_loop(0, D // deep, rows, 0)
            for p, target in enumerate(
                (
                    gate_up_ref.at[experts_ref[i], :, chunk * part : (chunk + 1) * part],
                    gate_up_ref.at[experts_ref[i], :, F + chunk * part : F + (chunk + 1) * part],
                    down_ref.at[experts_ref[i], :, chunk * part : (chunk + 1) * part],
                )
            ):
                copy = pltpu.make_async_copy(wide.at[i, :, p * part : (p + 1) * part], target, sems.at[i, p])
                copy.start()
                copies.append(copy)
        for copy in copies:
            copy.wait()

    return call(
        kernel,
        shapes,
        [SCALARS] + [whole(v.shape) for v in sources] + [STAY] * len(outs),
        (experts, *sources, *outs),
        out_specs=[STAY, STAY],
        scratch=[pltpu.VMEM((count, D, 3 * part), f32), pltpu.SemaphoreType.DMA((count, 3))],
        aliases={1 + len(sources) + i: i for i in range(len(outs))},
        vmem=28 * 1024 * 1024,
    )


def unpack(sources, offsets, rows):
    count = sum(source.shape[0] for source in sources)
    deep, wide = sources[0].shape[1:]
    widths = (QW + 2 * KVW, D)

    def kernel(offsets_ref, *refs):
        source_refs, refs = refs[: len(sources)], refs[len(sources) :]
        out_refs, router_ref, ffn_ref, attn_ref, values_ref, rest_ref, sems = refs[:2], *refs[2:]
        copies = []
        for i, source in enumerate([ref.at[i] for ref in source_refs for i in range(ref.shape[0])]):
            some = 32

            def rows_of(r, carry):
                place = pl.ds(pl.multiple_of(r * some, some), some)
                values_ref[i, place, :] = source[place, :].astype(f32)
                return carry

            lax.fori_loop(0, deep // some, rows_of, 0)
            at = pl.multiple_of(offsets_ref[i], 8)
            start = 0
            for p, (out_ref, width) in enumerate(zip(out_refs, widths)):
                copy = pltpu.make_async_copy(values_ref.at[i, :, start : start + width], out_ref.at[pl.ds(at, deep), :], sems.at[i, p])
                copy.start()
                copies.append(copy)
                start += width
            rest_ref[pl.ds(at, deep), :] = values_ref[i, :, start:]
        router_ref[...] = rest_ref[:, :EXPERTS]
        turned = rest_ref[...].T
        ffn_ref[...] = turned[EXPERTS : EXPERTS + 1]
        attn_ref[...] = turned[EXPERTS + 1 : EXPERTS + 2]
        for copy in copies:
            copy.wait()

    return call(
        kernel,
        [array((rows, width), f32) for width in widths] + [array((rows, EXPERTS), f32)] + [array((1, rows), f32)] * 2,
        [SCALARS] + [whole(v.shape) for v in sources],
        (offsets, *sources),
        out_specs=[STAY] * 2 + [whole((rows, EXPERTS))] + [whole((1, rows))] * 2,
        scratch=[
            pltpu.VMEM((count, deep, wide), f32),
            pltpu.VMEM((rows, wide - sum(widths)), f32),
            pltpu.SemaphoreType.DMA((count, 2)),
        ],
    )


def post(function, flags, arrays, outs, parts=8):
    def kernel(flags_ref, *refs):
        ins, results = refs[: len(arrays)], refs[len(arrays) :]
        scalars = [flags_ref[i] for i in range(flags.shape[0])]

        def part_of(ref, r):
            deep = ref.shape[-2] // parts
            return (slice(None),) * (len(ref.shape) - 2) + (pl.ds(pl.multiple_of(r * deep, deep), deep), slice(None))

        def rows(r, carry):
            values = function(scalars, *[ref[part_of(ref, r)] for ref in ins])
            for ref, value in zip(results, values):
                if isinstance(value, tuple):
                    value = jnp.stack(value)
                ref[part_of(ref, r)] = value.astype(ref.dtype)
            return carry

        lax.fori_loop(0, parts, rows, 0)

    near = pl.BlockSpec(memory_space=pltpu.VMEM)
    return pl.pallas_call(
        kernel,
        out_shape=list(outs),
        in_specs=[SCALARS] + [near] * len(arrays),
        out_specs=[near] * len(outs),
        compiler_params=pltpu.CompilerParams(vmem_limit_bytes=POST_VMEM),
        cost_estimate=pl.CostEstimate(flops=0, transcendentals=0, bytes_accessed=0),
    )(flags, *arrays)


def tie(values, after):
    return lax.optimization_barrier((values, after))[0]


def doubling_sum(value, axis):
    count, step = lax.axis_size(axis), 1
    if count & (count - 1):
        return lax.psum(value, axis)
    while step < count:
        value = value + lax.ppermute(value, axis, [(i, i ^ step) for i in range(count)])
        step *= 2
    return value


def body(
    hidden_in, routes, w_qkv, w_out, w_router, attn_gain, ffn_gain, w_gate_up, w_down, cotangent
):
    line, shards = lax.axis_size("line"), lax.axis_size("fsdp")
    side, cores = lax.axis_size("side"), lax.axis_size("core")
    shard, side_at, core_at = lax.axis_index("fsdp"), lax.axis_index("side"), lax.axis_index("core")
    length = hidden_in.shape[0]
    near = [(a, s) for s in range(shards) for a in range(side)]
    local_experts = w_gate_up.shape[0]
    count = local_experts // (side * cores)
    barrier = lax.optimization_barrier

    def other_core(value, core=1):
        return turn(value, "core", (core,), (cores,))

    def other_side(value, step=1):
        return turn(value, "side", (step,), (side,))

    def from_shard(part, step):
        return turn(part, "fsdp", (step,), (shards,))

    def fetch_start(piece, sides):
        part = own_part(piece, 0, core_at * sides + side_at % sides, cores * sides)
        return [from_shard(part, step) for step in range(1, shards)]

    def fetch_end(piece, first, sides):
        rows = piece.shape[0]
        out, offsets = [piece], [shard * rows]
        for step, part in enumerate(first, 1):
            base = (shard - step) % shards * rows
            for a in range(sides):
                theirs = other_side(part, a) if a else part
                for core in range(cores):
                    out.append(other_core(theirs, core) if core else theirs)
                    at = (core_at - core) % cores * sides + (side_at - a) % sides
                    offsets.append(base + at * part.shape[0])
        return out, jnp.stack(offsets).astype(jnp.int32)

    def over_cores(first):
        return [other_core(first, core) if core else first for core in range(cores)]

    def far_blocks(blocks):
        return [other_core(blocks[core * len(near) : (core + 1) * len(near)], -core % cores) for core in range(1, cores)]

    def add_up(first, others):
        for other in others:
            first = first + other
        return first

    def send_back(total):
        out = [total[0]]
        for i, (a, s) in enumerate(near):
            if (a, s) != (0, 0):
                out.append(turn(total[i], ("side", "fsdp"), (-a % side, -s % shards), (side, shards)))
        return out

    parity = shard % 2
    flag = parity.astype(jnp.int32)[None]
    later = [(i, i + 1) for i in range(0, shards, 2)]
    before = [(i + 1, i) for i in range(0, shards, 2)]

    small_rows = w_router.shape[0]
    small = jnp.concatenate([w_router.T, attn_gain[None], ffn_gain[None]], 0)
    qkv_first = fetch_start(w_qkv, side)
    hidden_prev = lax.ppermute(hidden_in, "fsdp", later)
    full_small = jnp.zeros((EXPERTS + 2, D), bf16)
    for step in range(shards):
        theirs = from_shard(small, step) if step else small
        full_small = lax.dynamic_update_slice_in_dim(full_small, theirs, (shard - step) % shards * small_rows, 1)
    gain_attn = full_small[EXPERTS : EXPERTS + 1].astype(f32)
    gain_ffn = full_small[EXPERTS + 1 :].astype(f32)
    router_w = jnp.pad(full_small[:EXPERTS], ((0, 128 - EXPERTS), (0, 0)))
    sideways = [other_side(cotangent, a) for a in range(1, side)]
    across = [from_shard(cotangent, s) for s in range(1, shards)]
    rows_at = jnp.arange(length, dtype=jnp.int32)
    cosines, sines = rotary_tables(jnp.concatenate([rows_at, parity * length + rows_at]))
    qkv_pieces, qkv_offsets = fetch_end(w_qkv, qkv_first, side)
    out_first = fetch_start(tie(w_out, (hidden_prev, qkv_first)), 1)

    across, hidden_prev = barrier((across, hidden_prev))
    corners = [[other_side(v, a) for a in range(1, side)] for v in across]
    queries, kv, inputs = project(hidden_prev, hidden_in, gain_attn, cosines, sines, qkv_pieces, qkv_offsets)
    out_first, queries, kv = barrier((out_first, queries, kv))
    out_pieces, out_offsets = fetch_end(w_out, out_first, 1)
    attended, lse = attend(queries, kv, flag)
    grads_near = [cotangent] + sideways + [v for first, rest in zip(across, corners) for v in [first] + rest]
    grads_near = jnp.stack(tie(grads_near, attended))
    out_pieces, attended, grads_near = barrier((out_pieces, attended, grads_near))
    grads_near = over_cores(grads_near)
    residual, router, payload = enter_experts(attended, hidden_in, gain_ffn, router_w, routes, out_pieces, out_offsets)
    rows_near = [turn(payload, ("side", "fsdp"), (a, s), (side, shards)) if (a, s) != (0, 0) else payload for a, s in near]
    rows_near = rows_near + [other_core(v, core) for core in range(1, cores) for v in rows_near]

    clock = []

    def run(function, *inputs):
        if clock:
            inputs = barrier((inputs, tuple(clock)))[0]
        out = function(*inputs)
        clock[:] = jax.tree.leaves(out)
        return out

    mine_at = (side_at * cores + core_at) * count
    indices = [jnp.stack([mine_at + e, shard * local_experts + mine_at + e]).astype(jnp.int32) for e in range(count)]
    both = jnp.concatenate(indices)
    order = jnp.stack([((side_at - a) % side * cores + (core_at - core) % cores) for core in range(cores) for a in range(side)])
    order = order.astype(jnp.int32) * count
    shapes = [array((local_experts, D, 2 * F), f32), array((local_experts, D, F), f32)]
    place_at = lax.axis_index("line")
    end = (place_at == 0) | (place_at == line - 1)

    def go_in(raw):
        return lax.ppermute(raw, "line", [(0, 1), (3, 2)])

    def cross(half):
        return lax.ppermute(half, "line", [(1, 2), (2, 1)])

    def in_and_out(sent):
        return lax.ppermute(sent, "line", [(0, 1), (1, 0), (2, 3), (3, 2)])

    def go_out(total):
        return lax.ppermute(total, "line", [(1, 0), (2, 3)])

    def chosen(got, kept):
        return jnp.where(end, got, kept)

    def sides(full):
        return [other_side(full, a) for a in range(1, side)]

    def core_swaps(pair):
        return [other_core(pair, core) for core in range(1, cores)]

    def stacked(full, others):
        return jnp.stack([full] + others)

    def plus(first, second):
        return first + second

    def split(blocks):
        return [blocks[core * len(near) : (core + 1) * len(near)] for core in range(cores)]

    def near_sums(first, others):
        total = add_up(first, others)
        return [total[i] for i in range(len(near))]

    def placed(pair, swaps, outs, e, c):
        return place([pair] + swaps, order + e, outs, shapes, c, CHUNKS)

    def back(terms):
        return backward(
            terms, residual, router, routes, cotangent, gain_ffn, router_w, queries, kv, lse, cosines, sines, inputs, hidden_prev,
            hidden_in, attended, out_pieces, out_offsets, qkv_pieces, qkv_offsets, flag, core_at.astype(jnp.int32)[None], shards, cores,
        )

    def by_shard(total):
        return total[0] if shards == 1 else own_part(total, 0, shard, shards)[0], [
            own_part(total, 0, (shard + step) % shards, shards)[0] for step in range(1, shards)
        ]

    def by_side(total):
        return own_part(total, 0, side_at, side), [own_part(total, 0, (side_at + a) % side, side) for a in range(1, side)]

    def by_step(total):
        return [total[s * side : (s + 1) * side] for s in range(shards)]

    def by_near(total):
        return total[0], [total[a] for a in range(1, side)]

    def swap_lines(value, step):
        return lax.ppermute(value, "line", [(i, i ^ step) for i in range(line)])

    flags = jnp.stack([end, shard > 0, side_at > 0]).astype(jnp.int32)

    def f(value):
        return value.astype(f32)

    def pick(flag, got, kept):
        return jnp.where(flag > 0, f(got), f(kept))

    def steps(function, outs, *arrays):
        outs = [v if isinstance(v, jax.ShapeDtypeStruct) else array(v, bf16) for v in outs]
        return run(lambda *v: tuple(post(function, flags, v, outs)), *arrays)

    if (line, side, cores, shards, count) != (4, 2, 2, 2, 2):
        grads_gu, hiddens, sums, chunks = [], [], [], []
        for e in range(count - 1):
            grad_gu, hidden, total, *parts = expert(rows_near, grads_near, w_gate_up, w_down, indices[e], CHUNKS, range(CHUNKS))
            grads_gu.append(grad_gu)
            hiddens.append(hidden)
            sums.append(total)
            chunks.append(parts)
        grad_gu, hidden, *blocks = last_expert(rows_near, grads_near, w_gate_up, w_down, both, grads_gu, sums)
        hiddens.append(hidden)
        chunks.append(weight_grads(rows_near, grads_near, grad_gu, hidden, CHUNKS, range(CHUNKS), both))
        terms = row_terms(hiddens, w_down, both, cores)
        returned = send_back([v for v in add_up(blocks[0], [other_core(g, -c % cores) for c, g in enumerate(blocks[1:], 1)])])
        mixed = send_back([v for v in add_up(terms[0], [other_core(g, -c % cores) for c, g in enumerate(terms[1:], 1)])])
        grad_residual, grad_own, grad_prev, own_w, *other_w = back(returned)
        joined = [jnp.concatenate(other_w[i : i + 3], -1) for i in range(0, len(other_w), 3)]
        own_w = add_up(own_w, [other_core(w, core) for core, w in enumerate(joined, 1)])
        own_w, other_w = by_shard(own_w)
        own_w = add_up(own_w, [from_shard(w, step) for step, w in enumerate(other_w, 1)])
        own_w = add_up(own_w, [other_side(own_w, a) for a in range(1, side)])

        def line_sum(value):
            if line & (line - 1):
                return lax.psum(value, "line")
            for bit in range(line.bit_length() - 1):
                value = value + swap_lines(value, 1 << bit)
            return value

        sum_w, outs = line_sum(own_w), ()
        for e, parts in enumerate(chunks):
            for c, part in enumerate(parts):
                full = line_sum(part)
                pair = jnp.stack([full] + sides(full))
                outs = placed(pair, core_swaps(pair), outs, e, c)
        at_w = jnp.stack([(core_at - core) % cores for core in range(cores)]).astype(jnp.int32) * sum_w.shape[0]
        qkv_sum, out_sum, router_sum, ffn_sum, attn_sum = unpack(
            [w[None] for w in [sum_w] + core_swaps(sum_w)], at_w, sum_w.shape[0] * cores
        )
        grad_sum = grad_own + lax.ppermute(grad_prev, "fsdp", before).astype(f32)
        grad_in = first_back(grad_sum, grad_residual, hidden_in, gain_attn)
        layer_out = add_up(residual, [m.astype(f32) for m in mixed]).astype(bf16)
        return (
            layer_out, grad_in, qkv_sum, out_sum, router_sum, attn_sum[0], ffn_sum[0], outs[0], outs[1],
        )

    gu_0, hid_0, sum_0, *parts_0 = run(lambda i: expert(rows_near, grads_near, w_gate_up, w_down, i, CHUNKS, (0,)), indices[0])
    chunk = parts_0[0].shape
    two = (2,) + chunk
    in_0 = go_in(parts_0[0])
    parts_0 += run(lambda i: weight_grads(rows_near, grads_near, gu_0, hid_0, CHUNKS, (1,), i), both)
    gu_1, hid_1, first_half, other_half = run(
        lambda i: last_expert(rows_near, grads_near, w_gate_up, w_down, i, [gu_0], [sum_0]), both
    )
    far = [other_core(other_half)]
    (half_0,) = steps(lambda flag, raw, got: (f(raw) + f(got),), [chunk], parts_0[0], in_0)
    middle_0, in_1 = cross(half_0), go_in(parts_0[1])
    tall = first_half.shape[1]

    def block_sums(flag, first, other):
        total = f(first) + f(other)
        return tuple(total[i] for i in range(len(near)))

    blocks = run(
        lambda first, other: post(lambda *v: block_sums(*v), flags, (first, other), [array((tall, D), bf16)] * len(near), tall // 16),
        first_half, far[0],
    )
    returned = send_back(blocks)
    mixed, mixed_other = run(lambda i: row_terms([hid_0, hid_1], w_down, i, cores), both)
    parts_1 = run(lambda i: weight_grads(rows_near, grads_near, gu_1, hid_1, CHUNKS, range(CHUNKS), i), both)

    def step_1(flag, half, middle, own, got, raw):
        total = f(half) + f(middle)
        return total, f(own) + f(got), pick(flag[0], raw, total)

    total_0, half_1, sent_2 = steps(step_1, [chunk] * 3, half_0, middle_0, parts_0[1], in_1, parts_1[0])
    both_2, middle_1 = in_and_out(sent_2), cross(half_1)
    grad_residual, grad_own, grad_prev, own_w, *other_w = run(back, returned)
    far_w = [other_core(w) for w in other_w]
    deep, wide = own_w.shape[1:]

    def step_2(flag, own, got, total, half, middle, raw, w, *far):
        summed = f(half) + f(middle)
        joined = f(w) + jnp.concatenate([f(v) for v in far], -1)
        mine, theirs = pick(flag[1], joined[1], joined[0]), pick(flag[1], joined[0], joined[1])
        return f(own) + f(got), pick(flag[0], got, total), summed, pick(flag[0], raw, summed), mine, theirs

    half_2, full_0, total_1, sent_3, own_w, other_w = steps(
        step_2, [chunk] * 4 + [(deep, wide)] * 2,
        parts_1[0], both_2, total_0, half_1, middle_1, parts_1[1], own_w, *far_w,
    )
    side_0, middle_2, both_3 = other_side(full_0), cross(half_2), in_and_out(sent_3)
    far_w, far_m = from_shard(other_w, 1), other_core(mixed_other)

    def step_3(flag, own, got, total, half, middle, first, other, w, far, m, m_far):
        terms = f(m) + f(m_far)
        return (
            f(own) + f(got), pick(flag[0], got, total), f(half) + f(middle), (first, other), f(w) + f(far), terms[:2], terms[2:],
        )

    rows_of = mixed.shape[1]
    half_3, full_1, total_2, pair_0, own_w, own_m, other_m = steps(
        step_3, [chunk] * 3 + [two, (deep, wide)] + [(2, rows_of, D)] * 2,
        parts_1[1], both_3, total_1, half_2, middle_2, full_0, side_0, own_w, far_w, mixed, far_m,
    )
    side_1, middle_3, out_2, core_0 = other_side(full_1), cross(half_3), go_out(total_2), other_core(pair_0)
    in_w = go_in(own_w)

    def step_4(flag, got, total, half, middle, first, other, w, far):
        return pick(flag[0], got, total), f(half) + f(middle), (first, other), f(w) + f(far)

    full_2, total_3, pair_1, half_w = steps(
        step_4, [chunk] * 2 + [two, (deep, wide)], out_2, total_2, half_3, middle_3, full_1, side_1, own_w, in_w
    )
    side_2, out_3, middle_w, core_1 = other_side(full_2), go_out(total_3), cross(half_w), other_core(pair_1)
    far_m = from_shard(other_m, 1)
    outs = run(lambda pair, swap: placed(pair, [swap], (), 0, 0), pair_0, core_0)

    def step_5(flag, got, total, first, other, w, far, m, m_far):
        terms = f(m) + f(m_far)
        return pick(flag[0], got, total), (first, other), f(w) + f(far), terms[0], terms[1]

    full_3, pair_2, total_w, own_m, other_m = steps(
        step_5, [chunk, two, (deep, wide)] + [(rows_of, D)] * 2, out_3, total_3, full_2, side_2, half_w, middle_w, own_m, far_m
    )
    side_3, out_w, core_2 = other_side(full_3), go_out(total_w), other_core(pair_2)
    far_m = other_side(other_m)
    grad_later = lax.ppermute(grad_prev, "fsdp", before)
    outs = run(lambda pair, swap, outs: placed(pair, [swap], outs, 0, 1), pair_1, core_1, outs)

    def step_6(flag, first, other, got, w, rest, m, m_far, own, back):
        return (first, other), pick(flag[0], got, w), rest + f(m) + f(m_far), own + f(back)

    pair_3, full_w, layer_out, grad_sum = steps(
        step_6, [two, (deep, wide), (rows_of, D), array((rows_of, D), f32)],
        full_3, side_3, out_w, total_w, residual, own_m, far_m, grad_own, grad_later,
    )
    core_3, side_w = other_core(pair_3), other_side(full_w)
    grad_in = run(lambda grad: first_back(grad, grad_residual, hidden_in, gain_attn), grad_sum)
    outs = run(lambda pair, swap, outs: placed(pair, [swap], outs, 1, 0), pair_2, core_2, outs)
    outs = run(lambda pair, swap, outs: placed(pair, [swap], outs, 1, 1), pair_3, core_3, outs)
    (sum_w,) = steps(lambda flag, w, far: (f(w) + f(far),), [(deep, wide)], full_w, side_w)
    core_w = other_core(sum_w)
    at_w = jnp.stack([(core_at - core) % cores for core in range(cores)]).astype(jnp.int32) * deep
    qkv_sum, out_sum, router_sum, ffn_sum, attn_sum = run(lambda *v: unpack([w[None] for w in v], at_w, deep * cores), sum_w, core_w)
    return (
        layer_out,
        grad_in,
        qkv_sum,
        out_sum,
        router_sum,
        attn_sum[0],
        ffn_sum[0],
        outs[0],
        outs[1],
    )


def solution(mesh):
    copies, shards = mesh.shape["rep"], mesh.shape["fsdp"]
    local = EXPERTS // shards
    cores = 2 if copies % 2 == 0 and local % 2 == 0 else 1
    side = 2 if cores == 2 and copies % 4 == 0 and local % 4 == 0 else 1
    names = ("line", "side", "core", "fsdp")
    parts = Mesh(mesh.devices.reshape(copies // (side * cores), side, cores, shards), names)
    rows, shard = P(names, None), P("fsdp", None)
    experts = P("fsdp", None, None)
    in_specs = (rows, rows, shard, shard, shard, P("fsdp"), P("fsdp"), experts, experts, rows)
    out_specs = (rows, rows, shard, shard, shard, P("fsdp"), P("fsdp"), experts, experts)
    return jax.shard_map(body, mesh=parts, in_specs=in_specs, out_specs=out_specs, check_vma=False)
```

```python
import math
from functools import partial

import jax
import jax.numpy as jnp
from jax import lax
from jax.experimental import pallas as pl
from jax.experimental.pallas import tpu as pltpu
from jax.sharding import Mesh, PartitionSpec as P

D = 1024
HEADS = 16
KV_HEADS = 8
HEAD_DIM = 64
F = 512
TOP = 8
EXPERTS = 16
BLOCK = 256
QW = HEADS * HEAD_DIM
KVW = KV_HEADS * HEAD_DIM
EXTRA = 16
CHUNKS = 2
PAIR = 2 * HEAD_DIM

norm_eps = 1e-06
masked_score = -1e30
score_scale = HEAD_DIM ** (-0.5)
bf16, f32 = jnp.bfloat16, jnp.float32
VMEM = 56 * 1024 * 1024
POST_VMEM = 18 * 1024 * 1024


def dot(left, right, dims=((1,), (0,))):
    return lax.dot_general(left, right, (dims, ((), ())), preferred_element_type=f32)


def turn(value, axes, steps, sizes):
    pairs = []
    for source in range(math.prod(sizes)):
        place, rest = [], source
        for size in reversed(sizes):
            place.append(rest % size)
            rest //= size
        place.reverse()
        target = 0
        for at, size, step in zip(place, sizes, steps):
            target = target * size + (at + step) % size
        pairs.append((source, target))
    return lax.ppermute(value, axes, pairs)


def own_part(value, axis, index, parts):
    size = value.shape[axis] // parts
    return lax.dynamic_slice_in_dim(value, index * size, size, axis)


def whole(shape):
    return pl.BlockSpec(shape, lambda *_: (0,) * len(shape))


SCALARS = pl.BlockSpec(memory_space=pltpu.SMEM)
STAY = pl.BlockSpec(memory_space=pl.ANY)


def call(kernel, out_shape, in_specs, operands, out_specs=None, scratch=(), grid=None, prefetch=0, aliases=None, vmem=VMEM):
    out_specs = [whole(s.shape) for s in out_shape] if out_specs is None else out_specs
    spec = pltpu.PrefetchScalarGridSpec(
        num_scalar_prefetch=prefetch,
        grid=grid or (1,),
        in_specs=in_specs,
        out_specs=out_specs,
        scratch_shapes=list(scratch),
    )
    return pl.pallas_call(
        kernel,
        out_shape=list(out_shape),
        grid_spec=spec,
        input_output_aliases=aliases or {},
        compiler_params=pltpu.CompilerParams(vmem_limit_bytes=vmem),
        cost_estimate=pl.CostEstimate(flops=0, transcendentals=0, bytes_accessed=0),
    )(*operands)


def array(shape, dtype):
    return jax.ShapeDtypeStruct(shape, dtype)


def normalize(rows):
    scale_inv = lax.rsqrt(jnp.mean(rows * rows, -1, keepdims=True) + norm_eps)
    return (rows * scale_inv, scale_inv)


def norm_back(normed, scale_inv, grad_normed):
    return scale_inv * (grad_normed - normed * jnp.mean(grad_normed * normed, -1, keepdims=True))


def lanes(shape):
    return lax.broadcasted_iota(jnp.int32, shape, len(shape) - 1)


def halves(values):
    low = lanes(values.shape) % HEAD_DIM < HEAD_DIM // 2
    half = HEAD_DIM // 2
    return jnp.where(low, pltpu.roll(values, PAIR - half, 1), pltpu.roll(values, half, 1))


def rotary_tables(places):
    at = jnp.arange(PAIR, dtype=jnp.int32) % HEAD_DIM
    middle = HEAD_DIM // 2
    frequency = 10000.0 ** (-(2.0 * (at % middle).astype(f32)) / HEAD_DIM)
    angles = places.astype(f32)[:, None] * frequency[None, :]
    sign = jnp.where(at < middle, -1.0, 1.0)[None, :]
    return (jnp.cos(angles), jnp.sin(angles) * sign)


def load_rows(pieces, offsets, target, sems):
    copies = []
    for i, piece in enumerate(pieces):
        copy = pltpu.make_async_copy(piece, target.at[pl.ds(pl.multiple_of(offsets[i], 16), piece.shape[0]), :], sems.at[i])
        copy.start()
        copies.append(copy)
    return copies


def project(hidden_prev, hidden_own, gain, cosines, sines, pieces, offsets):
    length, count = hidden_own.shape[0], len(pieces)

    def kernel(offsets_ref, prev_ref, own_ref, gain_ref, cos_ref, sin_ref, *rest):
        piece_refs, (q_ref, kv_ref, in_ref, weight, sems) = rest[:count], rest[count:]
        copies = load_rows(piece_refs, offsets_ref, weight, sems)
        deep = 64
        for i, ref in enumerate((prev_ref, own_ref)):

            def rows(r, carry):
                normed, _ = normalize(ref[pl.ds(pl.multiple_of(r * deep, deep), deep), :].astype(f32))
                at = pl.ds(pl.multiple_of(i * length + r * deep, deep), deep)
                in_ref[at, :] = (normed * gain_ref[...]).astype(bf16)
                return carry

            lax.fori_loop(0, length // deep, rows, 0)
        for copy in copies:
            copy.wait()
        values = dot(in_ref[length:, :], weight[:, :QW])
        cos_own, sin_own = cos_ref[length:, :], sin_ref[length:, :]
        for g in range(QW // PAIR):
            u = values[:, g * PAIR : (g + 1) * PAIR]
            q_ref[:, g * PAIR : (g + 1) * PAIR] = (u * cos_own + halves(u) * sin_own).astype(bf16)
        values = dot(in_ref[...], weight[:, QW:])
        for g in range(KVW // PAIR):
            u = values[:, g * PAIR : (g + 1) * PAIR]
            kv_ref[:, g * PAIR : (g + 1) * PAIR] = (u * cos_ref[...] + halves(u) * sin_ref[...]).astype(bf16)
        kv_ref[:, KVW:] = values[:, KVW:].astype(bf16)

    width = QW + 2 * KVW
    return call(
        kernel,
        [array((length, QW), bf16), array((2 * length, 2 * KVW), bf16), array((2 * length, D), bf16)],
        [SCALARS] + [whole(v.shape) for v in (hidden_prev, hidden_own, gain, cosines, sines)] + [STAY] * count,
        (offsets, hidden_prev, hidden_own, gain, cosines, sines, *pieces),
        scratch=[pltpu.VMEM((D, width), bf16), pltpu.SemaphoreType.DMA((count,))],
    )


def doubled(values, which):
    low = lanes(values.shape) < HEAD_DIM
    swapped = pltpu.roll(values, HEAD_DIM, 1)
    return jnp.where(low, values, swapped) if which == 0 else jnp.where(low, swapped, values)


def two_rows(pair):
    low = lanes(pair.shape) < HEAD_DIM
    zero = jnp.zeros_like(pair)
    return jnp.concatenate([jnp.where(low, pair, zero), jnp.where(low, zero, pair)], 0)


def named_experts(routes):
    shape = (routes.shape[0], 128)
    named = routes[:, 0:1] == lanes(shape)
    for k in range(1, TOP):
        named = named | (routes[:, k : k + 1] == lanes(shape))
    return named


def attend(query, kv, flag):
    length = query.shape[0]

    def kernel(flag_ref, q_ref, kv_ref, att_ref, lse_ref):
        bias = jnp.where((lanes((1, 2 * length)) >= length) | (flag_ref[0] > 0), 0.0, masked_score)
        lse_ref[...] = jnp.zeros(lse_ref.shape, f32)

        def pair_of_keys(jj, carry):
            at = pl.multiple_of(jj * PAIR, PAIR)
            keys = kv_ref[:, pl.ds(at, PAIR)].astype(f32)
            vals = kv_ref[:, pl.ds(KVW + at, PAIR)].astype(f32)
            for t in range(2):
                place = pl.multiple_of((2 * jj + t) * PAIR, PAIR)
                both = (two_rows(q_ref[:, pl.ds(place, PAIR)].astype(f32)) * score_scale).astype(bf16)
                scores = dot(both, doubled(keys, t).astype(bf16), ((1,), (1,))) + bias
                largest = jnp.max(scores, -1, keepdims=True)
                exponent = jnp.exp(scores - largest)
                totals = jnp.sum(exponent, -1, keepdims=True)
                probs = (exponent * (1.0 / totals)).astype(bf16)
                lse = largest + jnp.log(totals)
                lse_ref[...] = jnp.where(lanes(lse_ref.shape) == 2 * jj + t, lse, lse_ref[...])
                val = doubled(vals, t)
                low = lanes(val.shape) < HEAD_DIM
                zero = jnp.zeros_like(val)
                out = dot(probs[:length], jnp.where(low, val, zero).astype(bf16))
                out = out + dot(probs[length:], jnp.where(low, zero, val).astype(bf16))
                att_ref[:, pl.ds(place, PAIR)] = out.astype(bf16)
            return carry

        lax.fori_loop(0, KVW // PAIR, pair_of_keys, 0)

    return call(
        kernel,
        [array((length, QW), bf16), array((2 * length, 128), f32)],
        [SCALARS, whole(query.shape), whole(kv.shape)],
        (flag, query, kv),
    )


def enter_experts(attended, hidden_own, gain, router_w, routes, pieces, offsets):
    length, count = attended.shape[0], len(pieces)

    def kernel(offsets_ref, att_ref, own_ref, gain_ref, router_ref, routes_ref, *rest):
        piece_refs, (res_ref, gate_ref, pay_ref, weight, sems) = rest[:count], rest[count:]
        copies = load_rows(piece_refs, offsets_ref, weight, sems)
        for copy in copies:
            copy.wait()
        residual = own_ref[...].astype(f32) + dot(att_ref[...], weight[...])
        res_ref[...] = residual
        normed, _ = normalize(residual)
        rows = (normed * gain_ref[...]).astype(bf16)
        pay_ref[:length, :] = rows
        logits = dot(rows, router_ref[...], ((1,), (1,)))
        real = lanes(logits.shape) < EXPERTS
        logits = jnp.where(real, logits, masked_score)
        raised = jnp.where(real, jnp.exp(logits - jnp.max(logits, -1, keepdims=True)), 0.0)
        router = raised * (1.0 / jnp.sum(raised, -1, keepdims=True))
        gate_ref[...] = router
        gates = jnp.where(named_experts(routes_ref[...]), router, 0.0).T[:EXTRA]
        high = gates.astype(bf16)
        pay_ref[length:, :length] = high
        pay_ref[length:, length : 2 * length] = (gates - high.astype(f32)).astype(bf16)
        pay_ref[length:, 2 * length :] = jnp.zeros((EXTRA, D - 2 * length), bf16)

    operands = (attended, hidden_own, gain, router_w, routes)
    return call(
        kernel,
        [array((length, D), f32), array((length, 128), f32), array((length + EXTRA, D), bf16)],
        [SCALARS] + [whole(v.shape) for v in operands] + [STAY] * count,
        (offsets, *operands, *pieces),
        scratch=[pltpu.VMEM((QW, D), bf16), pltpu.SemaphoreType.DMA((count,))],
    )


def add_weights(i, steps, lefts, rights, which, chunks, accs, out_refs):
    part = F // chunks
    clear(i, accs)
    for c, acc, out_ref in zip(which, accs, out_refs):
        for p, (left, right) in enumerate(zip(lefts, rights)):
            at = slice(p * part, (p + 1) * part)
            acc[:, at] += dot(left, right[:, c * part : (c + 1) * part], ((0,), (0,)))

        @pl.when(i == steps - 1)
        def _():
            deep = 128

            def rows(r, carry):
                at = pl.ds(pl.multiple_of(r * deep, deep), deep)
                out_ref[at, :] = acc[at, :].astype(bf16)
                return carry

            lax.fori_loop(0, D // deep, rows, 0)


def load_blocks(i, step, row_refs, grad_refs, both_ref, grad_ref, table_ref, sems):
    length, each = row_refs[0].shape[0] - EXTRA, grad_refs[0].shape[0]

    def copies(j, row_ref, block_ref):
        at = pl.ds(pl.multiple_of(j * length, length), length)
        out = [
            pltpu.make_async_copy(row_ref.at[:length, :], both_ref.at[at, :], sems.at[j, 0]),
            pltpu.make_async_copy(block_ref, grad_ref.at[at, :], sems.at[j, 1]),
        ]
        if table_ref is not None:
            out.append(pltpu.make_async_copy(row_ref.at[length:, : 2 * length], table_ref.at[j], sems.at[j, 2]))
        return out

    @pl.when(i == 0)
    def _():
        for j, row_ref in enumerate(row_refs):
            for copy in copies(j, row_ref, grad_refs[j // each].at[j % each]):
                copy.start()

    for b in range(step):
        for copy in copies(i * step + b, row_refs[0], grad_refs[0].at[0]):
            copy.wait()
    at = pl.ds(pl.multiple_of(i * step * length, step * length), step * length)
    return both_ref[at, :], grad_ref[at, :]


def gate_table(pair):
    length = pair.shape[1] // 2
    return pair[:, :length].astype(f32) + pair[:, length:].astype(f32)


def clear(i, accs):
    deep = 128

    @pl.when(i == 0)
    def _():
        def rows(r, carry):
            for acc in accs:
                acc[pl.ds(pl.multiple_of(r * deep, deep), deep), :] = jnp.zeros((deep, acc.shape[1]), f32)
            return carry

        lax.fori_loop(0, D // deep, rows, 0)


def expert(rows, grads, w_gate_up, w_down, index, chunks, which):
    sources, blocks, tall = len(grads), len(rows), rows[0].shape[0]
    length = tall - EXTRA
    step = 2
    turns = grads[0].shape[0] // step
    steps = blocks // step

    def kernel(index_ref, *refs):
        row_refs, grad_refs, refs = refs[:blocks], refs[blocks : blocks + sources], refs[blocks + sources :]
        gate_up_ref, down_ref, dgu_ref, hid_ref, sum_ref = refs[:5]
        out_refs, (both_ref, grad_ref, table_ref, sems, *accs) = refs[5 : 5 + len(which)], refs[5 + len(which) :]
        i = pl.program_id(0)
        both, grad = load_blocks(i, step, row_refs, grad_refs, both_ref, grad_ref, table_ref, sems)
        columns = []
        for b in range(step):
            table = gate_table(table_ref[i * step + b])
            mine = lax.broadcasted_iota(jnp.int32, table.shape, 0) == index_ref[1]
            row = jnp.sum(jnp.where(mine, table, 0.0), 0, keepdims=True)
            columns.append(jnp.broadcast_to(row, (128, length)).T[:, :1])
        gate = jnp.concatenate(columns, 0)
        gate_up = dot(both, gate_up_ref[0])
        gate_part, up_part = gate_up[:, :F], gate_up[:, F:]
        sigmoid_g = jax.nn.sigmoid(gate_part)
        silu_g = gate_part * sigmoid_g
        hidden = silu_g * up_part
        raw = dot(grad, down_ref[0])
        sums = jnp.sum(raw * hidden, 1, keepdims=True)
        gated = (gate * hidden).astype(bf16)
        grad_hidden = gate * raw
        grad_gate = (grad_hidden * up_part * sigmoid_g * (1.0 + gate_part * (1.0 - sigmoid_g))).astype(bf16)
        grad_up = (grad_hidden * silu_g).astype(bf16)
        for b in range(step):
            at = slice(b * length, (b + 1) * length)
            dgu_ref[b, :, :F] = grad_gate[at]
            dgu_ref[b, :, F:] = grad_up[at]
            hid_ref[b] = gated[at]
            sum_ref[b] = jnp.broadcast_to(sums[at], (length, 128)).T[:8]
        add_weights(i, steps, (both, both, grad), (grad_gate, grad_up, gated), which, chunks, accs, out_refs)

    def block(*shape):
        return pl.BlockSpec((step,) + shape, lambda i, index: (i,) + (0,) * len(shape))

    def source_block(source, *shape):
        def at(i, index):
            return (jnp.clip(i - source * turns, 0, turns - 1),) + (0,) * len(shape)

        return pl.BlockSpec((step,) + shape, at)

    def weight(*shape):
        return pl.BlockSpec((1,) + shape, lambda i, index: (index[0], 0, 0))

    shapes = [array((blocks, length, 2 * F), bf16), array((blocks, length, F), bf16), array((blocks, 8, length), f32)]
    scratch = [
        pltpu.VMEM((blocks * length, D), bf16),
        pltpu.VMEM((blocks * length, D), bf16),
        pltpu.VMEM((blocks, EXTRA, 2 * length), bf16),
        pltpu.SemaphoreType.DMA((blocks, 3)),
    ]
    return call(
        kernel,
        shapes + [array((D, 3 * F // chunks), bf16)] * len(which),
        [STAY] * (blocks + sources)
        + [weight(D, 2 * F), weight(D, F)],
        (index, *rows, *grads, w_gate_up, w_down),
        out_specs=[block(length, 2 * F), block(length, F), block(8, length)]
        + [pl.BlockSpec((D, 3 * F // chunks), lambda i, index: (0, 0)) for _ in which],
        scratch=scratch + [pltpu.VMEM((D, 3 * F // chunks), f32)] * len(which),
        grid=(steps,),
        prefetch=1,
    )


def gate_column(table, expert):
    mine = lax.broadcasted_iota(jnp.int32, table.shape, 0) == expert
    row = jnp.sum(jnp.where(mine, table, 0.0), 0, keepdims=True)
    return jnp.broadcast_to(row, (128, table.shape[1])).T[:, :1]


def last_expert(rows, grads, w_gate_up, w_down, indices, earlier, sums):
    sources, blocks, tall = len(grads), len(rows), rows[0].shape[0]
    length = tall - EXTRA
    step = 2
    turns = grads[0].shape[0] // step
    steps = blocks // step
    others = len(earlier)

    def kernel(indices_ref, *refs):
        row_refs, grad_refs, refs = refs[:blocks], refs[blocks : blocks + sources], refs[blocks + sources :]
        gate_up_ref, down_ref, refs = refs[0], refs[1], refs[2:]
        earlier_refs, weight_refs, sum_refs, refs = refs[:others], refs[others : 2 * others], refs[2 * others : 3 * others], refs[3 * others :]
        dgu_ref, hid_ref, out_refs, (both_ref, grad_ref, table_ref, sems) = refs[0], refs[1], refs[2 : 2 + sources], refs[2 + sources :]
        i = pl.program_id(0)
        both, grad = load_blocks(i, step, row_refs, grad_refs, both_ref, grad_ref, table_ref, sems)
        gate = jnp.concatenate([gate_column(gate_table(table_ref[i * step + b]), indices_ref[2 * others + 1]) for b in range(step)], 0)
        gate_up = dot(both, gate_up_ref[0])
        gate_part, up_part = gate_up[:, :F], gate_up[:, F:]
        sigmoid_g = jax.nn.sigmoid(gate_part)
        silu_g = gate_part * sigmoid_g
        hidden = silu_g * up_part
        raw = dot(grad, down_ref[0])
        own = jnp.sum(raw * hidden, 1, keepdims=True)
        gated = (gate * hidden).astype(bf16)
        grad_hidden = gate * raw
        grad_gate = (grad_hidden * up_part * sigmoid_g * (1.0 + gate_part * (1.0 - sigmoid_g))).astype(bf16)
        grad_up = (grad_hidden * silu_g).astype(bf16)
        total = dot(jnp.concatenate([grad_gate, grad_up], 1), gate_up_ref[0], ((1,), (1,)))
        for part_ref, weight_ref in zip(earlier_refs, weight_refs):
            part = jnp.concatenate([part_ref[b] for b in range(step)], 0)
            total = total + dot(part, weight_ref[0], ((1,), (1,)))
        for b in range(step):
            at = slice(b * length, (b + 1) * length)
            dgu_ref[b, :, :F] = grad_gate[at]
            dgu_ref[b, :, F:] = grad_up[at]
            hid_ref[b] = gated[at]
            table = jnp.zeros((EXTRA, length), f32)
            place = lax.broadcasted_iota(jnp.int32, table.shape, 0)
            for e in range(others):
                table = jnp.where(place == indices_ref[2 * e + 1], sum_refs[e][b, :1, :], table)
            row = jnp.broadcast_to(own[at], (length, 128)).T[:1]
            table = jnp.where(place == indices_ref[2 * others + 1], row, table)
            high = table.astype(bf16)
            for source, out_ref in enumerate(out_refs):

                @pl.when((i >= source * turns) & (i < (source + 1) * turns))
                def _():
                    out_ref[b, :length, :] = total[at].astype(bf16)
                    out_ref[b, length:, :length] = high
                    out_ref[b, length:, length : 2 * length] = (table - high.astype(f32)).astype(bf16)
                    out_ref[b, length:, 2 * length :] = jnp.zeros((EXTRA, D - 2 * length), bf16)

    def block(*shape):
        return pl.BlockSpec((step,) + shape, lambda i, index: (i,) + (0,) * len(shape))

    def source_block(source, *shape):
        def at(i, index):
            return (jnp.clip(i - source * turns, 0, turns - 1),) + (0,) * len(shape)

        return pl.BlockSpec((step,) + shape, at)

    def weight(e, *shape):
        return pl.BlockSpec((1,) + shape, lambda i, index: (index[2 * e], 0, 0))

    return call(
        kernel,
        [array((blocks, length, 2 * F), bf16), array((blocks, length, F), bf16)]
        + [array((blocks // sources, tall, D), bf16)] * sources,
        [STAY] * (blocks + sources)
        + [weight(others, D, 2 * F), weight(others, D, F)]
        + [block(length, 2 * F)] * others
        + [weight(e, D, 2 * F) for e in range(others)]
        + [block(8, length)] * others,
        (indices, *rows, *grads, w_gate_up, w_down, *earlier, *[w_gate_up] * others, *sums),
        out_specs=[block(length, 2 * F), block(length, F)] + [source_block(s, tall, D) for s in range(sources)],
        scratch=[
            pltpu.VMEM((blocks * length, D), bf16),
            pltpu.VMEM((blocks * length, D), bf16),
            pltpu.VMEM((blocks, EXTRA, 2 * length), bf16),
            pltpu.SemaphoreType.DMA((blocks, 3)),
        ],
        grid=(steps,),
        prefetch=1,
    )


def weight_grads(rows, grads, grad_gate_up, hidden, chunks, which, after):
    sources, blocks, tall = len(grads), len(rows), rows[0].shape[0]
    length = tall - EXTRA
    step = 2
    turns = grads[0].shape[0] // step
    steps = blocks // step

    def kernel(after_ref, *refs):
        row_refs, grad_refs, refs = refs[:blocks], refs[blocks : blocks + sources], refs[blocks + sources :]
        dgu_ref, hid_ref, out_refs = refs[0], refs[1], refs[2 : 2 + len(which)]
        both_ref, grad_ref, sems, *accs = refs[2 + len(which) :]
        i = pl.program_id(0)
        both, grad = load_blocks(i, step, row_refs, grad_refs, both_ref, grad_ref, None, sems)
        grad_gate = jnp.concatenate([dgu_ref[b, :, :F] for b in range(step)], 0)
        grad_up = jnp.concatenate([dgu_ref[b, :, F:] for b in range(step)], 0)
        gated = jnp.concatenate([hid_ref[b] for b in range(step)], 0)
        add_weights(i, steps, (both, both, grad), (grad_gate, grad_up, gated), which, chunks, accs, out_refs)

    def block(*shape):
        return pl.BlockSpec((step,) + shape, lambda i, after: (i,) + (0,) * len(shape))

    def source_block(source, *shape):
        def at(i, after):
            return (jnp.clip(i - source * turns, 0, turns - 1),) + (0,) * len(shape)

        return pl.BlockSpec((step,) + shape, at)

    return call(
        kernel,
        [array((D, 3 * F // chunks), bf16)] * len(which),
        [STAY] * (blocks + sources)
        + [block(length, 2 * F), block(length, F)],
        (after, *rows, *grads, grad_gate_up, hidden),
        out_specs=[pl.BlockSpec((D, 3 * F // chunks), lambda i, after: (0, 0)) for _ in which],
        scratch=[pltpu.VMEM((blocks * length, D), bf16)] * 2
        + [pltpu.SemaphoreType.DMA((blocks, 3))]
        + [pltpu.VMEM((D, 3 * F // chunks), f32)] * len(which),
        grid=(steps,),
        prefetch=1,
    )


def row_terms(parts, weights, indices, sources):
    blocks, length, width = parts[0].shape
    count = len(parts)
    step = 2
    turns = blocks // step // sources

    def kernel(indices_ref, *refs):
        part_refs, weight_refs, out_refs = refs[:count], refs[count : 2 * count], refs[2 * count :]
        i = pl.program_id(0)
        total = None
        for part_ref, weight_ref in zip(part_refs, weight_refs):
            term = dot(jnp.concatenate([part_ref[b] for b in range(step)], 0), weight_ref[0], ((1,), (1,)))
            total = term if total is None else total + term
        for source, out_ref in enumerate(out_refs):

            @pl.when((i >= source * turns) & (i < (source + 1) * turns))
            def _():
                for b in range(step):
                    out_ref[b] = total[b * length : (b + 1) * length].astype(bf16)

    def weight(e):
        return pl.BlockSpec((1,) + weights.shape[1:], lambda i, index: (index[2 * e], 0, 0))

    def source_block(source):
        return pl.BlockSpec((step, length, D), lambda i, index: (jnp.clip(i - source * turns, 0, turns - 1), 0, 0))

    return call(
        kernel,
        [array((blocks // sources, length, D), bf16)] * sources,
        [pl.BlockSpec((step, length, width), lambda i, index: (i, 0, 0))] * count + [weight(e) for e in range(count)],
        (indices, *parts, *[weights] * count),
        out_specs=[source_block(s) for s in range(sources)],
        grid=(blocks // step,),
        prefetch=1,
    )


def backward(
    returned, residual, router, routes, cotangent, gain, router_w, query, kv, lse, cosines, sines, inputs,
    hidden_prev, hidden_own, attended, out_pieces, out_offsets, qkv_pieces, qkv_offsets, flag, core, shards, cores,
):
    length, terms = residual.shape[0], len(returned)
    width = QW + 2 * KVW
    out_count, qkv_count = len(out_pieces), len(qkv_pieces)

    deep = D // (shards * cores)

    def kernel(out_offsets_ref, qkv_offsets_ref, flag_ref, core_ref, *rest):
        term_refs, rest = rest[:terms], rest[terms:]
        res_ref, gate_ref, routes_ref, cot_ref, gain_ref, router_ref, q_ref, kv_ref, lse_ref, cos_ref, sin_ref = rest[:11]
        in_ref, prev_ref, own_ref, att_ref, rest = *rest[11:15], rest[15:]
        out_refs, qkv_refs, rest = rest[:out_count], rest[out_count : out_count + qkv_count], rest[out_count + qkv_count :]
        gres_ref, gown_ref, gprev_ref, own_grad_ref = rest[:4]
        far_refs, rest = rest[4 : 4 + 3 * (cores - 1)], rest[4 + 3 * (cores - 1) :]
        w_out, w_qkv, gatt_ref, dq_ref, dkv_ref, small_ref, sum_ref, out_sems, qkv_sems, end_sems = rest
        out_copies = load_rows(out_refs, out_offsets_ref, w_out, out_sems)
        qkv_copies = load_rows(qkv_refs, qkv_offsets_ref, w_qkv, qkv_sems)
        total = term_refs[0][...].astype(f32)
        for ref in term_refs[1:]:
            total = total + ref[...].astype(f32)
        table = total[length:, :length] + total[length:, length : 2 * length]
        gate_grads = jnp.concatenate([table, jnp.zeros((128 - EXTRA, length), f32)], 0).T
        grad_router = jnp.where(named_experts(routes_ref[...]), gate_grads, 0.0)
        router = gate_ref[...]
        grad_logits = (router * (grad_router - jnp.sum(router * grad_router, -1, keepdims=True))).astype(bf16)
        grad_input = total[:length] + dot(grad_logits, router_ref[...])
        normed, inverse = normalize(res_ref[...])
        gain_row = gain_ref[...]
        rows = (normed * gain_row).astype(bf16)
        small = dot(rows, grad_logits, ((0,), (0,)))
        gain_grad = jnp.sum(grad_input * normed, 0, keepdims=True)
        small_ref[...] = jnp.where(lanes((D, 128)) == EXPERTS, jnp.broadcast_to(gain_grad, (128, D)).T, small)
        grad_residual = cot_ref[...].astype(f32) + norm_back(normed, inverse, grad_input * gain_row)
        gres_ref[...] = grad_residual
        grad_attn = grad_residual.astype(bf16)
        for copy in out_copies:
            copy.wait()
        gatt_ref[...] = dot(grad_attn, w_out[...], ((1,), (1,))).astype(bf16)

        def write(at, values):
            sum_ref[:, at : at + values.shape[1]] = values.astype(bf16)

        write(width, dot(att_ref[...], grad_attn, ((0,), (0,))))

        bias = jnp.where((lanes((1, 2 * length)) >= length) | (flag_ref[0] > 0), 0.0, masked_score)
        cos_own, sin_own = cos_ref[length:, :], sin_ref[length:, :]

        def back(values, cos, sin):
            return (values * cos - halves(values) * sin).astype(bf16)

        def pair_of_keys(jj, carry):
            at = pl.multiple_of(jj * PAIR, PAIR)
            keys = kv_ref[:, pl.ds(at, PAIR)].astype(f32)
            vals = kv_ref[:, pl.ds(KVW + at, PAIR)].astype(f32)
            key_grads, val_grads = [], []
            for t in range(2):
                place = pl.multiple_of((2 * jj + t) * PAIR, PAIR)
                both = (two_rows(q_ref[:, pl.ds(place, PAIR)].astype(f32)) * score_scale).astype(bf16)
                outs = two_rows(gatt_ref[:, pl.ds(place, PAIR)].astype(f32)).astype(bf16)
                key = doubled(keys, t).astype(bf16)
                val = doubled(vals, t).astype(bf16)
                own = lanes(lse_ref.shape) == 2 * jj + t
                log_total = jnp.sum(jnp.where(own, lse_ref[...], 0.0), -1, keepdims=True)
                scores = dot(both, key, ((1,), (1,))) + bias
                probs = jnp.exp(scores - log_total)
                grad_probs = dot(outs, val, ((1,), (1,)))
                inner = jnp.sum(probs * grad_probs, -1, keepdims=True)
                grad_scores = (probs * (grad_probs - inner)).astype(bf16)
                grad_query = dot(grad_scores, key) * score_scale
                low = lanes((length, PAIR)) < HEAD_DIM
                grad_query = jnp.where(low, grad_query[:length], grad_query[length:])
                dq_ref[:, pl.ds(place, PAIR)] = back(grad_query, cos_own, sin_own)
                key_grad = dot(grad_scores, both, ((0,), (0,)))
                val_grad = dot(probs.astype(bf16), outs, ((0,), (0,)))
                key_grads.append(key_grad + pltpu.roll(key_grad, HEAD_DIM, 1))
                val_grads.append(val_grad + pltpu.roll(val_grad, HEAD_DIM, 1))
            low = lanes((2 * length, PAIR)) < HEAD_DIM
            dkv_ref[:, pl.ds(at, PAIR)] = back(jnp.where(low, *key_grads), cos_ref[...], sin_ref[...])
            dkv_ref[:, pl.ds(KVW + at, PAIR)] = jnp.where(low, *val_grads).astype(bf16)
            return carry

        lax.fori_loop(0, KVW // PAIR, pair_of_keys, 0)
        write(0, dot(in_ref[length:, :], dq_ref[...], ((0,), (0,))))
        write(QW, dot(in_ref[...], dkv_ref[...], ((0,), (0,))))
        for copy in qkv_copies:
            copy.wait()
        from_kv = dot(dkv_ref[...], w_qkv[:, QW:], ((1,), (1,)))
        own = from_kv[length:] + dot(dq_ref[...], w_qkv[:, :QW], ((1,), (1,)))
        gown_ref[...] = own
        gprev_ref[...] = from_kv[:length].astype(bf16)
        normed_own, _ = normalize(own_ref[...].astype(f32))
        normed_prev, _ = normalize(prev_ref[...].astype(f32))
        gain_grad = jnp.sum(own * normed_own + from_kv[:length] * normed_prev, 0, keepdims=True)
        column = jnp.broadcast_to(gain_grad, (128, D)).T
        write(width + D, jnp.where(lanes((D, 128)) == EXPERTS + 1, column, small_ref[...]))
        copies = []
        for s in range(shards):
            for j in range(cores):
                at = pl.multiple_of((s * cores + (core_ref[0] + j) % cores) * deep, 16)
                targets = [(own_grad_ref, 0)] if j == 0 else [(far_refs[3 * (j - 1) + g], g * D) for g in range(3)]
                for g, (target, start) in enumerate(targets):
                    source = sum_ref.at[pl.ds(at, deep), start : start + target.shape[2]]
                    copy = pltpu.make_async_copy(source, target.at[s], end_sems.at[s, j, g])
                    copy.start()
                    copies.append(copy)
        for copy in copies:
            copy.wait()

    operands = (
        *returned, residual, router, routes, cotangent, gain, router_w, query, kv, lse, cosines, sines, inputs,
        hidden_prev, hidden_own, attended,
    )
    return call(
        kernel,
        [
            array((length, D), f32),
            array((length, D), f32),
            array((length, D), bf16),
        ]
        + [array((shards, deep, width + D + 128), bf16)]
        + [array((shards, deep, w), bf16) for w in (D, D, D + 128)] * (cores - 1),
        [SCALARS] * 4 + [whole(v.shape) for v in operands] + [STAY] * (out_count + qkv_count),
        (out_offsets, qkv_offsets, flag, core, *operands, *out_pieces, *qkv_pieces),
        out_specs=[whole((length, D)), whole((length, D)), whole((length, D))] + [STAY] * (1 + 3 * (cores - 1)),
        scratch=[
            pltpu.VMEM((QW, D), bf16),
            pltpu.VMEM((D, width), bf16),
            pltpu.VMEM((length, QW), bf16),
            pltpu.VMEM((length, QW), bf16),
            pltpu.VMEM((2 * length, 2 * KVW), bf16),
            pltpu.VMEM((D, 128), f32),
            pltpu.VMEM((D, width + D + 128), bf16),
            pltpu.SemaphoreType.DMA((out_count,)),
            pltpu.SemaphoreType.DMA((qkv_count,)),
            pltpu.SemaphoreType.DMA((shards, cores, 3)),
        ],
    )


def first_back(grad_sum, grad_residual, hidden_own, gain):
    def kernel(sum_ref, res_ref, hid_ref, gain_ref, out_ref):
        deep = 32

        def rows(r, carry):
            at = pl.ds(pl.multiple_of(r * deep, deep), deep)
            normed, inverse = normalize(hid_ref[at, :].astype(f32))
            out_ref[at, :] = res_ref[at, :] + norm_back(normed, inverse, sum_ref[at, :] * gain_ref[...])
            return carry

        lax.fori_loop(0, out_ref.shape[0] // deep, rows, 0)

    operands = (grad_sum, grad_residual, hidden_own, gain)
    return call(kernel, [array(grad_sum.shape, f32)], [whole(v.shape) for v in operands], operands, vmem=16 * 1024 * 1024)[0]


def place(sources, experts, outs, shapes, chunk, chunks):
    part = F // chunks
    count = sum(source.shape[0] for source in sources)

    def kernel(experts_ref, *refs):
        source_refs = refs[: len(sources)]
        gate_up_ref, down_ref, wide, sems = refs[len(sources) + len(outs) :]
        copies = []
        deep = 128
        values = [ref.at[i] for ref in source_refs for i in range(ref.shape[0])]
        for i, source in enumerate(values):

            def rows(r, carry):
                at = pl.ds(pl.multiple_of(r * deep, deep), deep)
                wide[i, at, :] = source[at, :].astype(f32)
                return carry

            lax.fori_loop(0, D // deep, rows, 0)
            for p, target in enumerate(
                (
                    gate_up_ref.at[experts_ref[i], :, chunk * part : (chunk + 1) * part],
                    gate_up_ref.at[experts_ref[i], :, F + chunk * part : F + (chunk + 1) * part],
                    down_ref.at[experts_ref[i], :, chunk * part : (chunk + 1) * part],
                )
            ):
                copy = pltpu.make_async_copy(wide.at[i, :, p * part : (p + 1) * part], target, sems.at[i, p])
                copy.start()
                copies.append(copy)
        for copy in copies:
            copy.wait()

    return call(
        kernel,
        shapes,
        [SCALARS] + [whole(v.shape) for v in sources] + [STAY] * len(outs),
        (experts, *sources, *outs),
        out_specs=[STAY, STAY],
        scratch=[pltpu.VMEM((count, D, 3 * part), f32), pltpu.SemaphoreType.DMA((count, 3))],
        aliases={1 + len(sources) + i: i for i in range(len(outs))},
        vmem=28 * 1024 * 1024,
    )


def unpack(sources, offsets, rows, others=()):
    count = sum(source.shape[0] for source in sources)
    deep, wide = sources[0].shape[1:]
    widths = (QW + 2 * KVW, D)

    def kernel(offsets_ref, *refs):
        source_refs, refs = refs[: len(sources)], refs[len(sources) :]
        other_refs, refs = refs[: len(others)], refs[len(others) :]
        out_refs, router_ref, ffn_ref, attn_ref, values_ref, rest_ref, sems = refs[:2], *refs[2:]
        copies = []
        for i, source in enumerate([ref.at[i] for ref in source_refs for i in range(ref.shape[0])]):
            some = 32

            def rows_of(r, carry):
                place = pl.ds(pl.multiple_of(r * some, some), some)
                value = source[place, :].astype(f32)
                values_ref[i, place, :] = value + other_refs[i][0, place, :].astype(f32) if others else value
                return carry

            lax.fori_loop(0, deep // some, rows_of, 0)
            at = pl.multiple_of(offsets_ref[i], 8)
            start = 0
            for p, (out_ref, width) in enumerate(zip(out_refs, widths)):
                copy = pltpu.make_async_copy(values_ref.at[i, :, start : start + width], out_ref.at[pl.ds(at, deep), :], sems.at[i, p])
                copy.start()
                copies.append(copy)
                start += width
            rest_ref[pl.ds(at, deep), :] = values_ref[i, :, start:]
        router_ref[...] = rest_ref[:, :EXPERTS]
        turned = rest_ref[...].T
        ffn_ref[...] = turned[EXPERTS : EXPERTS + 1]
        attn_ref[...] = turned[EXPERTS + 1 : EXPERTS + 2]
        for copy in copies:
            copy.wait()

    return call(
        kernel,
        [array((rows, width), f32) for width in widths] + [array((rows, EXPERTS), f32)] + [array((1, rows), f32)] * 2,
        [SCALARS] + [whole(v.shape) for v in (*sources, *others)],
        (offsets, *sources, *others),
        out_specs=[STAY] * 2 + [whole((rows, EXPERTS))] + [whole((1, rows))] * 2,
        scratch=[
            pltpu.VMEM((count, deep, wide), f32),
            pltpu.VMEM((rows, wide - sum(widths)), f32),
            pltpu.SemaphoreType.DMA((count, 2)),
        ],
    )


def post(function, flags, arrays, outs, parts=8):
    def kernel(flags_ref, *refs):
        ins, results = refs[: len(arrays)], refs[len(arrays) :]
        scalars = [flags_ref[i] for i in range(flags.shape[0])]

        def part_of(ref, r):
            deep = ref.shape[-2] // parts
            return (slice(None),) * (len(ref.shape) - 2) + (pl.ds(pl.multiple_of(r * deep, deep), deep), slice(None))

        def rows(r, carry):
            values = function(scalars, *[ref[part_of(ref, r)] for ref in ins])
            for ref, value in zip(results, values):
                if isinstance(value, tuple):
                    value = jnp.stack(value)
                ref[part_of(ref, r)] = value.astype(ref.dtype)
            return carry

        lax.fori_loop(0, parts, rows, 0)

    near = pl.BlockSpec(memory_space=pltpu.VMEM)
    return pl.pallas_call(
        kernel,
        out_shape=list(outs),
        in_specs=[SCALARS] + [near] * len(arrays),
        out_specs=[near] * len(outs),
        compiler_params=pltpu.CompilerParams(vmem_limit_bytes=POST_VMEM),
        cost_estimate=pl.CostEstimate(flops=0, transcendentals=0, bytes_accessed=0),
    )(flags, *arrays)


def tie(values, after):
    return lax.optimization_barrier((values, after))[0]


def doubling_sum(value, axis):
    count, step = lax.axis_size(axis), 1
    if count & (count - 1):
        return lax.psum(value, axis)
    while step < count:
        value = value + lax.ppermute(value, axis, [(i, i ^ step) for i in range(count)])
        step *= 2
    return value


def body(
    hidden_in, routes, w_qkv, w_out, w_router, attn_gain, ffn_gain, w_gate_up, w_down, cotangent
):
    line, shards = lax.axis_size("line"), lax.axis_size("fsdp")
    side, cores = lax.axis_size("side"), lax.axis_size("core")
    shard, side_at, core_at = lax.axis_index("fsdp"), lax.axis_index("side"), lax.axis_index("core")
    length = hidden_in.shape[0]
    near = [(a, s) for s in range(shards) for a in range(side)]
    local_experts = w_gate_up.shape[0]
    count = local_experts // (side * cores)
    barrier = lax.optimization_barrier

    def other_core(value, core=1):
        return turn(value, "core", (core,), (cores,))

    def other_side(value, step=1):
        return turn(value, "side", (step,), (side,))

    def from_shard(part, step):
        return turn(part, "fsdp", (step,), (shards,))

    def fetch_start(piece, sides):
        part = own_part(piece, 0, core_at * sides + side_at % sides, cores * sides)
        return [from_shard(part, step) for step in range(1, shards)]

    def fetch_end(piece, first, sides):
        rows = piece.shape[0]
        out, offsets = [piece], [shard * rows]
        for step, part in enumerate(first, 1):
            base = (shard - step) % shards * rows
            for a in range(sides):
                theirs = other_side(part, a) if a else part
                for core in range(cores):
                    out.append(other_core(theirs, core) if core else theirs)
                    at = (core_at - core) % cores * sides + (side_at - a) % sides
                    offsets.append(base + at * part.shape[0])
        return out, jnp.stack(offsets).astype(jnp.int32)

    def over_cores(first):
        return [other_core(first, core) if core else first for core in range(cores)]

    def far_blocks(blocks):
        return [other_core(blocks[core * len(near) : (core + 1) * len(near)], -core % cores) for core in range(1, cores)]

    def add_up(first, others):
        for other in others:
            first = first + other
        return first

    def send_back(total):
        out = [total[0]]
        for i, (a, s) in enumerate(near):
            if (a, s) != (0, 0):
                out.append(turn(total[i], ("side", "fsdp"), (-a % side, -s % shards), (side, shards)))
        return out

    parity = shard % 2
    flag = parity.astype(jnp.int32)[None]
    later = [(i, i + 1) for i in range(0, shards, 2)]
    before = [(i + 1, i) for i in range(0, shards, 2)]

    small_rows = w_router.shape[0]
    small = jnp.concatenate([w_router.T, attn_gain[None], ffn_gain[None]], 0)
    qkv_first = fetch_start(w_qkv, side)
    hidden_prev = lax.ppermute(hidden_in, "fsdp", later)
    full_small = jnp.zeros((EXPERTS + 2, D), bf16)
    for step in range(shards):
        theirs = from_shard(small, step) if step else small
        full_small = lax.dynamic_update_slice_in_dim(full_small, theirs, (shard - step) % shards * small_rows, 1)
    gain_attn = full_small[EXPERTS : EXPERTS + 1].astype(f32)
    gain_ffn = full_small[EXPERTS + 1 :].astype(f32)
    router_w = jnp.pad(full_small[:EXPERTS], ((0, 128 - EXPERTS), (0, 0)))
    sideways = [other_side(cotangent, a) for a in range(1, side)]
    across = [from_shard(cotangent, s) for s in range(1, shards)]
    rows_at = jnp.arange(length, dtype=jnp.int32)
    cosines, sines = rotary_tables(jnp.concatenate([rows_at, parity * length + rows_at]))
    qkv_pieces, qkv_offsets = fetch_end(w_qkv, qkv_first, side)
    out_first = fetch_start(tie(w_out, (hidden_prev, qkv_first)), 1)

    across, hidden_prev = barrier((across, hidden_prev))
    corners = [[other_side(v, a) for a in range(1, side)] for v in across]
    queries, kv, inputs = project(hidden_prev, hidden_in, gain_attn, cosines, sines, qkv_pieces, qkv_offsets)
    out_first, queries, kv = barrier((out_first, queries, kv))
    out_pieces, out_offsets = fetch_end(w_out, out_first, 1)
    attended, lse = attend(queries, kv, flag)
    grads_near = [cotangent] + sideways + [v for first, rest in zip(across, corners) for v in [first] + rest]
    grads_near = jnp.stack(tie(grads_near, attended))
    out_pieces, attended, grads_near = barrier((out_pieces, attended, grads_near))
    grads_near = over_cores(grads_near)
    residual, router, payload = enter_experts(attended, hidden_in, gain_ffn, router_w, routes, out_pieces, out_offsets)
    rows_near = [turn(payload, ("side", "fsdp"), (a, s), (side, shards)) if (a, s) != (0, 0) else payload for a, s in near]
    rows_near = rows_near + [other_core(v, core) for core in range(1, cores) for v in rows_near]

    clock = []

    def run(function, *inputs):
        if clock:
            inputs = barrier((inputs, tuple(clock)))[0]
        out = function(*inputs)
        clock[:] = jax.tree.leaves(out)
        return out

    mine_at = (side_at * cores + core_at) * count
    indices = [jnp.stack([mine_at + e, shard * local_experts + mine_at + e]).astype(jnp.int32) for e in range(count)]
    both = jnp.concatenate(indices)
    order = jnp.stack([((side_at - a) % side * cores + (core_at - core) % cores) for core in range(cores) for a in range(side)])
    order = order.astype(jnp.int32) * count
    shapes = [array((local_experts, D, 2 * F), f32), array((local_experts, D, F), f32)]
    place_at = lax.axis_index("line")
    end = (place_at == 0) | (place_at == line - 1)

    def go_in(raw):
        return lax.ppermute(raw, "line", [(0, 1), (3, 2)])

    def cross(half):
        return lax.ppermute(half, "line", [(1, 2), (2, 1)])

    def in_and_out(sent):
        return lax.ppermute(sent, "line", [(0, 1), (1, 0), (2, 3), (3, 2)])

    def go_out(total):
        return lax.ppermute(total, "line", [(1, 0), (2, 3)])

    def chosen(got, kept):
        return jnp.where(end, got, kept)

    def sides(full):
        return [other_side(full, a) for a in range(1, side)]

    def core_swaps(pair):
        return [other_core(pair, core) for core in range(1, cores)]

    def stacked(full, others):
        return jnp.stack([full] + others)

    def plus(first, second):
        return first + second

    def split(blocks):
        return [blocks[core * len(near) : (core + 1) * len(near)] for core in range(cores)]

    def near_sums(first, others):
        total = add_up(first, others)
        return [total[i] for i in range(len(near))]

    def placed(pair, swaps, outs, e, c):
        return place([pair] + swaps, order + e, outs, shapes, c, CHUNKS)

    def back(terms):
        return backward(
            terms, residual, router, routes, cotangent, gain_ffn, router_w, queries, kv, lse, cosines, sines, inputs, hidden_prev,
            hidden_in, attended, out_pieces, out_offsets, qkv_pieces, qkv_offsets, flag, core_at.astype(jnp.int32)[None], shards, cores,
        )

    def by_shard(total):
        return total[0] if shards == 1 else own_part(total, 0, shard, shards)[0], [
            own_part(total, 0, (shard + step) % shards, shards)[0] for step in range(1, shards)
        ]

    def by_side(total):
        return own_part(total, 0, side_at, side), [own_part(total, 0, (side_at + a) % side, side) for a in range(1, side)]

    def by_step(total):
        return [total[s * side : (s + 1) * side] for s in range(shards)]

    def by_near(total):
        return total[0], [total[a] for a in range(1, side)]

    def swap_lines(value, step):
        return lax.ppermute(value, "line", [(i, i ^ step) for i in range(line)])

    flags = jnp.stack([end, shard > 0, side_at > 0]).astype(jnp.int32)

    def f(value):
        return value.astype(f32)

    def pick(flag, got, kept):
        return jnp.where(flag > 0, f(got), f(kept))

    def steps(function, outs, *arrays):
        outs = [v if isinstance(v, jax.ShapeDtypeStruct) else array(v, bf16) for v in outs]
        return run(lambda *v: tuple(post(function, flags, v, outs)), *arrays)

    if (line, side, cores, shards, count) != (4, 2, 2, 2, 2):
        grads_gu, hiddens, sums, chunks = [], [], [], []
        for e in range(count - 1):
            grad_gu, hidden, total, *parts = expert(rows_near, grads_near, w_gate_up, w_down, indices[e], CHUNKS, range(CHUNKS))
            grads_gu.append(grad_gu)
            hiddens.append(hidden)
            sums.append(total)
            chunks.append(parts)
        grad_gu, hidden, *blocks = last_expert(rows_near, grads_near, w_gate_up, w_down, both, grads_gu, sums)
        hiddens.append(hidden)
        chunks.append(weight_grads(rows_near, grads_near, grad_gu, hidden, CHUNKS, range(CHUNKS), both))
        terms = row_terms(hiddens, w_down, both, cores)
        returned = send_back([v for v in add_up(blocks[0], [other_core(g, -c % cores) for c, g in enumerate(blocks[1:], 1)])])
        mixed = send_back([v for v in add_up(terms[0], [other_core(g, -c % cores) for c, g in enumerate(terms[1:], 1)])])
        grad_residual, grad_own, grad_prev, own_w, *other_w = back(returned)
        joined = [jnp.concatenate(other_w[i : i + 3], -1) for i in range(0, len(other_w), 3)]
        own_w = add_up(own_w, [other_core(w, core) for core, w in enumerate(joined, 1)])
        own_w, other_w = by_shard(own_w)
        own_w = add_up(own_w, [from_shard(w, step) for step, w in enumerate(other_w, 1)])
        own_w = add_up(own_w, [other_side(own_w, a) for a in range(1, side)])

        def line_sum(value):
            if line & (line - 1):
                return lax.psum(value, "line")
            for bit in range(line.bit_length() - 1):
                value = value + swap_lines(value, 1 << bit)
            return value

        sum_w, outs = line_sum(own_w), ()
        for e, parts in enumerate(chunks):
            for c, part in enumerate(parts):
                full = line_sum(part)
                pair = jnp.stack([full] + sides(full))
                outs = placed(pair, core_swaps(pair), outs, e, c)
        at_w = jnp.stack([(core_at - core) % cores for core in range(cores)]).astype(jnp.int32) * sum_w.shape[0]
        qkv_sum, out_sum, router_sum, ffn_sum, attn_sum = unpack(
            [w[None] for w in [sum_w] + core_swaps(sum_w)], at_w, sum_w.shape[0] * cores
        )
        grad_sum = grad_own + lax.ppermute(grad_prev, "fsdp", before).astype(f32)
        grad_in = first_back(grad_sum, grad_residual, hidden_in, gain_attn)
        layer_out = add_up(residual, [m.astype(f32) for m in mixed]).astype(bf16)
        return (
            layer_out, grad_in, qkv_sum, out_sum, router_sum, attn_sum[0], ffn_sum[0], outs[0], outs[1],
        )

    gu_0, hid_0, sum_0, *parts_0 = run(lambda i: expert(rows_near, grads_near, w_gate_up, w_down, i, CHUNKS, (0,)), indices[0])
    chunk = parts_0[0].shape
    two = (2,) + chunk
    in_0 = go_in(parts_0[0])
    parts_0 += run(lambda i: weight_grads(rows_near, grads_near, gu_0, hid_0, CHUNKS, (1,), i), both)
    gu_1, hid_1, first_half, other_half = run(
        lambda i: last_expert(rows_near, grads_near, w_gate_up, w_down, i, [gu_0], [sum_0]), both
    )
    far = [other_core(other_half)]
    (half_0,) = steps(lambda flag, raw, got: (f(raw) + f(got),), [chunk], parts_0[0], in_0)
    middle_0, in_1 = cross(half_0), go_in(parts_0[1])
    tall = first_half.shape[1]

    def block_sums(flag, first, other):
        total = f(first) + f(other)
        return tuple(total[i] for i in range(len(near)))

    blocks = run(
        lambda first, other: post(lambda *v: block_sums(*v), flags, (first, other), [array((tall, D), bf16)] * len(near), tall // 16),
        first_half, far[0],
    )
    returned = send_back(blocks)
    mixed, mixed_other = run(lambda i: row_terms([hid_0, hid_1], w_down, i, cores), both)
    parts_1 = run(lambda i: weight_grads(rows_near, grads_near, gu_1, hid_1, CHUNKS, range(CHUNKS), i), both)

    def step_1(flag, half, middle, own, got, raw):
        total = f(half) + f(middle)
        return total, f(own) + f(got), pick(flag[0], raw, total)

    total_0, half_1, sent_2 = steps(step_1, [chunk] * 3, half_0, middle_0, parts_0[1], in_1, parts_1[0])
    both_2, middle_1 = in_and_out(sent_2), cross(half_1)
    grad_residual, grad_own, grad_prev, own_w, *other_w = run(back, returned)
    far_w = [other_core(w) for w in other_w]
    deep, wide = own_w.shape[1:]

    def step_2(flag, own, got, total, half, middle, raw, w, *far):
        summed = f(half) + f(middle)
        joined = f(w) + jnp.concatenate([f(v) for v in far], -1)
        mine, theirs = pick(flag[1], joined[1], joined[0]), pick(flag[1], joined[0], joined[1])
        return f(own) + f(got), pick(flag[0], got, total), summed, pick(flag[0], raw, summed), mine, theirs

    half_2, full_0, total_1, sent_3, own_w, other_w = steps(
        step_2, [chunk] * 4 + [(deep, wide)] * 2,
        parts_1[0], both_2, total_0, half_1, middle_1, parts_1[1], own_w, *far_w,
    )
    side_0, middle_2, both_3 = other_side(full_0), cross(half_2), in_and_out(sent_3)
    far_w, far_m = from_shard(other_w, 1), other_core(mixed_other)

    def step_3(flag, own, got, total, half, middle, first, other, w, far, m, m_far):
        terms = f(m) + f(m_far)
        return (
            f(own) + f(got), pick(flag[0], got, total), f(half) + f(middle), (first, other), f(w) + f(far), terms[:2], terms[2:],
        )

    rows_of = mixed.shape[1]
    half_3, full_1, total_2, pair_0, own_w, own_m, other_m = steps(
        step_3, [chunk] * 3 + [two, (deep, wide)] + [(2, rows_of, D)] * 2,
        parts_1[1], both_3, total_1, half_2, middle_2, full_0, side_0, own_w, far_w, mixed, far_m,
    )
    side_1, middle_3, out_2, core_0 = other_side(full_1), cross(half_3), go_out(total_2), other_core(pair_0)
    in_w = go_in(own_w)

    def step_4(flag, got, total, half, middle, first, other, w, far):
        return pick(flag[0], got, total), f(half) + f(middle), (first, other), f(w) + f(far)

    full_2, total_3, pair_1, half_w = steps(
        step_4, [chunk] * 2 + [two, (deep, wide)], out_2, total_2, half_3, middle_3, full_1, side_1, own_w, in_w
    )
    side_2, out_3, middle_w, core_1 = other_side(full_2), go_out(total_3), cross(half_w), other_core(pair_1)
    far_m = from_shard(other_m, 1)
    outs = run(lambda pair, swap: placed(pair, [swap], (), 0, 0), pair_0, core_0)

    def step_5(flag, got, total, first, other, w, far, m, m_far):
        terms = f(m) + f(m_far)
        return pick(flag[0], got, total), (first, other), f(w) + f(far), terms[0], terms[1]

    full_3, pair_2, total_w, own_m, other_m = steps(
        step_5, [chunk, two, (deep, wide)] + [(rows_of, D)] * 2, out_3, total_3, full_2, side_2, half_w, middle_w, own_m, far_m
    )
    side_3, out_w, core_2 = other_side(full_3), go_out(total_w), other_core(pair_2)
    far_m = other_side(other_m)
    grad_later = lax.ppermute(grad_prev, "fsdp", before)
    outs = run(lambda pair, swap, outs: placed(pair, [swap], outs, 0, 1), pair_1, core_1, outs)

    def step_6(flag, first, other, got, w, rest, m, m_far, own, back):
        return (first, other), pick(flag[0], got, w), rest + f(m) + f(m_far), own + f(back)

    pair_3, full_w, layer_out, grad_sum = steps(
        step_6, [two, (deep, wide), (rows_of, D), array((rows_of, D), f32)],
        full_3, side_3, out_w, total_w, residual, own_m, far_m, grad_own, grad_later,
    )
    core_3, side_w, core_w = other_core(pair_3), other_side(full_w), other_core(full_w)
    grad_in = run(lambda grad: first_back(grad, grad_residual, hidden_in, gain_attn), grad_sum)
    outs = run(lambda pair, swap, outs: placed(pair, [swap], outs, 1, 0), pair_2, core_2, outs)
    outs = run(lambda pair, swap, outs: placed(pair, [swap], outs, 1, 1), pair_3, core_3, outs)
    side_w, core_w = run(lambda *v: v, side_w, core_w)
    both_w = other_core(side_w)
    at_w = jnp.stack([(core_at - core) % cores for core in range(cores)]).astype(jnp.int32) * deep
    qkv_sum, out_sum, router_sum, ffn_sum, attn_sum = run(
        lambda *v: unpack([w[None] for w in v[:2]], at_w, deep * cores, [w[None] for w in v[2:]]), full_w, core_w, side_w, both_w
    )
    return (
        layer_out,
        grad_in,
        qkv_sum,
        out_sum,
        router_sum,
        attn_sum[0],
        ffn_sum[0],
        outs[0],
        outs[1],
    )


def solution(mesh):
    copies, shards = mesh.shape["rep"], mesh.shape["fsdp"]
    local = EXPERTS // shards
    cores = 2 if copies % 2 == 0 and local % 2 == 0 else 1
    side = 2 if cores == 2 and copies % 4 == 0 and local % 4 == 0 else 1
    names = ("line", "side", "core", "fsdp")
    parts = Mesh(mesh.devices.reshape(copies // (side * cores), side, cores, shards), names)
    rows, shard = P(names, None), P("fsdp", None)
    experts = P("fsdp", None, None)
    in_specs = (rows, rows, shard, shard, shard, P("fsdp"), P("fsdp"), experts, experts, rows)
    out_specs = (rows, rows, shard, shard, shard, P("fsdp"), P("fsdp"), experts, experts)
    return jax.shard_map(body, mesh=parts, in_specs=in_specs, out_specs=out_specs, check_vma=False)
```
